32 devices in a mesh: groups: 2 (over x), tiles: 16 (over z, y, core).
Axes of the slice: x: 2, y: 2, z: 4, core: 2. Of those that a mesh axis runs over, the one named last changes fastest.
Arguments:
- pieces: bfloat16 [512, 6, 128, 128], P(('groups', 'tiles')), parts along dimension 0, may hold values from -6 to 6
- piece_blend: int32 [512], P(('groups', 'tiles')), parts along dimension 0, may hold values from 0 to 63, as said below
- corners: int32 [512, 2], P(('groups', 'tiles')), parts along dimension 0, may hold values from -96 to 223
- blend_home: int32 [128], P('groups'), parts along dimension 0, may hold values from 0 to 63, as said below
- source_count: int32 [128], P(('groups', 'tiles')), parts along dimension 0, may hold values from 1 to 4
- footprint: int32 [128, 128, 128], P(('groups', 'tiles')), parts along dimension 0, may hold values from 0 to 4
- spectra: float32 [128, 4, 6], P(('groups', 'tiles')), parts along dimension 0, may hold values from 0.2 to 1
- giant_pieces: bfloat16 [32, 6, 128, 128], P(('groups', 'tiles')), parts along dimension 0, may hold values from -6 to 6
- giant_footprint: int32 [32, 128, 128], P(('groups', 'tiles')), parts along dimension 0, may hold values from 0 to 4
- giant_spectra: float32 [32, 4, 6], P(('groups', 'tiles')), parts along dimension 0, may hold values from 0.2 to 1
- psf_matrix: bfloat16 [6, 128, 128], replicated, may hold values from 0 to 1
Outputs:
- blend_morph: bfloat16 [128, 4, 128, 128], P(('groups', 'tiles')), parts along dimension 0
- blend_spectra: bfloat16 [128, 4, 6], P(('groups', 'tiles')), parts along dimension 0
- tile_model: float32 [32, 6, 256, 256], P(('groups', 'tiles')), parts along dimension 0
- giant_morph: float32 [32, 4, 128, 128], P(('groups', 'tiles')), parts along dimension 0
The draws below stay inside these ranges and needn't reach their ends.
There are 2 independent parts, one for each index of `groups`. The reference program is written for one: setup_inputs(seed, part) draws one part's arguments, and reference() takes and returns one part's arrays. A program takes and returns all parts, laid end to end along the dimension named above; an argument that names none is the same for every part. Nothing has to cross between parts.
Inputs may be any that keep to these rules, and one draw needn't show every extreme that they name: `piece_blend`: at most 2 pieces of one device belong to blends of one owner; in every draw some owner gets exactly 2 pieces from every device. `blend_home`: A permutation of 0 to 63.
All inputs are finite; a program needn't handle non-finite values.
Results may differ from the reference program's by a relative error of at most 0.006.
Values may be sent and summed in bfloat16 or wider, within the bound.
A program may use at most 128 MiB of HBM per device.

```python
import math
import jax
import jax.numpy as jnp
from jax import lax

BANDS = 6
PIX = 128
SRC = 4
GSRC = 4
SLOT_CAP = 2
TILE = 256
ITERS = 3
PIECE_DEV = 16
BLEND_DEV = 4
PIECES = 256
BLENDS = 64
N_TILES = 16


def route_table(key):
    base_key = jax.random.fold_in(key, 7)
    key_hot, key_pref, key_score, key_slot, key_perm, key_order = jax.random.split(base_key, 6)
    slot_load_total = N_TILES * SLOT_CAP
    busiest_owner = jax.random.randint(key_hot, (), 0, N_TILES)
    owner_preference = jax.random.randint(key_pref, (N_TILES,), 0, 4000)
    placement_scores = jax.random.randint(key_score, (N_TILES, slot_load_total), 0, 4000)
    destination_for = jnp.arange(slot_load_total, dtype=jnp.int32) // SLOT_CAP
    extra_reward = owner_preference[destination_for] + jnp.where(destination_for == busiest_owner, 100000, 0)
    running_totals = (placement_scores + extra_reward[None, :]) * slot_load_total + jnp.arange(slot_load_total, dtype=jnp.int32)[None, :]
    unused, chosen = lax.top_k(running_totals, PIECE_DEV)
    dests = chosen // SLOT_CAP
    order_keys = jax.random.randint(key_order, (N_TILES, PIECE_DEV), 0, 1 << 20) * PIECE_DEV + jnp.arange(PIECE_DEV, dtype=jnp.int32)[None, :]
    order = jnp.argsort(order_keys, axis=1)
    dests = jnp.take_along_axis(dests, order, axis=1)
    places = jax.random.randint(key_slot, (N_TILES, PIECE_DEV), 0, BLEND_DEV)
    homes = (dests * BLEND_DEV + places).reshape(-1)
    blend_at_home = jax.random.permutation(key_perm, BLENDS).astype(jnp.int32)
    piece_blend = blend_at_home[homes].astype(jnp.int32)
    blend_home = jnp.argsort(blend_at_home).astype(jnp.int32)
    return (piece_blend, blend_home)


def draw_piece_blend(key, part):
    return route_table(key)[0]


def draw_blend_home(key, part):
    return route_table(key)[1]


def group_labels(group_key):
    key_cells, key_row, key_col, key_label = jax.random.split(group_key, 4)
    cell_owner = (jax.random.permutation(key_cells, 32).astype(jnp.int32) % 8).astype(jnp.int32)
    row_shift = jax.random.randint(key_row, (), 0, PIX // 4) * 4 + 2
    col_shift = jax.random.randint(key_col, (), 0, PIX // 4) * 4 + 2
    rows = (jnp.arange(PIX, dtype=jnp.int32) + row_shift) % PIX
    cols = (jnp.arange(PIX, dtype=jnp.int32) + col_shift) % PIX
    cell = ((rows // (PIX // 4))[:, None] * 8 + (cols // (PIX // 8))[None, :]).astype(jnp.int32)
    pixel_owner = cell_owner[cell]
    labels = jax.random.randint(key_label, (8, PIX, PIX), 1, GSRC + 1)
    mine = pixel_owner[None, :, :] == jnp.arange(8, dtype=jnp.int32)[:, None, None]
    return jnp.where(mine, labels, 0).astype(jnp.int32)


def draw_giant_footprint(key, part):
    base_key = jax.random.fold_in(key, 11)
    group_keys = jax.random.split(base_key, N_TILES // 8)
    return jax.vmap(group_labels)(group_keys).reshape(N_TILES, PIX, PIX).astype(jnp.int32)


def draw_psf_matrix(key, part):
    row_ids = jnp.arange(PIX, dtype=jnp.float32)[:, None]
    col_ids = jnp.arange(PIX, dtype=jnp.float32)[None, :]
    offset = row_ids - col_ids
    band_ids = jnp.arange(BANDS, dtype=jnp.float32)[:, None, None]
    spread = 1.5 + 0.5 * band_ids
    rough = jax.random.uniform(key, (BANDS, PIX, PIX), jnp.float32, 0.5, 1.5)
    weights = jnp.exp(-offset[None] ** 2 / (2.0 * spread ** 2)) * rough * (jnp.abs(offset)[None] <= 12.0)
    return (weights / jnp.sum(weights, axis=2, keepdims=True)).astype(jnp.bfloat16)


def with_ends(array, stream_key, least, high):
    spot = [jax.random.randint(jax.random.fold_in(stream_key, axis), (), 0, length) for axis, length in enumerate(array.shape)]
    widest = array.shape.index(max(array.shape))
    next_to = spot[:widest] + [(spot[widest] + 1) % array.shape[widest]] + spot[widest + 1:]
    return array.at[tuple(spot)].set(least).at[tuple(next_to)].set(high)


def steps_of(rng, extent, shards, smallest, top_value):
    gain = 1.0
    for position, blocks in shards:
        heights = jax.random.uniform(jax.random.fold_in(jax.random.fold_in(rng, 6), position), (blocks,), jnp.float32, smallest / len(shards), top_value / len(shards))
        gain = gain * jnp.repeat(jnp.exp(heights), extent[position] // blocks).reshape((-1,) + (1,) * (len(extent) - 1 - position))
    return gain


def noise(key, extent, width, most, cuts=(), held_as=jnp.bfloat16):
    array = jax.random.normal(key, extent, jnp.float32) * width
    if len(cuts) > 0:
        array = steps_of(key, extent, cuts, -0.22, 0.18) * array
    return jnp.clip(array, min=-most, max=most).astype(held_as)


def setup_inputs(seed: int = 0, part: int = 0) -> dict:
    key_list = jax.random.split(jax.random.key(seed), 12)
    part_keys = jax.random.split(jax.random.fold_in(key_list[11], part), 12)
    return {
        "pieces": noise(part_keys[0], (PIECES, BANDS, PIX, PIX), 1.0, 6.0, ((0, 16),)),
        "piece_blend": draw_piece_blend(jax.random.fold_in(jax.random.fold_in(key_list[11], part), 71), part),
        "corners": with_ends(jax.random.randint(part_keys[2], (PIECES, 2), 0 - (PIX - PIX // 4), TILE - PIX // 4), jax.random.fold_in(part_keys[2], 1), 0 - (PIX - PIX // 4), (TILE - PIX // 4) - 1).astype(jnp.int32),
        "blend_home": draw_blend_home(jax.random.fold_in(jax.random.fold_in(key_list[11], part), 71), part),
        "source_count": with_ends(jax.random.randint(part_keys[4], (BLENDS,), 1, SRC + 1), jax.random.fold_in(part_keys[4], 1), 1, SRC).astype(jnp.int32),
        "footprint": with_ends(jax.random.randint(part_keys[5], (BLENDS, PIX, PIX), 0, SRC + 1), jax.random.fold_in(part_keys[5], 1), 0, SRC).astype(jnp.int32),
        "spectra": jnp.clip(jnp.exp(math.log(1.0) - 1.609438 * jax.random.uniform(part_keys[6], (BLENDS, SRC, BANDS), jnp.float32) ** steps_of(part_keys[6], (BLENDS, SRC, BANDS), ((0, 16),), -0.2, 0.2)), 0.2, 1.0),
        "giant_pieces": noise(part_keys[7], (N_TILES, BANDS, PIX, PIX), 1.0, 6.0, ((0, 16),)),
        "giant_footprint": draw_giant_footprint(jax.random.fold_in(jax.random.fold_in(key_list[11], part), 71), part),
        "giant_spectra": jnp.clip(jnp.exp(math.log(1.0) - 1.609438 * jax.random.uniform(part_keys[9], (N_TILES, GSRC, BANDS), jnp.float32) ** steps_of(part_keys[9], (N_TILES, GSRC, BANDS), ((0, 16),), -0.2, 0.2)), 0.2, 1.0),
        "psf_matrix": draw_psf_matrix(jax.random.fold_in(key_list[11], 71), part),
    }


step_size = 0.1


def psf_blur(mix, psf_matrix):
    kernel = psf_matrix.astype(jnp.float32)
    half_way = jnp.einsum('bij,nbjk->nbik', kernel, mix.astype(jnp.float32)).astype(jnp.bfloat16)
    return jnp.einsum('nbij,bkj->nbik', half_way.astype(jnp.float32), kernel)


def adjoint(resid, psf_matrix):
    kernel = psf_matrix.astype(jnp.float32)
    half_way = jnp.einsum('bji,nbjk->nbik', kernel, resid.astype(jnp.float32)).astype(jnp.bfloat16)
    return jnp.einsum('nbij,bjk->nbik', half_way.astype(jnp.float32), kernel)


def combine(sed, morph):
    return jnp.einsum('nkb,nkij->nbij', sed, morph, precision=lax.Precision.HIGHEST)


def initial(image, labels, active):
    source_total = active.shape[1]
    base_map = jnp.maximum(jnp.mean(image, axis=1), 0.0)
    marks = (labels[:, None] == (jnp.arange(source_total, dtype=jnp.int32) + 1)[None, :, None, None]).astype(jnp.float32)
    return marks * base_map[:, None] * active[:, :, None, None]


def refine(image, morph, sed, active, psf_matrix, total):
    for iteration in range(ITERS):
        model_now = total(psf_blur(combine(sed, morph).astype(jnp.bfloat16), psf_matrix))
        resid = (image - model_now).astype(jnp.bfloat16)
        grad = adjoint(resid, psf_matrix)
        inner = jnp.einsum('nkij,nbij->nkb', morph, grad, precision=lax.Precision.HIGHEST)
        energy = jnp.sum(morph * morph, axis=(2, 3))
        push = jnp.einsum('nkb,nbij->nkij', sed, grad, precision=lax.Precision.HIGHEST)
        sed_next = jnp.maximum(sed + inner / (energy + 1.0)[:, :, None], 0.0) * active[:, :, None]
        morph = jnp.maximum(morph + step_size * push, 0.0) * active[:, :, None, None]
        sed = sed_next
    return morph, sed


def reference(pieces, piece_blend, corners, blend_home, source_count, footprint, spectra, giant_pieces, giant_footprint, giant_spectra, psf_matrix):
    piece_home = blend_home[piece_blend].astype(jnp.int32)
    flat = pieces.astype(jnp.float32).reshape(PIECES, BANDS * PIX * PIX)
    blend_image = jax.ops.segment_sum(flat, piece_home, num_segments=BLENDS).reshape(BLENDS, BANDS, PIX, PIX)
    active = (jnp.arange(SRC, dtype=jnp.int32)[None, :] < source_count[:, None]).astype(jnp.float32)

    def per_owner(owner_block):
        image, labels, start_sed, act = owner_block
        morph = initial(image, labels, act)
        sed = start_sed * act[:, :, None]
        morph, sed = refine(image, morph, sed, act, psf_matrix, lambda summed: summed)
        final_morph = morph.astype(jnp.bfloat16)
        final_sed = sed.astype(jnp.bfloat16)
        mix = combine(final_sed.astype(jnp.float32), final_morph.astype(jnp.float32)).astype(jnp.bfloat16)
        model = psf_blur(mix, psf_matrix).astype(jnp.bfloat16)
        return final_morph, final_sed, model

    blocks = (blend_image.reshape(N_TILES, BLEND_DEV, BANDS, PIX, PIX),
              footprint.reshape(N_TILES, BLEND_DEV, PIX, PIX),
              spectra.reshape(N_TILES, BLEND_DEV, SRC, BANDS),
              active.reshape(N_TILES, BLEND_DEV, SRC))
    final_morph, final_sed, models = lax.map(per_owner, blocks)
    final_morph = final_morph.reshape(BLENDS, SRC, PIX, PIX)
    final_sed = final_sed.reshape(BLENDS, SRC, BANDS)
    models = models.reshape(BLENDS, BANDS, PIX, PIX)

    margin = PIX - PIX // 4

    def per_tile(tile_block):
        spots, homes = tile_block
        canvas = jnp.zeros((BANDS, TILE + 2 * margin, TILE + 2 * margin), jnp.float32)

        def place(piece_index, canvas):
            patch_model = lax.dynamic_index_in_dim(models, homes[piece_index], 0, keepdims=False).astype(jnp.float32)
            row_start = (spots[piece_index, 0] + margin).astype(jnp.int32)
            col_start = (spots[piece_index, 1] + margin).astype(jnp.int32)
            anchor = (jnp.zeros((), jnp.int32), row_start, col_start)
            region = lax.dynamic_slice(canvas, anchor, (BANDS, PIX, PIX))
            return lax.dynamic_update_slice(canvas, region + patch_model, anchor)

        canvas = lax.fori_loop(0, PIECE_DEV, place, canvas)
        return canvas[:, margin:margin + TILE, margin:margin + TILE]

    tile_model = lax.map(per_tile, (corners.reshape(N_TILES, PIECE_DEV, 2), piece_home.reshape(N_TILES, PIECE_DEV)))

    group_count = N_TILES // 8

    def group_sum(field_sum):
        summed = field_sum.reshape((group_count, 8) + field_sum.shape[1:]).sum(axis=1)
        return jnp.repeat(summed, 8, axis=0)

    giant_image = group_sum(giant_pieces.astype(jnp.float32))
    giant_active = jnp.ones((N_TILES, GSRC), jnp.float32)
    giant_start = initial(giant_image, giant_footprint, giant_active)
    giant_morph, giant_sed = refine(giant_image, giant_start, giant_spectra, giant_active, psf_matrix, group_sum)
    return final_morph, final_sed, tile_model, giant_morph
```

```python
import functools

import jax
import jax.numpy as jnp
from jax import lax
from jax.experimental import pallas as pl
from jax.experimental.pallas import tpu as pltpu
from jax.sharding import PartitionSpec as P

TILE = 256
ITERS = 3
GROUP = 8
CHUNKS = 4
MESH = pl.DeviceIdType.MESH
F32 = jnp.float32
BF16 = jnp.bfloat16
I32 = jnp.int32

step_size = 0.1

VMEM = pl.BlockSpec(memory_space=pltpu.VMEM)
SMEM = pl.BlockSpec(memory_space=pltpu.SMEM)
ANY = pl.BlockSpec(memory_space=pl.ANY)


def matmul(a, b):
    return jnp.dot(a, b, preferred_element_type=F32)


def t_matmul(a, b):
    return lax.dot_general(a, b, (((0,), (0,)), ((), ())), preferred_element_type=F32)


def barrier_all(me, count):
    barrier = pltpu.get_barrier_semaphore()
    for k in range(1, count):
        pl.semaphore_signal(
            barrier, inc=1, device_id={"tiles": lax.rem(me + k, count)}, device_id_type=MESH
        )
    pl.semaphore_wait(barrier, count - 1)


def remote(src, dst, send_sem, recv_sem, peer):
    return pltpu.make_async_remote_copy(
        src_ref=src,
        dst_ref=dst,
        send_sem=send_sem,
        recv_sem=recv_sem,
        device_id={"tiles": peer},
        device_id_type=MESH,
    )


def mix_band(sed_ref, maps, b, bands, sources):
    total = sed_ref[b : b + 1, :] * maps[0]
    for k in range(1, sources):
        row = k * bands + b
        total = total + sed_ref[row : row + 1, :] * maps[k]
    return total.astype(BF16)


def update(sed_ref, morph_ref, grad_ref, part_ref, energy_ref, act_ref, bands, sources):
    for k in range(sources):
        morph = morph_ref[k]
        energy = jnp.sum(morph * morph, axis=0, keepdims=True)
        push = None
        for b in range(bands):
            row = k * bands + b
            grad = grad_ref[b]
            part_ref[row : row + 1, :] = jnp.sum(morph * grad, axis=0, keepdims=True)
            energy_ref[row : row + 1, :] = energy
            term = sed_ref[row : row + 1, :] * grad
            push = term if push is None else push + term
        fresh = jnp.maximum(morph + step_size * push, 0.0)
        if act_ref is not None:
            fresh = fresh * act_ref[k * bands : k * bands + 1, :]
        morph_ref[k] = fresh
    inner = jnp.sum(part_ref[...], axis=1, keepdims=True)
    energy = jnp.sum(energy_ref[...], axis=1, keepdims=True)
    sed = jnp.maximum(sed_ref[...] + inner / (energy + 1.0), 0.0)
    if act_ref is not None:
        sed = sed * act_ref[...]
    sed_ref[...] = sed


def spread_rows(sed_ref, table, bands, sources, lanes):
    for k in range(sources):
        line = jnp.broadcast_to(table[k : k + 1, :], (bands, bands))
        row = lax.broadcasted_iota(I32, (bands, bands), 0)
        col = lax.broadcasted_iota(I32, (bands, bands), 1)
        value = jnp.sum(jnp.where(row == col, line, 0.0), axis=1, keepdims=True)
        sed_ref[k * bands : (k + 1) * bands, :] = jnp.broadcast_to(value, (bands, lanes))


def first_kernel(
    piece_count,
    pieces_ref,
    blend_ref,
    table_ref,
    recv_ref,
    homes_ref,
    home_buf,
    own_sem,
    send_sem,
    recv_sem,
    home_send,
    home_recv,
):
    me = lax.axis_index("tiles")
    rank = lax.rem(me, GROUP)
    base = me - rank
    barrier = pltpu.get_barrier_semaphore()
    for k in range(1, GROUP):
        pl.semaphore_signal(
            barrier,
            inc=1,
            device_id={"tiles": base + lax.rem(rank + k, GROUP)},
            device_id_type=MESH,
        )
    pl.semaphore_wait(barrier, GROUP - 1)

    exchange = []
    for k in range(1, GROUP):
        other = lax.rem(rank + k, GROUP)
        exchange.append(
            remote(
                pieces_ref.at[:, other],
                recv_ref.at[rank],
                send_sem.at[k - 1],
                recv_sem.at[k - 1],
                base + other,
            )
        )
    for copy in exchange:
        copy.start()
    own = pltpu.make_async_copy(pieces_ref.at[:, rank], recv_ref.at[rank], own_sem)
    own.start()
    lane = lax.broadcasted_iota(I32, home_buf.shape, 1)
    line = jnp.zeros(home_buf.shape, I32)
    for index in range(piece_count):
        line = jnp.where(lane == index, table_ref[blend_ref[index]], line)
    home_buf[...] = line
    homes_ref[rank] = line
    for k in range(1, GROUP):
        other = lax.rem(rank + k, GROUP)
        copy = remote(
            home_buf,
            homes_ref.at[rank],
            home_send.at[k - 1],
            home_recv.at[k - 1],
            base + other,
        )
        copy.start()
        exchange.append(copy)
    own.wait()
    for copy in exchange:
        copy.wait()


def segment_kernel(piece_count, homes_ref, recv_ref, out_ref, total):
    total[...] = jnp.zeros_like(total)
    for source in range(GROUP):

        def add(index, carry):
            home = homes_ref[source, 0, index]
            total[home] = total[home] + recv_ref[source, index].astype(F32)
            return carry

        lax.fori_loop(0, piece_count, add, 0, unroll=4)
    out_ref[...] = total[...].astype(BF16)


def core_kernel(
    count,
    bands,
    sources,
    owned,
    piece_count,
    homes_ref,
    counts_ref,
    summed_ref,
    labels_ref,
    spectra_ref,
    psf_ref,
    corners_ref,
    giant_ref,
    giant_labels_ref,
    giant_spectra_ref,
    out_morph,
    out_sed,
    out_tile,
    out_giant,
    arrived,
    morph_ref,
    sed_ref,
    act_ref,
    adj_ref,
    grad_ref,
    part_ref,
    energy_ref,
    gram,
    psf_t,
    sed_table,
    sed_all,
    held,
    picked,
    landed,
    row_psf,
    col_psf,
    left_ref,
    strips,
    base_buf,
    band_buf,
    mix_buf,
    adj_own,
    giant_sed,
    giant_grad,
    in_send,
    in_recv,
    back_send,
    back_recv,
    sed_send,
    sed_recv,
    last_send,
    last_recv,
    strip_send,
    strip_recv,
    base_send,
    base_recv,
    band_send,
    band_recv,
    grad_send,
    grad_recv,
):
    me = lax.axis_index("tiles")
    rank = lax.rem(me, GROUP)
    base = me - rank
    mine = me // GROUP
    groups = count // GROUP
    side = labels_ref.shape[1]
    lanes = side
    strip = side // GROUP
    table = bands * sources
    half = (bands + 1) // 2
    per_chunk = piece_count // CHUNKS
    barrier_all(me, count)

    def keeper(b):
        return (b // half) * (GROUP // 2) + b % half

    upper = rank // (GROUP // 2)
    lower = lax.rem(rank, GROUP // 2)
    own_band = upper * half + lower
    keeps = jnp.logical_and(lower < half, own_band < bands)
    safe_band = jnp.where(keeps, own_band, 0)

    def incoming(n, k):
        peer = lax.rem(me + k, count)
        return remote(
            summed_ref.at[peer * owned + n],
            arrived.at[n, mine, rank],
            in_send.at[n, k - 1],
            in_recv.at[n, k - 1],
            peer,
        )

    def outgoing(n, k):
        peer = lax.rem(me + k, count)
        return remote(
            out_morph.at[n, lax.rem(peer, GROUP)],
            held.at[me * owned + n],
            back_send.at[n, k - 1],
            back_recv.at[n, k - 1],
            peer,
        )

    def sed_copy(k):
        return remote(
            sed_all.at[me], sed_all.at[me], sed_send.at[k - 1], sed_recv.at[k - 1],
            lax.rem(me + k, count),
        )

    def last_copy(chunk, k):
        other = lax.rem(rank + k, GROUP)
        return remote(
            picked.at[chunk, other],
            landed.at[chunk, :, rank],
            last_send.at[chunk, k - 1],
            last_recv.at[chunk, k - 1],
            base + other,
        )

    def strip_copy(k):
        other = lax.rem(rank + k, GROUP)
        return remote(
            giant_ref.at[:, other], strips.at[rank], strip_send.at[k - 1], strip_recv.at[k - 1],
            base + other,
        )

    def base_copy(k):
        other = lax.rem(rank + k, GROUP)
        return remote(
            base_buf.at[rank], base_buf.at[rank], base_send.at[k - 1], base_recv.at[k - 1],
            base + other,
        )

    def band_copy(slot, src, b):
        return remote(
            src, band_buf.at[slot, rank], band_send.at[slot, b], band_recv.at[slot, rank],
            base + keeper(b),
        )

    def grad_copy(slot, k):
        other = lax.rem(rank + k, GROUP)
        return remote(
            giant_grad.at[slot, safe_band],
            giant_grad.at[slot, safe_band],
            grad_send.at[slot, k - 1],
            grad_recv.at[slot, safe_band],
            base + other,
        )

    def send_bands(slot, ref):
        for b in range(bands):
            @pl.when(rank != keeper(b))
            def _():
                band_copy(slot, ref.at[b], b).start()

            @pl.when(rank == keeper(b))
            def _():
                band_buf[slot, rank] = ref[b]

    def sent_bands(slot, ref):
        for b in range(bands):
            @pl.when(rank != keeper(b))
            def _():
                band_copy(slot, ref.at[b], b).wait_send()

    def kept_sum(slot):
        for k in range(1, GROUP):
            source = lax.rem(rank + k, GROUP)
            pltpu.make_async_remote_copy(
                src_ref=band_buf.at[slot, source],
                dst_ref=band_buf.at[slot, source],
                send_sem=band_send.at[slot, 0],
                recv_sem=band_recv.at[slot, source],
                device_id={"tiles": base + source},
                device_id_type=MESH,
            ).wait_recv()
        total = band_buf[slot, 0].astype(F32)
        for source in range(1, GROUP):
            total = total + band_buf[slot, source].astype(F32)
        return total.reshape(side, side).astype(BF16)

    def giant_open():
        for k in range(1, GROUP):
            strip_copy(k).wait_recv()
        mean = None
        for k in range(GROUP):
            source = lax.rem(rank + k, GROUP)
            part = giant_ref[:, rank] if k == 0 else strips[source]
            part = jnp.sum(part.astype(F32), axis=0)
            mean = part if mean is None else mean + part
        base_buf[rank] = jnp.maximum(mean / bands, 0.0)
        for k in range(1, GROUP):
            base_copy(k).start()

        @pl.when(keeps)
        def _():
            total = kept_sum(ITERS)
            back = matmul(psf_t[safe_band], total).astype(BF16)
            adj_own[...] = matmul(back, psf_ref[safe_band])

    def giant_mix(slot):
        for b in range(bands):
            mix = mix_band(giant_sed, out_giant, b, bands, sources)
            mix_buf[slot, b] = mix.reshape(GROUP, strip, side)
        send_bands(slot, mix_buf.at[slot])

    def giant_start():
        for k in range(1, GROUP):
            base_copy(k).wait_recv()
        base_map = base_buf[...].reshape(side, side)
        for k in range(sources):
            out_giant[k] = jnp.where(giant_labels_ref[0] == k + 1, base_map, 0.0)
        spread_rows(giant_sed, giant_spectra_ref[0], bands, sources, lanes)
        giant_mix(0)

    def giant_keep(slot):
        @pl.when(keeps)
        def _():
            total = kept_sum(slot)
            gram_own = gram[safe_band]
            grad = adj_own[...] - matmul(matmul(gram_own, total).astype(BF16), gram_own)
            giant_grad[slot, safe_band] = grad.astype(BF16)
            for k in range(1, GROUP):
                grad_copy(slot, k).start()

    def giant_update(slot):
        for b in range(bands):
            @pl.when(rank != keeper(b))
            def _():
                pltpu.make_async_remote_copy(
                    src_ref=giant_grad.at[slot, b],
                    dst_ref=giant_grad.at[slot, b],
                    send_sem=grad_send.at[slot, 0],
                    recv_sem=grad_recv.at[slot, b],
                    device_id={"tiles": base + keeper(b)},
                    device_id_type=MESH,
                ).wait_recv()

        for b in range(bands):
            grad_ref[b] = giant_grad[slot, b].astype(F32)
        update(giant_sed, out_giant, grad_ref, part_ref, energy_ref, None, bands, sources)

    steps = [giant_start]
    for it in range(ITERS):
        steps.append(functools.partial(giant_keep, it))
        if it < ITERS - 1:

            def advance(it=it):
                giant_update(it)
                giant_mix(it + 1)

            steps.append(advance)
        else:
            steps.append(functools.partial(giant_update, it))

    for k in range(1, GROUP):
        strip_copy(k).start()
    send_bands(ITERS, giant_ref)

    def launch(n):
        for k in range(1, count):
            incoming(n, k).start()

    ahead = 2
    for n in range(min(ahead, owned)):
        launch(n)

    for b in range(bands):
        psf = psf_ref[b]
        gram[b] = t_matmul(psf, psf).astype(BF16)
        psf_t[b] = jnp.transpose(psf.astype(F32)).astype(BF16)

    def prepare(index, carry):
        row_at = corners_ref[pl.ds(index, 1), 0:1]
        col_at = corners_ref[pl.ds(index, 1), 1:2]
        rows = lax.broadcasted_iota(I32, (TILE, side), 0)
        inner = lax.broadcasted_iota(I32, (TILE, side), 1)
        row_hot = jnp.where(rows == inner + row_at, 1.0, 0.0).astype(BF16)
        cols = lax.broadcasted_iota(I32, (side, TILE), 1)
        inner_c = lax.broadcasted_iota(I32, (side, TILE), 0)
        col_hot = jnp.where(cols == inner_c + col_at, 1.0, 0.0).astype(BF16)
        for b in range(bands):
            row_psf[index, b] = matmul(row_hot, psf_ref[b]).astype(BF16)
            col_psf[b, index] = matmul(psf_t[b], col_hot).astype(BF16)
        return carry

    lax.fori_loop(0, piece_count, prepare, 0)
    sed_table[...] = jnp.zeros_like(sed_table)
    giant_open()

    def blend(n, carry):
        arrived[n, mine, rank] = summed_ref[me * owned + n]
        for k in range(1, count):
            incoming(n, k).wait_recv()
        source_of_row = lax.broadcasted_iota(I32, (table, lanes), 0) // bands
        act_ref[...] = jnp.where(source_of_row < counts_ref[n], 1.0, 0.0)
        spread_rows(sed_ref, spectra_ref[n], bands, sources, lanes)
        sed_ref[...] = sed_ref[...] * act_ref[...]
        total = arrived[n, 0].astype(F32)
        for g in range(1, groups):
            total = total + arrived[n, g].astype(F32)
        grad_ref[...] = total.reshape(bands, side, side)
        mean = grad_ref[0]
        for b in range(1, bands):
            mean = mean + grad_ref[b]
        base_map = jnp.maximum(mean / bands, 0.0)
        for k in range(sources):
            morph_ref[k] = (
                jnp.where(labels_ref[n] == k + 1, base_map, 0.0)
                * act_ref[k * bands : k * bands + 1, :]
            )
        for b in range(bands):
            back = matmul(psf_t[b], grad_ref[b].astype(BF16)).astype(BF16)
            adj_ref[b] = matmul(back, psf_ref[b])

        def iteration(it, carry):
            for b in range(bands):
                mix = mix_band(sed_ref, morph_ref, b, bands, sources)
                grad_ref[b] = adj_ref[b] - matmul(matmul(gram[b], mix).astype(BF16), gram[b])
            update(sed_ref, morph_ref, grad_ref, part_ref, energy_ref, act_ref, bands, sources)
            return carry

        lax.fori_loop(0, ITERS, iteration, 0)
        out_morph[n] = morph_ref[...].astype(BF16).reshape(out_morph.shape[1:])
        for k in range(1, count):
            outgoing(n, k).start()
        held[me * owned + n] = out_morph[n, rank]
        diag = lax.broadcasted_iota(I32, (table, lanes), 0) == lax.broadcasted_iota(
            I32, (table, lanes), 1
        )
        line = jnp.sum(jnp.where(diag, sed_ref[...], 0.0), axis=0, keepdims=True)
        here = lax.broadcasted_iota(I32, sed_table.shape, 0) == n
        sed_table[...] = jnp.where(here, line, sed_table[...])

        @pl.when(n + ahead < owned)
        def _():
            launch(n + ahead)

        for index, step in enumerate(steps):
            if index < owned:
                pl.when(n == index)(step)
        return carry

    lax.fori_loop(0, owned, blend, 0)
    sed_all[me] = sed_table[...].astype(BF16)
    for k in range(1, count):
        sed_copy(k).start()
    out_sed[...] = sed_table[...]
    rest = list(steps[owned:])
    while len(rest) > 1:
        rest.pop(0)()

    def settle(n, carry):
        for k in range(1, count):
            outgoing(n, k).wait_recv()
        return carry

    lax.fori_loop(0, owned, settle, 0)

    for k in range(1, GROUP + 1):
        other = lax.rem(rank + k, GROUP)

        def pick(index, carry, other=other):
            for chunk in range(CHUNKS):
                found = held[homes_ref[other, 0, chunk * per_chunk + index]]
                if k < GROUP:
                    picked[chunk, other, index] = found
                else:
                    landed[chunk, index, rank] = found
            return carry

        lax.fori_loop(0, per_chunk, pick, 0)
    for chunk in range(CHUNKS):
        for k in range(1, GROUP):
            last_copy(chunk, k).start()

    for step in rest:
        step()
    for k in range(1, count):
        sed_copy(k).wait_recv()
    out_tile[...] = jnp.zeros_like(out_tile)

    def finish(chunk, carry):
        for k in range(1, GROUP):
            last_copy(chunk, k).wait_recv()
        for index in range(per_chunk):
            piece = chunk * per_chunk + index
            home = homes_ref[rank, 0, piece]
            owner = lax.div(home, owned)
            place = home - owner * owned
            rows = sed_all[owner].astype(F32)
            here = lax.broadcasted_iota(I32, rows.shape, 0) == place
            line = jnp.sum(jnp.where(here, rows, 0.0), axis=0, keepdims=True)
            diag = lax.broadcasted_iota(I32, (table, lanes), 0) == lax.broadcasted_iota(
                I32, (table, lanes), 1
            )
            column = jnp.sum(jnp.where(diag, line, 0.0), axis=1, keepdims=True)
            sed_ref[...] = jnp.broadcast_to(column, (table, lanes))
            morph_ref[...] = landed[chunk, index].astype(F32).reshape(sources, side, side)
            for b in range(bands):
                mix = mix_band(sed_ref, morph_ref, b, bands, sources)
                left_ref[b, :, index * side : (index + 1) * side] = matmul(
                    row_psf[piece, b], mix
                ).astype(BF16)
        for b in range(bands):
            right = col_psf[b, pl.ds(chunk * per_chunk, per_chunk)].reshape(
                per_chunk * side, TILE
            )
            out_tile[b] = out_tile[b] + matmul(left_ref[b], right)
        return carry

    lax.fori_loop(0, CHUNKS, finish, 0)

    def drain(n, carry):
        for k in range(1, count):
            incoming(n, k).wait_send()
            outgoing(n, k).wait_send()
        return carry

    lax.fori_loop(0, owned, drain, 0)
    for k in range(1, count):
        sed_copy(k).wait_send()
    for chunk in range(CHUNKS):
        for k in range(1, GROUP):
            last_copy(chunk, k).wait_send()
    for k in range(1, GROUP):
        strip_copy(k).wait_send()
        base_copy(k).wait_send()
    sent_bands(ITERS, giant_ref)
    for it in range(ITERS):
        sent_bands(it, mix_buf.at[it])

        @pl.when(keeps)
        def _():
            for k in range(1, GROUP):
                grad_copy(it, k).wait_send()


def on_device(
    pieces,
    piece_blend,
    corners,
    blend_home,
    source_count,
    footprint,
    spectra,
    giant_pieces,
    giant_footprint,
    giant_spectra,
    psf_matrix,
):
    count = lax.axis_size("tiles")
    piece_count, bands, side, _ = pieces.shape
    owned = footprint.shape[0]
    blend_count = blend_home.shape[0]
    sources = spectra.shape[1]
    rows = bands * side // GROUP
    back_rows = sources * side // GROUP
    groups = count // GROUP
    lanes = side
    table = sources * bands
    strip = side // GROUP
    per_chunk = piece_count // CHUNKS

    dma = pltpu.SemaphoreType.DMA
    recv, homes = pl.pallas_call(
        functools.partial(first_kernel, piece_count),
        out_shape=(
            jax.ShapeDtypeStruct((GROUP, piece_count, rows, lanes), BF16),
            jax.ShapeDtypeStruct((GROUP, 8, lanes), I32),
        ),
        in_specs=[ANY, SMEM, SMEM],
        out_specs=(ANY, VMEM),
        scratch_shapes=[
            pltpu.VMEM((8, lanes), I32),
            dma,
            dma((GROUP - 1,)),
            dma((GROUP - 1,)),
            dma((GROUP - 1,)),
            dma((GROUP - 1,)),
        ],
        compiler_params=pltpu.CompilerParams(collective_id=0, has_side_effects=True),
        name="first",
    )(pieces.reshape(piece_count, GROUP, rows, lanes), piece_blend, blend_home)

    summed = pl.pallas_call(
        functools.partial(segment_kernel, piece_count),
        out_shape=jax.ShapeDtypeStruct((blend_count, rows, lanes), BF16),
        in_specs=[SMEM, VMEM],
        out_specs=VMEM,
        scratch_shapes=[pltpu.VMEM((blend_count, rows, lanes), F32)],
        compiler_params=pltpu.CompilerParams(vmem_limit_bytes=24 << 20),
        name="segment",
    )(homes, recv)

    chunk = (GROUP, rows, lanes)
    whole_map = (GROUP, strip, side)
    final_morph, sed_rows, tile_model, giant_morph = pl.pallas_call(
        functools.partial(core_kernel, count, bands, sources, owned, piece_count),
        out_shape=(
            jax.ShapeDtypeStruct((owned, GROUP, back_rows, lanes), BF16),
            jax.ShapeDtypeStruct((16, lanes), F32),
            jax.ShapeDtypeStruct((bands, TILE, TILE), F32),
            jax.ShapeDtypeStruct((sources, side, side), F32),
        ),
        in_specs=[SMEM, SMEM] + [VMEM] * 8,
        out_specs=(VMEM,) * 4,
        scratch_shapes=[
            pltpu.VMEM((owned, groups) + chunk, BF16),
            pltpu.VMEM((sources, side, side), F32),
            pltpu.VMEM((table, lanes), F32),
            pltpu.VMEM((table, lanes), F32),
            pltpu.VMEM((bands, side, side), F32),
            pltpu.VMEM((bands, side, side), F32),
            pltpu.VMEM((table, lanes), F32),
            pltpu.VMEM((table, lanes), F32),
            pltpu.VMEM((bands, side, side), BF16),
            pltpu.VMEM((bands, side, side), BF16),
            pltpu.VMEM((16, lanes), F32),
            pltpu.VMEM((count, 16, lanes), BF16),
            pltpu.VMEM((blend_count, back_rows, lanes), BF16),
            pltpu.VMEM((CHUNKS, GROUP, per_chunk, back_rows, lanes), BF16),
            pltpu.VMEM((CHUNKS, per_chunk, GROUP, back_rows, lanes), BF16),
            pltpu.VMEM((piece_count, bands, TILE, side), BF16),
            pltpu.VMEM((bands, piece_count, side, TILE), BF16),
            pltpu.VMEM((bands, TILE, per_chunk * side), BF16),
            pltpu.VMEM((GROUP, bands, strip, side), BF16),
            pltpu.VMEM((GROUP, strip, side), F32),
            pltpu.VMEM((ITERS + 1, GROUP) + whole_map, BF16),
            pltpu.VMEM((ITERS, bands) + whole_map, BF16),
            pltpu.VMEM((side, side), F32),
            pltpu.VMEM((table, lanes), F32),
            pltpu.VMEM((ITERS, bands, side, side), BF16),
            dma((owned, count - 1)),
            dma((owned, count - 1)),
            dma((owned, count - 1)),
            dma((owned, count - 1)),
            dma((count - 1,)),
            dma((count - 1,)),
            dma((CHUNKS, GROUP - 1)),
            dma((CHUNKS, GROUP - 1)),
            dma((GROUP - 1,)),
            dma((GROUP - 1,)),
            dma((GROUP - 1,)),
            dma((GROUP - 1,)),
            dma((ITERS + 1, bands)),
            dma((ITERS + 1, GROUP)),
            dma((ITERS, GROUP - 1)),
            dma((ITERS, bands)),
        ],
        compiler_params=pltpu.CompilerParams(
            collective_id=1, has_side_effects=True, vmem_limit_bytes=56 << 20
        ),
        name="core",
    )(
        homes,
        source_count,
        summed,
        footprint,
        spectra,
        psf_matrix,
        corners,
        giant_pieces.reshape(bands, GROUP, strip, side),
        giant_footprint,
        giant_spectra,
    )
    final_sed = sed_rows[:owned, :table].reshape(owned, sources, bands).astype(BF16)
    return (
        final_morph.reshape(owned, sources, side, side),
        final_sed,
        tile_model[None],
        giant_morph[None],
    )


def solution(mesh):
    in_specs = (
        P(("groups", "tiles"), None, None, None),
        P(("groups", "tiles")),
        P(("groups", "tiles"), None),
        P("groups"),
        P(("groups", "tiles")),
        P(("groups", "tiles"), None, None),
        P(("groups", "tiles"), None, None),
        P(("groups", "tiles"), None, None, None),
        P(("groups", "tiles"), None, None),
        P(("groups", "tiles"), None, None),
        P(),
    )
    out_specs = (
        P(("groups", "tiles"), None, None, None),
        P(("groups", "tiles"), None, None),
        P(("groups", "tiles"), None, None, None),
        P(("groups", "tiles"), None, None, None),
    )
    return jax.shard_map(
        on_device, mesh=mesh, in_specs=in_specs, out_specs=out_specs, check_vma=False
    )
```

```python
import functools

import jax
import jax.numpy as jnp
from jax import lax
from jax.experimental import pallas as pl
from jax.experimental.pallas import tpu as pltpu
from jax.sharding import PartitionSpec as P

TILE = 256
ITERS = 3
GROUP = 8
CHUNKS = 4
MESH = pl.DeviceIdType.MESH
F32 = jnp.float32
BF16 = jnp.bfloat16
I32 = jnp.int32

step_size = 0.1

VMEM = pl.BlockSpec(memory_space=pltpu.VMEM)
SMEM = pl.BlockSpec(memory_space=pltpu.SMEM)
ANY = pl.BlockSpec(memory_space=pl.ANY)


def matmul(a, b):
    return jnp.dot(a, b, preferred_element_type=F32)


def t_matmul(a, b):
    return lax.dot_general(a, b, (((0,), (0,)), ((), ())), preferred_element_type=F32)


def barrier_all(me, count):
    barrier = pltpu.get_barrier_semaphore()
    for k in range(1, count):
        pl.semaphore_signal(
            barrier, inc=1, device_id={"tiles": lax.rem(me + k, count)}, device_id_type=MESH
        )
    pl.semaphore_wait(barrier, count - 1)


def remote(src, dst, send_sem, recv_sem, peer):
    return pltpu.make_async_remote_copy(
        src_ref=src,
        dst_ref=dst,
        send_sem=send_sem,
        recv_sem=recv_sem,
        device_id={"tiles": peer},
        device_id_type=MESH,
    )


def mix_band(sed_ref, maps, b, bands, sources):
    total = sed_ref[b : b + 1, :] * maps[0]
    for k in range(1, sources):
        row = k * bands + b
        total = total + sed_ref[row : row + 1, :] * maps[k]
    return total.astype(BF16)


def update(sed_ref, morph_ref, grad_ref, part_ref, energy_ref, act_ref, bands, sources):
    for k in range(sources):
        morph = morph_ref[k]
        energy = jnp.sum(morph * morph, axis=0, keepdims=True)
        push = None
        for b in range(bands):
            row = k * bands + b
            grad = grad_ref[b]
            part_ref[row : row + 1, :] = jnp.sum(morph * grad, axis=0, keepdims=True)
            energy_ref[row : row + 1, :] = energy
            term = sed_ref[row : row + 1, :] * grad
            push = term if push is None else push + term
        fresh = jnp.maximum(morph + step_size * push, 0.0)
        if act_ref is not None:
            fresh = fresh * act_ref[k * bands : k * bands + 1, :]
        morph_ref[k] = fresh
    inner = jnp.sum(part_ref[...], axis=1, keepdims=True)
    energy = jnp.sum(energy_ref[...], axis=1, keepdims=True)
    sed = jnp.maximum(sed_ref[...] + inner / (energy + 1.0), 0.0)
    if act_ref is not None:
        sed = sed * act_ref[...]
    sed_ref[...] = sed


def spread_rows(sed_ref, table, bands, sources, lanes):
    for k in range(sources):
        line = jnp.broadcast_to(table[k : k + 1, :], (bands, bands))
        row = lax.broadcasted_iota(I32, (bands, bands), 0)
        col = lax.broadcasted_iota(I32, (bands, bands), 1)
        value = jnp.sum(jnp.where(row == col, line, 0.0), axis=1, keepdims=True)
        sed_ref[k * bands : (k + 1) * bands, :] = jnp.broadcast_to(value, (bands, lanes))


def sort_tables(homes_ref, lanes):
    line = homes_ref[0]
    for source in range(1, GROUP):
        line = line + homes_ref[source]
    across = jnp.broadcast_to(line[0:1, :], (lanes, lanes))
    sub = lax.broadcasted_iota(I32, (lanes, lanes), 0)
    lane = lax.broadcasted_iota(I32, (lanes, lanes), 1)
    down = jnp.sum(jnp.where(sub == lane, across, 0), axis=1, keepdims=True)
    key_across = across * lanes + lane
    key_down = down * lanes + sub
    place = jnp.sum(jnp.where(key_across < key_down, 1, 0), axis=1, keepdims=True)
    order = jnp.sum(jnp.where(place == lane, sub, 0), axis=0, keepdims=True)
    sorted_home = jnp.sum(jnp.where(place == lane, down, 0), axis=0, keepdims=True)
    before = jnp.sum(jnp.where(place + 1 == lane, down, 0), axis=0, keepdims=True)
    keep = jnp.where(sorted_home == before, 1, 0)
    upto = jnp.sum(jnp.where(down <= lane, 1, 0), axis=0, keepdims=True)
    same = jnp.sum(jnp.where(down == lane, 1, 0), axis=0, keepdims=True)
    last = jnp.maximum(upto - 1, 0)
    some = jnp.where(same > 0, 1, 0)
    rows = [order, keep, last, some]
    which = lax.broadcasted_iota(I32, (8, lanes), 0)
    result = jnp.where(which == len(rows), line, 0)
    for index, row in enumerate(rows):
        result = jnp.where(which == index, row, result)
    return result


def core_kernel(
    count,
    bands,
    sources,
    owned,
    piece_count,
    blend_ref,
    home_of_ref,
    counts_ref,
    pieces_ref,
    labels_ref,
    spectra_ref,
    psf_ref,
    corners_ref,
    giant_ref,
    giant_labels_ref,
    giant_spectra_ref,
    out_morph,
    out_sed,
    out_tile,
    out_giant,
    homes_ref,
    table_vmem,
    table_ref,
    running,
    summed,
    piece_bufs,
    arrived,
    morph_ref,
    sed_ref,
    act_ref,
    adj_ref,
    grad_ref,
    part_ref,
    energy_ref,
    gram,
    psf_t,
    sed_table,
    sed_all,
    held,
    picked,
    landed,
    row_psf,
    col_psf,
    left_ref,
    strips,
    base_buf,
    band_buf,
    mix_buf,
    adj_own,
    giant_sed,
    giant_grad,
    own_sem,
    table_sem,
    home_send,
    home_recv,
    piece_send,
    piece_recv,
    in_send,
    in_recv,
    back_send,
    back_recv,
    sed_send,
    sed_recv,
    last_send,
    last_recv,
    strip_send,
    strip_recv,
    base_send,
    base_recv,
    band_send,
    band_recv,
    grad_send,
    grad_recv,
):
    me = lax.axis_index("tiles")
    rank = lax.rem(me, GROUP)
    base = me - rank
    mine = me // GROUP
    groups = count // GROUP
    side = labels_ref.shape[1]
    lanes = side
    strip = side // GROUP
    table = bands * sources
    half = (bands + 1) // 2
    per_chunk = piece_count // CHUNKS
    barrier_all(me, count)

    def keeper(b):
        return (b // half) * (GROUP // 2) + b % half

    upper = rank // (GROUP // 2)
    lower = lax.rem(rank, GROUP // 2)
    own_band = upper * half + lower
    keeps = jnp.logical_and(lower < half, own_band < bands)
    safe_band = jnp.where(keeps, own_band, 0)

    def home_copy(k):
        other = lax.rem(rank + k, GROUP)
        return remote(
            homes_ref.at[rank], homes_ref.at[rank], home_send.at[k - 1], home_recv.at[k - 1],
            base + other,
        )

    def piece_slot(b):
        return piece_bufs[b].at[pl.ds(rank * piece_count, piece_count)]

    def piece_copy(b, k):
        other = lax.rem(rank + k, GROUP)
        return remote(
            pieces_ref.at[:, b, other], piece_slot(b), piece_send.at[b, k - 1],
            piece_recv.at[b, k - 1], base + other,
        )

    def own_copy(b):
        return pltpu.make_async_copy(pieces_ref.at[:, b, rank], piece_slot(b), own_sem.at[b])

    def incoming(b, k):
        peer = lax.rem(me + k, count)
        return remote(
            summed.at[b, pl.ds(peer * owned, owned)],
            arrived.at[b, mine, rank],
            in_send.at[b, k - 1],
            in_recv.at[b, k - 1],
            peer,
        )

    def outgoing(n, k):
        peer = lax.rem(me + k, count)
        return remote(
            out_morph.at[n, lax.rem(peer, GROUP)],
            held.at[me * owned + n],
            back_send.at[n, k - 1],
            back_recv.at[n, k - 1],
            peer,
        )

    def sed_copy(k):
        return remote(
            sed_all.at[me], sed_all.at[me], sed_send.at[k - 1], sed_recv.at[k - 1],
            lax.rem(me + k, count),
        )

    def last_copy(chunk, k):
        other = lax.rem(rank + k, GROUP)
        return remote(
            picked.at[chunk, other],
            landed.at[chunk, :, rank],
            last_send.at[chunk, k - 1],
            last_recv.at[chunk, k - 1],
            base + other,
        )

    def strip_copy(k):
        other = lax.rem(rank + k, GROUP)
        return remote(
            giant_ref.at[:, other], strips.at[rank], strip_send.at[k - 1], strip_recv.at[k - 1],
            base + other,
        )

    def base_copy(k):
        other = lax.rem(rank + k, GROUP)
        return remote(
            base_buf.at[rank], base_buf.at[rank], base_send.at[k - 1], base_recv.at[k - 1],
            base + other,
        )

    def band_copy(slot, src, b):
        return remote(
            src, band_buf.at[slot, rank], band_send.at[slot, b], band_recv.at[slot, rank],
            base + keeper(b),
        )

    def grad_copy(slot, k):
        other = lax.rem(rank + k, GROUP)
        return remote(
            giant_grad.at[slot, safe_band],
            giant_grad.at[slot, safe_band],
            grad_send.at[slot, k - 1],
            grad_recv.at[slot, safe_band],
            base + other,
        )

    def send_bands(slot, ref):
        for b in range(bands):
            @pl.when(rank != keeper(b))
            def _():
                band_copy(slot, ref.at[b], b).start()

            @pl.when(rank == keeper(b))
            def _():
                band_buf[slot, rank] = ref[b]

    def sent_bands(slot, ref):
        for b in range(bands):
            @pl.when(rank != keeper(b))
            def _():
                band_copy(slot, ref.at[b], b).wait_send()

    def kept_sum(slot):
        for k in range(1, GROUP):
            source = lax.rem(rank + k, GROUP)
            pltpu.make_async_remote_copy(
                src_ref=band_buf.at[slot, source],
                dst_ref=band_buf.at[slot, source],
                send_sem=band_send.at[slot, 0],
                recv_sem=band_recv.at[slot, source],
                device_id={"tiles": base + source},
                device_id_type=MESH,
            ).wait_recv()
        total = band_buf[slot, 0].astype(F32)
        for source in range(1, GROUP):
            total = total + band_buf[slot, source].astype(F32)
        return total.reshape(side, side).astype(BF16)

    def giant_open():
        for k in range(1, GROUP):
            strip_copy(k).wait_recv()
        mean = None
        for k in range(GROUP):
            source = lax.rem(rank + k, GROUP)
            part = giant_ref[:, rank] if k == 0 else strips[source]
            part = jnp.sum(part.astype(F32), axis=0)
            mean = part if mean is None else mean + part
        base_buf[rank] = jnp.maximum(mean / bands, 0.0)
        for k in range(1, GROUP):
            base_copy(k).start()

        @pl.when(keeps)
        def _():
            total = kept_sum(ITERS)
            back = matmul(psf_t[safe_band], total).astype(BF16)
            adj_own[...] = matmul(back, psf_ref[safe_band])

    def giant_mix(slot):
        for b in range(bands):
            mix = mix_band(giant_sed, out_giant, b, bands, sources)
            mix_buf[slot, b] = mix.reshape(GROUP, strip, side)
        send_bands(slot, mix_buf.at[slot])

    def giant_start():
        for k in range(1, GROUP):
            base_copy(k).wait_recv()
        base_map = base_buf[...].reshape(side, side)
        for k in range(sources):
            out_giant[k] = jnp.where(giant_labels_ref[0] == k + 1, base_map, 0.0)
        spread_rows(giant_sed, giant_spectra_ref[0], bands, sources, lanes)
        giant_mix(0)

    def giant_keep(slot):
        @pl.when(keeps)
        def _():
            total = kept_sum(slot)
            gram_own = gram[safe_band]
            grad = adj_own[...] - matmul(matmul(gram_own, total).astype(BF16), gram_own)
            giant_grad[slot, safe_band] = grad.astype(BF16)
            for k in range(1, GROUP):
                grad_copy(slot, k).start()

    def giant_update(slot):
        for b in range(bands):
            @pl.when(rank != keeper(b))
            def _():
                pltpu.make_async_remote_copy(
                    src_ref=giant_grad.at[slot, b],
                    dst_ref=giant_grad.at[slot, b],
                    send_sem=grad_send.at[slot, 0],
                    recv_sem=grad_recv.at[slot, b],
                    device_id={"tiles": base + keeper(b)},
                    device_id_type=MESH,
                ).wait_recv()

        for b in range(bands):
            grad_ref[b] = giant_grad[slot, b].astype(F32)
        update(giant_sed, out_giant, grad_ref, part_ref, energy_ref, None, bands, sources)

    steps = [giant_start]
    for it in range(ITERS):
        steps.append(functools.partial(giant_keep, it))
        if it < ITERS - 1:

            def advance(it=it):
                giant_update(it)
                giant_mix(it + 1)

            steps.append(advance)
        else:
            steps.append(functools.partial(giant_update, it))

    def launch(b):
        for k in range(1, GROUP):
            piece_copy(b, k).start()
        own_copy(b).start()

    at = lax.broadcasted_iota(I32, (8, lanes), 1) - rank * piece_count
    line = jnp.zeros((8, lanes), I32)
    for index in range(piece_count):
        line = jnp.where(at == index, home_of_ref[blend_ref[index]], line)
    homes_ref[rank] = line
    for k in range(1, GROUP):
        home_copy(k).start()
    ahead = 2
    launch(0)
    for k in range(1, GROUP):
        strip_copy(k).start()
    send_bands(ITERS, giant_ref)
    for b in range(1, min(ahead, bands)):
        launch(b)

    for b in range(bands):
        psf = psf_ref[b]
        gram[b] = t_matmul(psf, psf).astype(BF16)
        psf_t[b] = jnp.transpose(psf.astype(F32)).astype(BF16)
    for k in range(1, GROUP):
        home_copy(k).wait_recv()
    table_vmem[...] = sort_tables(homes_ref, lanes)
    to_scalar = pltpu.make_async_copy(table_vmem, table_ref, table_sem)
    to_scalar.start()
    to_scalar.wait()

    def prepare(index, carry):
        row_at = corners_ref[pl.ds(index, 1), 0:1]
        col_at = corners_ref[pl.ds(index, 1), 1:2]
        rows = lax.broadcasted_iota(I32, (TILE, side), 0)
        inner = lax.broadcasted_iota(I32, (TILE, side), 1)
        row_hot = jnp.where(rows == inner + row_at, 1.0, 0.0).astype(BF16)
        cols = lax.broadcasted_iota(I32, (side, TILE), 1)
        inner_c = lax.broadcasted_iota(I32, (side, TILE), 0)
        col_hot = jnp.where(cols == inner_c + col_at, 1.0, 0.0).astype(BF16)
        for b in range(bands):
            row_psf[index, b] = matmul(row_hot, psf_ref[b]).astype(BF16)
            col_psf[b, index] = matmul(psf_t[b], col_hot).astype(BF16)
        return carry

    sed_table[...] = jnp.zeros_like(sed_table)

    early = [giant_open] + steps[: bands - 1]
    steps = steps[bands - 1 :]
    for b in range(bands):
        for k in range(1, GROUP):
            piece_copy(b, k).wait_recv()
        own_copy(b).wait()
        band_pieces = piece_bufs[b]

        def add(index, total, band_pieces=band_pieces):
            keep = table_ref[1, index].astype(F32)
            total = total * keep + band_pieces[table_ref[0, index]].astype(F32)
            running[index] = total
            return total

        lax.fori_loop(0, GROUP * piece_count, add, jnp.zeros((strip, lanes), F32), unroll=8)

        def put(home, carry, b=b):
            some = table_ref[3, home].astype(F32)
            summed[b, home] = (running[table_ref[2, home]] * some).astype(BF16)
            return carry

        lax.fori_loop(0, count * owned, put, 0, unroll=8)
        for k in range(1, count):
            incoming(b, k).start()
        arrived[b, mine, rank] = summed[b, pl.ds(me * owned, owned)]
        if b + ahead < bands:
            launch(b + ahead)
        if b == 0:
            lax.fori_loop(0, piece_count, prepare, 0)
        if b < len(early):
            early[b]()

    for b in range(bands):
        for k in range(1, count):
            incoming(b, k).wait_recv()

    def blend(n, carry):
        source_of_row = lax.broadcasted_iota(I32, (table, lanes), 0) // bands
        act_ref[...] = jnp.where(source_of_row < counts_ref[n], 1.0, 0.0)
        spread_rows(sed_ref, spectra_ref[n], bands, sources, lanes)
        sed_ref[...] = sed_ref[...] * act_ref[...]
        for b in range(bands):
            total = arrived[b, 0, :, n].astype(F32)
            for g in range(1, groups):
                total = total + arrived[b, g, :, n].astype(F32)
            grad_ref[b] = total.reshape(side, side)
        mean = grad_ref[0]
        for b in range(1, bands):
            mean = mean + grad_ref[b]
        base_map = jnp.maximum(mean / bands, 0.0)
        for k in range(sources):
            morph_ref[k] = (
                jnp.where(labels_ref[n] == k + 1, base_map, 0.0)
                * act_ref[k * bands : k * bands + 1, :]
            )
        for b in range(bands):
            back = matmul(psf_t[b], grad_ref[b].astype(BF16)).astype(BF16)
            adj_ref[b] = matmul(back, psf_ref[b])

        def iteration(it, carry):
            for b in range(bands):
                mix = mix_band(sed_ref, morph_ref, b, bands, sources)
                grad_ref[b] = adj_ref[b] - matmul(matmul(gram[b], mix).astype(BF16), gram[b])
            update(sed_ref, morph_ref, grad_ref, part_ref, energy_ref, act_ref, bands, sources)
            return carry

        lax.fori_loop(0, ITERS, iteration, 0)
        out_morph[n] = morph_ref[...].astype(BF16).reshape(out_morph.shape[1:])
        for k in range(1, count):
            outgoing(n, k).start()
        held[me * owned + n] = out_morph[n, rank]
        diag = lax.broadcasted_iota(I32, (table, lanes), 0) == lax.broadcasted_iota(
            I32, (table, lanes), 1
        )
        line = jnp.sum(jnp.where(diag, sed_ref[...], 0.0), axis=0, keepdims=True)
        here = lax.broadcasted_iota(I32, sed_table.shape, 0) == n
        sed_table[...] = jnp.where(here, line, sed_table[...])

        for index, step in enumerate(steps):
            if index < owned:
                pl.when(n == index)(step)
        return carry

    lax.fori_loop(0, owned, blend, 0)
    sed_all[me] = sed_table[...].astype(BF16)
    for k in range(1, count):
        sed_copy(k).start()
    out_sed[...] = sed_table[...]
    rest = list(steps[owned:])
    while len(rest) > 1:
        rest.pop(0)()

    def settle(n, carry):
        for k in range(1, count):
            outgoing(n, k).wait_recv()
        return carry

    lax.fori_loop(0, owned, settle, 0)

    for k in range(1, GROUP + 1):
        other = lax.rem(rank + k, GROUP)

        def pick(index, carry, other=other):
            for chunk in range(CHUNKS):
                found = held[table_ref[4, other * piece_count + chunk * per_chunk + index]]
                if k < GROUP:
                    picked[chunk, other, index] = found
                else:
                    landed[chunk, index, rank] = found
            return carry

        lax.fori_loop(0, per_chunk, pick, 0)
    for chunk in range(CHUNKS):
        for k in range(1, GROUP):
            last_copy(chunk, k).start()

    for step in rest:
        step()
    for k in range(1, count):
        sed_copy(k).wait_recv()
    out_tile[...] = jnp.zeros_like(out_tile)

    def finish(chunk, carry):
        for k in range(1, GROUP):
            last_copy(chunk, k).wait_recv()
        for index in range(per_chunk):
            piece = chunk * per_chunk + index
            home = table_ref[4, rank * piece_count + piece]
            owner = lax.div(home, owned)
            place = home - owner * owned
            rows = sed_all[owner].astype(F32)
            here = lax.broadcasted_iota(I32, rows.shape, 0) == place
            line = jnp.sum(jnp.where(here, rows, 0.0), axis=0, keepdims=True)
            diag = lax.broadcasted_iota(I32, (table, lanes), 0) == lax.broadcasted_iota(
                I32, (table, lanes), 1
            )
            column = jnp.sum(jnp.where(diag, line, 0.0), axis=1, keepdims=True)
            sed_ref[...] = jnp.broadcast_to(column, (table, lanes))
            morph_ref[...] = landed[chunk, index].astype(F32).reshape(sources, side, side)
            for b in range(bands):
                mix = mix_band(sed_ref, morph_ref, b, bands, sources)
                left_ref[b, :, index * side : (index + 1) * side] = matmul(
                    row_psf[piece, b], mix
                ).astype(BF16)
        for b in range(bands):
            right = col_psf[b, pl.ds(chunk * per_chunk, per_chunk)].reshape(
                per_chunk * side, TILE
            )
            out_tile[b] = out_tile[b] + matmul(left_ref[b], right)
        return carry

    lax.fori_loop(0, CHUNKS, finish, 0)

    def drain(n, carry):
        for k in range(1, count):
            outgoing(n, k).wait_send()
        return carry

    lax.fori_loop(0, owned, drain, 0)
    for b in range(bands):
        for k in range(1, GROUP):
            piece_copy(b, k).wait_send()
        for k in range(1, count):
            incoming(b, k).wait_send()
    for k in range(1, GROUP):
        home_copy(k).wait_send()
    for k in range(1, count):
        sed_copy(k).wait_send()
    for chunk in range(CHUNKS):
        for k in range(1, GROUP):
            last_copy(chunk, k).wait_send()
    for k in range(1, GROUP):
        strip_copy(k).wait_send()
        base_copy(k).wait_send()
    sent_bands(ITERS, giant_ref)
    for it in range(ITERS):
        sent_bands(it, mix_buf.at[it])

        @pl.when(keeps)
        def _():
            for k in range(1, GROUP):
                grad_copy(it, k).wait_send()


def on_device(
    pieces,
    piece_blend,
    corners,
    blend_home,
    source_count,
    footprint,
    spectra,
    giant_pieces,
    giant_footprint,
    giant_spectra,
    psf_matrix,
):
    count = lax.axis_size("tiles")
    piece_count, bands, side, _ = pieces.shape
    owned = footprint.shape[0]
    blend_count = blend_home.shape[0]
    sources = spectra.shape[1]
    back_rows = sources * side // GROUP
    groups = count // GROUP
    lanes = side
    table = sources * bands
    strip = side // GROUP
    per_chunk = piece_count // CHUNKS

    dma = pltpu.SemaphoreType.DMA
    whole_map = (GROUP, strip, side)
    final_morph, sed_rows, tile_model, giant_morph = pl.pallas_call(
        functools.partial(core_kernel, count, bands, sources, owned, piece_count),
        out_shape=(
            jax.ShapeDtypeStruct((owned, GROUP, back_rows, lanes), BF16),
            jax.ShapeDtypeStruct((16, lanes), F32),
            jax.ShapeDtypeStruct((bands, TILE, TILE), F32),
            jax.ShapeDtypeStruct((sources, side, side), F32),
        ),
        in_specs=[SMEM, SMEM, SMEM, ANY] + [VMEM] * 7,
        out_specs=(VMEM,) * 4,
        scratch_shapes=[
            pltpu.VMEM((GROUP, 8, lanes), I32),
            pltpu.VMEM((8, lanes), I32),
            pltpu.SMEM((8, lanes), I32),
            pltpu.VMEM((GROUP * piece_count, strip, lanes), F32),
            pltpu.VMEM((bands, blend_count, strip, lanes), BF16),
            [pltpu.VMEM((GROUP * piece_count, strip, lanes), BF16) for _ in range(bands)],
            pltpu.VMEM((bands, groups, GROUP, owned, strip, lanes), BF16),
            pltpu.VMEM((sources, side, side), F32),
            pltpu.VMEM((table, lanes), F32),
            pltpu.VMEM((table, lanes), F32),
            pltpu.VMEM((bands, side, side), F32),
            pltpu.VMEM((bands, side, side), F32),
            pltpu.VMEM((table, lanes), F32),
            pltpu.VMEM((table, lanes), F32),
            pltpu.VMEM((bands, side, side), BF16),
            pltpu.VMEM((bands, side, side), BF16),
            pltpu.VMEM((16, lanes), F32),
            pltpu.VMEM((count, 16, lanes), BF16),
            pltpu.VMEM((blend_count, back_rows, lanes), BF16),
            pltpu.VMEM((CHUNKS, GROUP, per_chunk, back_rows, lanes), BF16),
            pltpu.VMEM((CHUNKS, per_chunk, GROUP, back_rows, lanes), BF16),
            pltpu.VMEM((piece_count, bands, TILE, side), BF16),
            pltpu.VMEM((bands, piece_count, side, TILE), BF16),
            pltpu.VMEM((bands, TILE, per_chunk * side), BF16),
            pltpu.VMEM((GROUP, bands, strip, side), BF16),
            pltpu.VMEM((GROUP, strip, side), F32),
            pltpu.VMEM((ITERS + 1, GROUP) + whole_map, BF16),
            pltpu.VMEM((ITERS, bands) + whole_map, BF16),
            pltpu.VMEM((side, side), F32),
            pltpu.VMEM((table, lanes), F32),
            pltpu.VMEM((ITERS, bands, side, side), BF16),
            dma((bands,)),
            dma,
            dma((GROUP - 1,)),
            dma((GROUP - 1,)),
            dma((bands, GROUP - 1)),
            dma((bands, GROUP - 1)),
            dma((bands, count - 1)),
            dma((bands, count - 1)),
            dma((owned, count - 1)),
            dma((owned, count - 1)),
            dma((count - 1,)),
            dma((count - 1,)),
            dma((CHUNKS, GROUP - 1)),
            dma((CHUNKS, GROUP - 1)),
            dma((GROUP - 1,)),
            dma((GROUP - 1,)),
            dma((GROUP - 1,)),
            dma((GROUP - 1,)),
            dma((ITERS + 1, bands)),
            dma((ITERS + 1, GROUP)),
            dma((ITERS, GROUP - 1)),
            dma((ITERS, bands)),
        ],
        compiler_params=pltpu.CompilerParams(
            collective_id=0, has_side_effects=True, vmem_limit_bytes=56 << 20
        ),
        name="core",
    )(
        piece_blend,
        blend_home,
        source_count,
        pieces.reshape(piece_count, bands, GROUP, strip, side),
        footprint,
        spectra,
        psf_matrix,
        corners,
        giant_pieces.reshape(bands, GROUP, strip, side),
        giant_footprint,
        giant_spectra,
    )
    final_sed = sed_rows[:owned, :table].reshape(owned, sources, bands).astype(BF16)
    return (
        final_morph.reshape(owned, sources, side, side),
        final_sed,
        tile_model[None],
        giant_morph[None],
    )


def solution(mesh):
    in_specs = (
        P(("groups", "tiles"), None, None, None),
        P(("groups", "tiles")),
        P(("groups", "tiles"), None),
        P("groups"),
        P(("groups", "tiles")),
        P(("groups", "tiles"), None, None),
        P(("groups", "tiles"), None, None),
        P(("groups", "tiles"), None, None, None),
        P(("groups", "tiles"), None, None),
        P(("groups", "tiles"), None, None),
        P(),
    )
    out_specs = (
        P(("groups", "tiles"), None, None, None),
        P(("groups", "tiles"), None, None),
        P(("groups", "tiles"), None, None, None),
        P(("groups", "tiles"), None, None, None),
    )
    return jax.shard_map(
        on_device, mesh=mesh, in_specs=in_specs, out_specs=out_specs, check_vma=False
    )
```

```python
import functools

import jax
import jax.numpy as jnp
from jax import lax
from jax.experimental import pallas as pl
from jax.experimental.pallas import tpu as pltpu
from jax.sharding import PartitionSpec as P

TILE = 256
ITERS = 3
GROUP = 8
QUAD = 4
CHUNKS = 4
MESH = pl.DeviceIdType.MESH
F32 = jnp.float32
BF16 = jnp.bfloat16
I32 = jnp.int32

step_size = 0.1

VMEM = pl.BlockSpec(memory_space=pltpu.VMEM)
SMEM = pl.BlockSpec(memory_space=pltpu.SMEM)
ANY = pl.BlockSpec(memory_space=pl.ANY)


def matmul(a, b):
    return jnp.dot(a, b, preferred_element_type=F32)


def t_matmul(a, b):
    return lax.dot_general(a, b, (((0,), (0,)), ((), ())), preferred_element_type=F32)


def barrier_all(me, count):
    barrier = pltpu.get_barrier_semaphore()
    for k in range(1, count):
        pl.semaphore_signal(
            barrier, inc=1, device_id={"tiles": lax.rem(me + k, count)}, device_id_type=MESH
        )
    pl.semaphore_wait(barrier, count - 1)


def remote(src, dst, send_sem, recv_sem, peer):
    return pltpu.make_async_remote_copy(
        src_ref=src,
        dst_ref=dst,
        send_sem=send_sem,
        recv_sem=recv_sem,
        device_id={"tiles": peer},
        device_id_type=MESH,
    )


def mix_band(sed_ref, maps, b, bands, sources):
    total = sed_ref[b : b + 1, :] * maps[0]
    for k in range(1, sources):
        row = k * bands + b
        total = total + sed_ref[row : row + 1, :] * maps[k]
    return total.astype(BF16)


def update(sed_ref, morph_ref, grad_ref, part_ref, energy_ref, act_ref, bands, sources):
    for k in range(sources):
        morph = morph_ref[k]
        energy = jnp.sum(morph * morph, axis=0, keepdims=True)
        push = None
        for b in range(bands):
            row = k * bands + b
            grad = grad_ref[b]
            part_ref[row : row + 1, :] = jnp.sum(morph * grad, axis=0, keepdims=True)
            energy_ref[row : row + 1, :] = energy
            term = sed_ref[row : row + 1, :] * grad
            push = term if push is None else push + term
        fresh = jnp.maximum(morph + step_size * push, 0.0)
        if act_ref is not None:
            fresh = fresh * act_ref[k * bands : k * bands + 1, :]
        morph_ref[k] = fresh
    inner = jnp.sum(part_ref[...], axis=1, keepdims=True)
    energy = jnp.sum(energy_ref[...], axis=1, keepdims=True)
    sed = jnp.maximum(sed_ref[...] + inner / (energy + 1.0), 0.0)
    if act_ref is not None:
        sed = sed * act_ref[...]
    sed_ref[...] = sed


def spread_rows(sed_ref, table, bands, sources, lanes):
    for k in range(sources):
        line = jnp.broadcast_to(table[k : k + 1, :], (bands, bands))
        row = lax.broadcasted_iota(I32, (bands, bands), 0)
        col = lax.broadcasted_iota(I32, (bands, bands), 1)
        value = jnp.sum(jnp.where(row == col, line, 0.0), axis=1, keepdims=True)
        sed_ref[k * bands : (k + 1) * bands, :] = jnp.broadcast_to(value, (bands, lanes))


def sort_tables(homes_ref, upper, used, lanes):
    line = homes_ref[0]
    for source in range(1, GROUP):
        line = line + homes_ref[source]
    near = jnp.where(upper == 0, line[0:1, :], line[1:2, :])
    near = jnp.where(lax.broadcasted_iota(I32, (1, lanes), 1) < used, near, 2 * lanes)
    across = jnp.broadcast_to(near, (lanes, lanes))
    sub = lax.broadcasted_iota(I32, (lanes, lanes), 0)
    lane = lax.broadcasted_iota(I32, (lanes, lanes), 1)
    down = jnp.sum(jnp.where(sub == lane, across, 0), axis=1, keepdims=True)
    key_across = across * lanes + lane
    key_down = down * lanes + sub
    place = jnp.sum(jnp.where(key_across < key_down, 1, 0), axis=1, keepdims=True)
    order = jnp.sum(jnp.where(place == lane, sub, 0), axis=0, keepdims=True)
    sorted_home = jnp.sum(jnp.where(place == lane, down, 0), axis=0, keepdims=True)
    before = jnp.sum(jnp.where(place + 1 == lane, down, 0), axis=0, keepdims=True)
    keep = jnp.where(sorted_home == before, 1, 0)
    upto = jnp.sum(jnp.where(down <= lane, 1, 0), axis=0, keepdims=True)
    same = jnp.sum(jnp.where(down == lane, 1, 0), axis=0, keepdims=True)
    last = jnp.maximum(upto - 1, 0)
    some = jnp.where(same > 0, 1, 0)
    rows = [order, keep, last, some]
    for half in range(GROUP // QUAD):
        rows.append(line[half : half + 1, :])
    which = lax.broadcasted_iota(I32, (8, lanes), 0)
    result = jnp.zeros((8, lanes), I32)
    for index, row in enumerate(rows):
        result = jnp.where(which == index, row, result)
    return result


def core_kernel(
    count,
    bands,
    sources,
    owned,
    piece_count,
    blend_ref,
    home_of_ref,
    counts_ref,
    pieces_ref,
    labels_ref,
    spectra_ref,
    psf_ref,
    corners_ref,
    giant_ref,
    giant_labels_ref,
    giant_spectra_ref,
    out_morph,
    out_sed,
    out_tile,
    out_giant,
    homes_ref,
    table_vmem,
    table_ref,
    running,
    aside,
    pair_buf,
    summed,
    piece_bufs,
    arrived,
    morph_ref,
    sed_ref,
    act_ref,
    adj_ref,
    grad_ref,
    part_ref,
    energy_ref,
    gram,
    psf_t,
    sed_table,
    sed_all,
    held,
    picked,
    landed,
    row_psf,
    col_psf,
    left_ref,
    strips,
    base_buf,
    band_buf,
    mix_buf,
    adj_own,
    giant_sed,
    giant_grad,
    own_sem,
    table_sem,
    home_send,
    home_recv,
    piece_send,
    piece_recv,
    pair_send,
    pair_recv,
    in_send,
    in_recv,
    back_send,
    back_recv,
    sed_send,
    sed_recv,
    last_send,
    last_recv,
    strip_send,
    strip_recv,
    base_send,
    base_recv,
    band_send,
    band_recv,
    grad_send,
    grad_recv,
):
    me = lax.axis_index("tiles")
    rank = lax.rem(me, GROUP)
    base = me - rank
    mine = me // GROUP
    side = labels_ref.shape[1]
    lanes = side
    strip = side // GROUP
    quarter = side // QUAD
    quads = count // QUAD
    near_blends = QUAD * owned
    table = bands * sources
    half = (bands + 1) // 2
    per_chunk = piece_count // CHUNKS
    barrier_all(me, count)

    def keeper(b):
        return (b // half) * (GROUP // 2) + b % half

    upper = rank // QUAD
    lower = lax.rem(rank, QUAD)
    own_band = upper * half + lower
    keeps = jnp.logical_and(lower < half, own_band < bands)
    safe_band = jnp.where(keeps, own_band, 0)

    def home_copy(k):
        other = lax.rem(rank + k, GROUP)
        return remote(
            homes_ref.at[rank], homes_ref.at[rank], home_send.at[k - 1], home_recv.at[k - 1],
            base + other,
        )

    quad = me // QUAD
    pair = quad // 2
    parity = lax.rem(quad, 2)

    def piece_slot(b):
        return piece_bufs[b].at[pl.ds(lower * piece_count, piece_count)]

    def piece_copy(b, k):
        other = lax.rem(lower + k, QUAD)
        return remote(
            pieces_ref.at[:, b, other], piece_slot(b), piece_send.at[b, k - 1],
            piece_recv.at[b, k - 1], quad * QUAD + other,
        )

    def own_copy(b):
        return pltpu.make_async_copy(pieces_ref.at[:, b, lower], piece_slot(b), own_sem.at[b])

    def pair_copy(b):
        partner = (quad + 1 - 2 * parity) * QUAD + lower
        return remote(aside.at[b], pair_buf.at[b], pair_send.at[b], pair_recv.at[b], partner)

    def incoming(b, k):
        to_pair = lax.rem(pair + k // QUAD, quads // 2)
        to_lower = lax.rem(lower + k % QUAD, QUAD)
        return remote(
            summed.at[b, to_pair, pl.ds(to_lower * owned, owned)],
            arrived.at[b, pair, lower],
            in_send.at[b, k - 1],
            in_recv.at[b, k - 1],
            (2 * to_pair + parity) * QUAD + to_lower,
        )

    owners = quads // 2 * QUAD

    def outgoing(n, k):
        peer = lax.rem(me + k, count)
        return remote(
            out_morph.at[n, lax.rem(peer, GROUP)],
            held.at[me * owned + n],
            back_send.at[n, k - 1],
            back_recv.at[n, k - 1],
            peer,
        )

    def sed_copy(k):
        return remote(
            sed_all.at[me], sed_all.at[me], sed_send.at[k - 1], sed_recv.at[k - 1],
            lax.rem(me + k, count),
        )

    def last_copy(chunk, k):
        other = lax.rem(rank + k, GROUP)
        return remote(
            picked.at[chunk, other],
            landed.at[chunk, :, rank],
            last_send.at[chunk, k - 1],
            last_recv.at[chunk, k - 1],
            base + other,
        )

    def strip_copy(k):
        other = lax.rem(rank + k, GROUP)
        return remote(
            giant_ref.at[:, other], strips.at[rank], strip_send.at[k - 1], strip_recv.at[k - 1],
            base + other,
        )

    def base_copy(k):
        other = lax.rem(rank + k, GROUP)
        return remote(
            base_buf.at[rank], base_buf.at[rank], base_send.at[k - 1], base_recv.at[k - 1],
            base + other,
        )

    def band_copy(slot, src, b):
        return remote(
            src, band_buf.at[slot, rank], band_send.at[slot, b], band_recv.at[slot, rank],
            base + keeper(b),
        )

    def grad_copy(slot, k):
        other = lax.rem(rank + k, GROUP)
        return remote(
            giant_grad.at[slot, safe_band],
            giant_grad.at[slot, safe_band],
            grad_send.at[slot, k - 1],
            grad_recv.at[slot, safe_band],
            base + other,
        )

    def send_bands(slot, ref):
        for b in range(bands):
            @pl.when(rank != keeper(b))
            def _():
                band_copy(slot, ref.at[b], b).start()

            @pl.when(rank == keeper(b))
            def _():
                band_buf[slot, rank] = ref[b]

    def sent_bands(slot, ref):
        for b in range(bands):
            @pl.when(rank != keeper(b))
            def _():
                band_copy(slot, ref.at[b], b).wait_send()

    def kept_sum(slot):
        for k in range(1, GROUP):
            source = lax.rem(rank + k, GROUP)
            pltpu.make_async_remote_copy(
                src_ref=band_buf.at[slot, source],
                dst_ref=band_buf.at[slot, source],
                send_sem=band_send.at[slot, 0],
                recv_sem=band_recv.at[slot, source],
                device_id={"tiles": base + source},
                device_id_type=MESH,
            ).wait_recv()
        total = band_buf[slot, 0].astype(F32)
        for source in range(1, GROUP):
            total = total + band_buf[slot, source].astype(F32)
        return total.reshape(side, side).astype(BF16)

    def giant_open():
        for k in range(1, GROUP):
            strip_copy(k).wait_recv()
        mean = None
        for k in range(GROUP):
            source = lax.rem(rank + k, GROUP)
            part = giant_ref[:, rank] if k == 0 else strips[source]
            part = jnp.sum(part.astype(F32), axis=0)
            mean = part if mean is None else mean + part
        base_buf[rank] = jnp.maximum(mean / bands, 0.0)
        for k in range(1, GROUP):
            base_copy(k).start()

        @pl.when(keeps)
        def _():
            total = kept_sum(ITERS)
            back = matmul(psf_t[safe_band], total).astype(BF16)
            adj_own[...] = matmul(back, psf_ref[safe_band])

    def giant_mix(slot):
        for b in range(bands):
            mix = mix_band(giant_sed, out_giant, b, bands, sources)
            mix_buf[slot, b] = mix.reshape(GROUP, strip, side)
        send_bands(slot, mix_buf.at[slot])

    def giant_start():
        for k in range(1, GROUP):
            base_copy(k).wait_recv()
        base_map = base_buf[...].reshape(side, side)
        for k in range(sources):
            out_giant[k] = jnp.where(giant_labels_ref[0] == k + 1, base_map, 0.0)
        spread_rows(giant_sed, giant_spectra_ref[0], bands, sources, lanes)
        giant_mix(0)

    def giant_keep(slot):
        @pl.when(keeps)
        def _():
            total = kept_sum(slot)
            gram_own = gram[safe_band]
            grad = adj_own[...] - matmul(matmul(gram_own, total).astype(BF16), gram_own)
            giant_grad[slot, safe_band] = grad.astype(BF16)
            for k in range(1, GROUP):
                grad_copy(slot, k).start()

    def giant_update(slot):
        for b in range(bands):
            @pl.when(rank != keeper(b))
            def _():
                pltpu.make_async_remote_copy(
                    src_ref=giant_grad.at[slot, b],
                    dst_ref=giant_grad.at[slot, b],
                    send_sem=grad_send.at[slot, 0],
                    recv_sem=grad_recv.at[slot, b],
                    device_id={"tiles": base + keeper(b)},
                    device_id_type=MESH,
                ).wait_recv()

        for b in range(bands):
            grad_ref[b] = giant_grad[slot, b].astype(F32)
        update(giant_sed, out_giant, grad_ref, part_ref, energy_ref, None, bands, sources)

    steps = [giant_start]
    for it in range(ITERS):
        steps.append(functools.partial(giant_keep, it))
        if it < ITERS - 1:

            def advance(it=it):
                giant_update(it)
                giant_mix(it + 1)

            steps.append(advance)
        else:
            steps.append(functools.partial(giant_update, it))

    def launch(b):
        for k in range(1, QUAD):
            piece_copy(b, k).start()
        own_copy(b).start()

    at = lax.broadcasted_iota(I32, (8, lanes), 1) - lower * piece_count
    at = jnp.where(lax.broadcasted_iota(I32, (8, lanes), 0) == upper, at, -1)
    line = jnp.zeros((8, lanes), I32)
    for index in range(piece_count):
        line = jnp.where(at == index, home_of_ref[blend_ref[index]], line)
    homes_ref[rank] = line
    for k in range(1, GROUP):
        home_copy(k).start()
    ahead = 2
    launch(0)
    for k in range(1, GROUP):
        strip_copy(k).start()
    send_bands(ITERS, giant_ref)
    for b in range(1, min(ahead, bands)):
        launch(b)

    for b in range(bands):
        psf = psf_ref[b]
        gram[b] = t_matmul(psf, psf).astype(BF16)
        psf_t[b] = jnp.transpose(psf.astype(F32)).astype(BF16)
    for k in range(1, GROUP):
        home_copy(k).wait_recv()
    table_vmem[...] = sort_tables(homes_ref, upper, QUAD * piece_count, lanes)
    to_scalar = pltpu.make_async_copy(table_vmem, table_ref, table_sem)
    to_scalar.start()
    to_scalar.wait()

    def prepare(index, carry):
        row_at = corners_ref[pl.ds(index, 1), 0:1]
        col_at = corners_ref[pl.ds(index, 1), 1:2]
        rows = lax.broadcasted_iota(I32, (TILE, side), 0)
        inner = lax.broadcasted_iota(I32, (TILE, side), 1)
        row_hot = jnp.where(rows == inner + row_at, 1.0, 0.0).astype(BF16)
        cols = lax.broadcasted_iota(I32, (side, TILE), 1)
        inner_c = lax.broadcasted_iota(I32, (side, TILE), 0)
        col_hot = jnp.where(cols == inner_c + col_at, 1.0, 0.0).astype(BF16)
        for b in range(bands):
            row_psf[index, b] = matmul(row_hot, psf_ref[b]).astype(BF16)
            col_psf[b, index] = matmul(psf_t[b], col_hot).astype(BF16)
        return carry

    sed_table[...] = jnp.zeros_like(sed_table)

    early = [giant_open] + steps[: bands - 1]
    steps = steps[bands - 1 :]
    def combine(b):
        pair_copy(b).wait_recv()
        for group in range(quads // 2):
            first = (2 * group + parity) * near_blends

            def join(index, carry, group=group, first=first):
                some = table_ref[3, first + index].astype(F32)
                mine_part = running[b % 2, table_ref[2, first + index]] * some
                summed[b, group, index] = (
                    mine_part + pair_buf[b, group, index].astype(F32)
                ).astype(BF16)
                return carry

            lax.fori_loop(0, near_blends, join, 0, unroll=4)
        for k in range(1, owners):
            incoming(b, k).start()
        arrived[b, pair, lower] = summed[b, pair, pl.ds(lower * owned, owned)]

    for b in range(bands):
        for k in range(1, QUAD):
            piece_copy(b, k).wait_recv()
        own_copy(b).wait()
        band_pieces = piece_bufs[b]

        def add(index, total, band_pieces=band_pieces, b=b):
            keep = table_ref[1, index].astype(F32)
            total = total * keep + band_pieces[table_ref[0, index]].astype(F32)
            running[b % 2, index] = total
            return total

        lax.fori_loop(0, QUAD * piece_count, add, jnp.zeros((quarter, lanes), F32), unroll=8)
        for group in range(quads // 2):
            first = (2 * group + 1 - parity) * near_blends

            def put(index, carry, b=b, group=group, first=first):
                some = table_ref[3, first + index].astype(F32)
                aside[b, group, index] = (
                    running[b % 2, table_ref[2, first + index]] * some
                ).astype(BF16)
                return carry

            lax.fori_loop(0, near_blends, put, 0, unroll=4)
        pair_copy(b).start()
        if b + ahead < bands:
            launch(b + ahead)
        if b > 0:
            combine(b - 1)
        if b == 0:
            lax.fori_loop(0, piece_count, prepare, 0)
        if b < len(early):
            early[b]()
    combine(bands - 1)

    for b in range(bands):
        for k in range(1, owners):
            incoming(b, k).wait_recv()

    def blend(n, carry):
        source_of_row = lax.broadcasted_iota(I32, (table, lanes), 0) // bands
        act_ref[...] = jnp.where(source_of_row < counts_ref[n], 1.0, 0.0)
        spread_rows(sed_ref, spectra_ref[n], bands, sources, lanes)
        sed_ref[...] = sed_ref[...] * act_ref[...]
        for b in range(bands):
            total = arrived[b, 0, :, n].astype(F32)
            for g in range(1, quads // 2):
                total = total + arrived[b, g, :, n].astype(F32)
            grad_ref[b] = total.reshape(side, side)
        mean = grad_ref[0]
        for b in range(1, bands):
            mean = mean + grad_ref[b]
        base_map = jnp.maximum(mean / bands, 0.0)
        for k in range(sources):
            morph_ref[k] = (
                jnp.where(labels_ref[n] == k + 1, base_map, 0.0)
                * act_ref[k * bands : k * bands + 1, :]
            )
        for b in range(bands):
            back = matmul(psf_t[b], grad_ref[b].astype(BF16)).astype(BF16)
            adj_ref[b] = matmul(back, psf_ref[b])

        def iteration(it, carry):
            for b in range(bands):
                mix = mix_band(sed_ref, morph_ref, b, bands, sources)
                grad_ref[b] = adj_ref[b] - matmul(matmul(gram[b], mix).astype(BF16), gram[b])
            update(sed_ref, morph_ref, grad_ref, part_ref, energy_ref, act_ref, bands, sources)
            return carry

        lax.fori_loop(0, ITERS, iteration, 0)
        out_morph[n] = morph_ref[...].astype(BF16).reshape(out_morph.shape[1:])
        for k in range(1, count):
            outgoing(n, k).start()
        held[me * owned + n] = out_morph[n, rank]
        diag = lax.broadcasted_iota(I32, (table, lanes), 0) == lax.broadcasted_iota(
            I32, (table, lanes), 1
        )
        line = jnp.sum(jnp.where(diag, sed_ref[...], 0.0), axis=0, keepdims=True)
        here = lax.broadcasted_iota(I32, sed_table.shape, 0) == n
        sed_table[...] = jnp.where(here, line, sed_table[...])

        for index, step in enumerate(steps):
            if index < owned:
                pl.when(n == index)(step)
        return carry

    lax.fori_loop(0, owned, blend, 0)
    sed_all[me] = sed_table[...].astype(BF16)
    for k in range(1, count):
        sed_copy(k).start()
    out_sed[...] = sed_table[...]
    rest = list(steps[owned:])
    while len(rest) > 1:
        rest.pop(0)()

    def settle(n, carry):
        for k in range(1, count):
            outgoing(n, k).wait_recv()
        return carry

    lax.fori_loop(0, owned, settle, 0)

    for k in range(1, GROUP + 1):
        other = lax.rem(rank + k, GROUP)

        def pick(index, carry, other=other):
            for chunk in range(CHUNKS):
                found = held[
                    table_ref[
                        4 + other // QUAD,
                        lax.rem(other, QUAD) * piece_count + chunk * per_chunk + index,
                    ]
                ]
                if k < GROUP:
                    picked[chunk, other, index] = found
                else:
                    landed[chunk, index, rank] = found
            return carry

        lax.fori_loop(0, per_chunk, pick, 0)
    for chunk in range(CHUNKS):
        for k in range(1, GROUP):
            last_copy(chunk, k).start()

    for step in rest:
        step()
    for k in range(1, count):
        sed_copy(k).wait_recv()
    out_tile[...] = jnp.zeros_like(out_tile)

    def finish(chunk, carry):
        for k in range(1, GROUP):
            last_copy(chunk, k).wait_recv()
        for index in range(per_chunk):
            piece = chunk * per_chunk + index
            home = table_ref[4 + upper, lower * piece_count + piece]
            owner = lax.div(home, owned)
            place = home - owner * owned
            rows = sed_all[owner].astype(F32)
            here = lax.broadcasted_iota(I32, rows.shape, 0) == place
            line = jnp.sum(jnp.where(here, rows, 0.0), axis=0, keepdims=True)
            diag = lax.broadcasted_iota(I32, (table, lanes), 0) == lax.broadcasted_iota(
                I32, (table, lanes), 1
            )
            column = jnp.sum(jnp.where(diag, line, 0.0), axis=1, keepdims=True)
            sed_ref[...] = jnp.broadcast_to(column, (table, lanes))
            morph_ref[...] = landed[chunk, index].astype(F32).reshape(sources, side, side)
            for b in range(bands):
                mix = mix_band(sed_ref, morph_ref, b, bands, sources)
                left_ref[b, :, index * side : (index + 1) * side] = matmul(
                    row_psf[piece, b], mix
                ).astype(BF16)
        for b in range(bands):
            right = col_psf[b, pl.ds(chunk * per_chunk, per_chunk)].reshape(
                per_chunk * side, TILE
            )
            out_tile[b] = out_tile[b] + matmul(left_ref[b], right)
        return carry

    lax.fori_loop(0, CHUNKS, finish, 0)

    def drain(n, carry):
        for k in range(1, count):
            outgoing(n, k).wait_send()
        return carry

    lax.fori_loop(0, owned, drain, 0)
    for b in range(bands):
        for k in range(1, QUAD):
            piece_copy(b, k).wait_send()
        pair_copy(b).wait_send()
        for k in range(1, owners):
            incoming(b, k).wait_send()
    for k in range(1, GROUP):
        home_copy(k).wait_send()
    for k in range(1, count):
        sed_copy(k).wait_send()
    for chunk in range(CHUNKS):
        for k in range(1, GROUP):
            last_copy(chunk, k).wait_send()
    for k in range(1, GROUP):
        strip_copy(k).wait_send()
        base_copy(k).wait_send()
    sent_bands(ITERS, giant_ref)
    for it in range(ITERS):
        sent_bands(it, mix_buf.at[it])

        @pl.when(keeps)
        def _():
            for k in range(1, GROUP):
                grad_copy(it, k).wait_send()


def on_device(
    pieces,
    piece_blend,
    corners,
    blend_home,
    source_count,
    footprint,
    spectra,
    giant_pieces,
    giant_footprint,
    giant_spectra,
    psf_matrix,
):
    count = lax.axis_size("tiles")
    piece_count, bands, side, _ = pieces.shape
    owned = footprint.shape[0]
    blend_count = blend_home.shape[0]
    sources = spectra.shape[1]
    back_rows = sources * side // GROUP
    lanes = side
    table = sources * bands
    strip = side // GROUP
    per_chunk = piece_count // CHUNKS
    quarter = side // QUAD
    pairs = count // QUAD // 2

    dma = pltpu.SemaphoreType.DMA
    whole_map = (GROUP, strip, side)
    final_morph, sed_rows, tile_model, giant_morph = pl.pallas_call(
        functools.partial(core_kernel, count, bands, sources, owned, piece_count),
        out_shape=(
            jax.ShapeDtypeStruct((owned, GROUP, back_rows, lanes), BF16),
            jax.ShapeDtypeStruct((16, lanes), F32),
            jax.ShapeDtypeStruct((bands, TILE, TILE), F32),
            jax.ShapeDtypeStruct((sources, side, side), F32),
        ),
        in_specs=[SMEM, SMEM, SMEM, ANY] + [VMEM] * 7,
        out_specs=(VMEM,) * 4,
        scratch_shapes=[
            pltpu.VMEM((GROUP, 8, lanes), I32),
            pltpu.VMEM((8, lanes), I32),
            pltpu.SMEM((8, lanes), I32),
            pltpu.VMEM((2, QUAD * piece_count, quarter, lanes), F32),
            pltpu.VMEM((bands, pairs, QUAD * owned, quarter, lanes), BF16),
            pltpu.VMEM((bands, pairs, QUAD * owned, quarter, lanes), BF16),
            pltpu.VMEM((bands, pairs, QUAD * owned, quarter, lanes), BF16),
            [pltpu.VMEM((QUAD * piece_count, quarter, lanes), BF16) for _ in range(bands)],
            pltpu.VMEM((bands, pairs, QUAD, owned, quarter, lanes), BF16),
            pltpu.VMEM((sources, side, side), F32),
            pltpu.VMEM((table, lanes), F32),
            pltpu.VMEM((table, lanes), F32),
            pltpu.VMEM((bands, side, side), F32),
            pltpu.VMEM((bands, side, side), F32),
            pltpu.VMEM((table, lanes), F32),
            pltpu.VMEM((table, lanes), F32),
            pltpu.VMEM((bands, side, side), BF16),
            pltpu.VMEM((bands, side, side), BF16),
            pltpu.VMEM((16, lanes), F32),
            pltpu.VMEM((count, 16, lanes), BF16),
            pltpu.VMEM((blend_count, back_rows, lanes), BF16),
            pltpu.VMEM((CHUNKS, GROUP, per_chunk, back_rows, lanes), BF16),
            pltpu.VMEM((CHUNKS, per_chunk, GROUP, back_rows, lanes), BF16),
            pltpu.VMEM((piece_count, bands, TILE, side), BF16),
            pltpu.VMEM((bands, piece_count, side, TILE), BF16),
            pltpu.VMEM((bands, TILE, per_chunk * side), BF16),
            pltpu.VMEM((GROUP, bands, strip, side), BF16),
            pltpu.VMEM((GROUP, strip, side), F32),
            pltpu.VMEM((ITERS + 1, GROUP) + whole_map, BF16),
            pltpu.VMEM((ITERS, bands) + whole_map, BF16),
            pltpu.VMEM((side, side), F32),
            pltpu.VMEM((table, lanes), F32),
            pltpu.VMEM((ITERS, bands, side, side), BF16),
            dma((bands,)),
            dma,
            dma((GROUP - 1,)),
            dma((GROUP - 1,)),
            dma((bands, QUAD - 1)),
            dma((bands, QUAD - 1)),
            dma((bands,)),
            dma((bands,)),
            dma((bands, pairs * QUAD - 1)),
            dma((bands, pairs * QUAD - 1)),
            dma((owned, count - 1)),
            dma((owned, count - 1)),
            dma((count - 1,)),
            dma((count - 1,)),
            dma((CHUNKS, GROUP - 1)),
            dma((CHUNKS, GROUP - 1)),
            dma((GROUP - 1,)),
            dma((GROUP - 1,)),
            dma((GROUP - 1,)),
            dma((GROUP - 1,)),
            dma((ITERS + 1, bands)),
            dma((ITERS + 1, GROUP)),
            dma((ITERS, GROUP - 1)),
            dma((ITERS, bands)),
        ],
        compiler_params=pltpu.CompilerParams(
            collective_id=0, has_side_effects=True, vmem_limit_bytes=56 << 20
        ),
        name="core",
    )(
        piece_blend,
        blend_home,
        source_count,
        pieces.reshape(piece_count, bands, QUAD, quarter, side),
        footprint,
        spectra,
        psf_matrix,
        corners,
        giant_pieces.reshape(bands, GROUP, strip, side),
        giant_footprint,
        giant_spectra,
    )
    final_sed = sed_rows[:owned, :table].reshape(owned, sources, bands).astype(BF16)
    return (
        final_morph.reshape(owned, sources, side, side),
        final_sed,
        tile_model[None],
        giant_morph[None],
    )


def solution(mesh):
    in_specs = (
        P(("groups", "tiles"), None, None, None),
        P(("groups", "tiles")),
        P(("groups", "tiles"), None),
        P("groups"),
        P(("groups", "tiles")),
        P(("groups", "tiles"), None, None),
        P(("groups", "tiles"), None, None),
        P(("groups", "tiles"), None, None, None),
        P(("groups", "tiles"), None, None),
        P(("groups", "tiles"), None, None),
        P(),
    )
    out_specs = (
        P(("groups", "tiles"), None, None, None),
        P(("groups", "tiles"), None, None),
        P(("groups", "tiles"), None, None, None),
        P(("groups", "tiles"), None, None, None),
    )
    return jax.shard_map(
        on_device, mesh=mesh, in_specs=in_specs, out_specs=out_specs, check_vma=False
    )
```

```python
import functools

import jax
import jax.numpy as jnp
from jax import lax
from jax.experimental import pallas as pl
from jax.experimental.pallas import tpu as pltpu
from jax.sharding import PartitionSpec as P

TILE = 256
ITERS = 3
GROUP = 8
QUAD = 4
CHUNKS = 4
MESH = pl.DeviceIdType.MESH
F32 = jnp.float32
BF16 = jnp.bfloat16
I32 = jnp.int32

step_size = 0.1

VMEM = pl.BlockSpec(memory_space=pltpu.VMEM)
SMEM = pl.BlockSpec(memory_space=pltpu.SMEM)
ANY = pl.BlockSpec(memory_space=pl.ANY)


def matmul(a, b):
    return jnp.dot(a, b, preferred_element_type=F32)


def t_matmul(a, b):
    return lax.dot_general(a, b, (((0,), (0,)), ((), ())), preferred_element_type=F32)


def barrier_all(me, count):
    barrier = pltpu.get_barrier_semaphore()
    for k in range(1, count):
        pl.semaphore_signal(
            barrier, inc=1, device_id={"tiles": lax.rem(me + k, count)}, device_id_type=MESH
        )
    pl.semaphore_wait(barrier, count - 1)


def remote(src, dst, send_sem, recv_sem, peer):
    return pltpu.make_async_remote_copy(
        src_ref=src,
        dst_ref=dst,
        send_sem=send_sem,
        recv_sem=recv_sem,
        device_id={"tiles": peer},
        device_id_type=MESH,
    )


def mix_band(sed_ref, maps, b, bands, sources):
    total = sed_ref[b : b + 1, :] * maps[0]
    for k in range(1, sources):
        row = k * bands + b
        total = total + sed_ref[row : row + 1, :] * maps[k]
    return total.astype(BF16)


def update(sed_ref, morph_ref, grad_ref, part_ref, energy_ref, act_ref, bands, sources):
    for k in range(sources):
        morph = morph_ref[k]
        energy = jnp.sum(morph * morph, axis=0, keepdims=True)
        push = None
        for b in range(bands):
            row = k * bands + b
            grad = grad_ref[b]
            part_ref[row : row + 1, :] = jnp.sum(morph * grad, axis=0, keepdims=True)
            energy_ref[row : row + 1, :] = energy
            term = sed_ref[row : row + 1, :] * grad
            push = term if push is None else push + term
        fresh = jnp.maximum(morph + step_size * push, 0.0)
        if act_ref is not None:
            fresh = fresh * act_ref[k * bands : k * bands + 1, :]
        morph_ref[k] = fresh
    inner = jnp.sum(part_ref[...], axis=1, keepdims=True)
    energy = jnp.sum(energy_ref[...], axis=1, keepdims=True)
    sed = jnp.maximum(sed_ref[...] + inner / (energy + 1.0), 0.0)
    if act_ref is not None:
        sed = sed * act_ref[...]
    sed_ref[...] = sed


def spread_rows(sed_ref, table, bands, sources, lanes):
    for k in range(sources):
        line = jnp.broadcast_to(table[k : k + 1, :], (bands, bands))
        row = lax.broadcasted_iota(I32, (bands, bands), 0)
        col = lax.broadcasted_iota(I32, (bands, bands), 1)
        value = jnp.sum(jnp.where(row == col, line, 0.0), axis=1, keepdims=True)
        sed_ref[k * bands : (k + 1) * bands, :] = jnp.broadcast_to(value, (bands, lanes))


def sort_tables(homes_ref, upper, used, lanes):
    line = homes_ref[0]
    for source in range(1, GROUP):
        line = line + homes_ref[source]
    near = jnp.where(upper == 0, line[0:1, :], line[1:2, :])
    near = jnp.where(lax.broadcasted_iota(I32, (1, lanes), 1) < used, near, 2 * lanes)
    across = jnp.broadcast_to(near, (lanes, lanes))
    sub = lax.broadcasted_iota(I32, (lanes, lanes), 0)
    lane = lax.broadcasted_iota(I32, (lanes, lanes), 1)
    down = jnp.sum(jnp.where(sub == lane, across, 0), axis=1, keepdims=True)
    key_across = across * lanes + lane
    key_down = down * lanes + sub
    place = jnp.sum(jnp.where(key_across < key_down, 1, 0), axis=1, keepdims=True)
    order = jnp.sum(jnp.where(place == lane, sub, 0), axis=0, keepdims=True)
    sorted_home = jnp.sum(jnp.where(place == lane, down, 0), axis=0, keepdims=True)
    before = jnp.sum(jnp.where(place + 1 == lane, down, 0), axis=0, keepdims=True)
    keep = jnp.where(sorted_home == before, 1, 0)
    upto = jnp.sum(jnp.where(down <= lane, 1, 0), axis=0, keepdims=True)
    same = jnp.sum(jnp.where(down == lane, 1, 0), axis=0, keepdims=True)
    last = jnp.maximum(upto - 1, 0)
    some = jnp.where(same > 0, 1, 0)
    rows = [order, keep, last, some]
    for half in range(GROUP // QUAD):
        rows.append(line[half : half + 1, :])
    which = lax.broadcasted_iota(I32, (8, lanes), 0)
    result = jnp.zeros((8, lanes), I32)
    for index, row in enumerate(rows):
        result = jnp.where(which == index, row, result)
    return result


def core_kernel(
    count,
    bands,
    sources,
    owned,
    piece_count,
    blend_ref,
    home_of_ref,
    counts_ref,
    pieces_ref,
    labels_ref,
    spectra_ref,
    psf_ref,
    corners_ref,
    giant_ref,
    giant_labels_ref,
    giant_spectra_ref,
    out_morph,
    out_sed,
    out_tile,
    out_giant,
    homes_ref,
    table_vmem,
    table_ref,
    running,
    aside,
    pair_buf,
    summed,
    piece_bufs,
    arrived,
    morph_ref,
    sed_ref,
    act_ref,
    adj_ref,
    grad_ref,
    part_ref,
    energy_ref,
    gram,
    psf_t,
    sed_table,
    sed_all,
    held,
    picked,
    landed,
    row_psf,
    col_psf,
    left_ref,
    strips,
    base_buf,
    band_buf,
    mix_buf,
    adj_own,
    giant_sed,
    giant_grad,
    own_sem,
    table_sem,
    home_send,
    home_recv,
    piece_send,
    piece_recv,
    pair_send,
    pair_recv,
    in_send,
    in_recv,
    back_send,
    back_recv,
    sed_send,
    sed_recv,
    half_send,
    half_recv,
    last_send,
    last_recv,
    strip_send,
    strip_recv,
    base_send,
    base_recv,
    band_send,
    band_recv,
    grad_send,
    grad_recv,
):
    me = lax.axis_index("tiles")
    rank = lax.rem(me, GROUP)
    base = me - rank
    mine = me // GROUP
    side = labels_ref.shape[1]
    lanes = side
    strip = side // GROUP
    quarter = side // QUAD
    quads = count // QUAD
    near_blends = QUAD * owned
    table = bands * sources
    half = (bands + 1) // 2
    per_chunk = piece_count // CHUNKS
    barrier_all(me, count)

    def keeper(b):
        return (b // half) * (GROUP // 2) + b % half

    upper = rank // QUAD
    lower = lax.rem(rank, QUAD)
    own_band = upper * half + lower
    keeps = jnp.logical_and(lower < half, own_band < bands)
    safe_band = jnp.where(keeps, own_band, 0)

    def home_copy(k):
        other = lax.rem(rank + k, GROUP)
        return remote(
            homes_ref.at[rank], homes_ref.at[rank], home_send.at[k - 1], home_recv.at[k - 1],
            base + other,
        )

    quad = me // QUAD
    pair = quad // 2
    parity = lax.rem(quad, 2)

    def piece_slot(b):
        return piece_bufs[b].at[pl.ds(lower * piece_count, piece_count)]

    def piece_copy(b, k):
        other = lax.rem(lower + k, QUAD)
        return remote(
            pieces_ref.at[:, b, other], piece_slot(b), piece_send.at[b, k - 1],
            piece_recv.at[b, k - 1], quad * QUAD + other,
        )

    def own_copy(b):
        return pltpu.make_async_copy(pieces_ref.at[:, b, lower], piece_slot(b), own_sem.at[b])

    def pair_copy(b):
        partner = (quad + 1 - 2 * parity) * QUAD + lower
        return remote(aside.at[b], pair_buf.at[b], pair_send.at[b], pair_recv.at[b], partner)

    def incoming(b, k):
        to_pair = lax.rem(pair + k // QUAD, quads // 2)
        to_lower = lax.rem(lower + k % QUAD, QUAD)
        return remote(
            summed.at[b, to_pair, pl.ds(to_lower * owned, owned)],
            arrived.at[b, pair, lower],
            in_send.at[b, k - 1],
            in_recv.at[b, k - 1],
            (2 * to_pair + parity) * QUAD + to_lower,
        )

    owners = quads // 2 * QUAD

    def outgoing(h, n, k):
        peer = lax.rem(me + k, count)
        return remote(
            out_morph.at[n, lax.rem(peer, GROUP), h],
            held[h].at[me * owned + n],
            back_send.at[h, n, k - 1],
            back_recv.at[h, n, k - 1],
            peer,
        )

    def sed_copy(k):
        return remote(
            sed_all.at[me], sed_all.at[me], sed_send.at[k - 1], sed_recv.at[k - 1],
            lax.rem(me + k, count),
        )

    def half_copy(k):
        other = lax.rem(rank + k, GROUP)
        return remote(
            picked.at[0, other],
            landed.at[:, :, rank, 0],
            half_send.at[k - 1],
            half_recv.at[k - 1],
            base + other,
        )

    def last_copy(chunk, k):
        other = lax.rem(rank + k, GROUP)
        return remote(
            picked.at[1, other, chunk],
            landed.at[chunk, :, rank, 1],
            last_send.at[chunk, k - 1],
            last_recv.at[chunk, k - 1],
            base + other,
        )

    def strip_copy(k):
        other = lax.rem(rank + k, GROUP)
        return remote(
            giant_ref.at[:, other], strips.at[rank], strip_send.at[k - 1], strip_recv.at[k - 1],
            base + other,
        )

    def base_copy(k):
        other = lax.rem(rank + k, GROUP)
        return remote(
            base_buf.at[rank], base_buf.at[rank], base_send.at[k - 1], base_recv.at[k - 1],
            base + other,
        )

    def band_copy(slot, src, b):
        return remote(
            src, band_buf.at[slot, rank], band_send.at[slot, b], band_recv.at[slot, rank],
            base + keeper(b),
        )

    def grad_copy(slot, k):
        other = lax.rem(rank + k, GROUP)
        return remote(
            giant_grad.at[slot, safe_band],
            giant_grad.at[slot, safe_band],
            grad_send.at[slot, k - 1],
            grad_recv.at[slot, safe_band],
            base + other,
        )

    def send_bands(slot, ref):
        for b in range(bands):
            @pl.when(rank != keeper(b))
            def _():
                band_copy(slot, ref.at[b], b).start()

            @pl.when(rank == keeper(b))
            def _():
                band_buf[slot, rank] = ref[b]

    def sent_bands(slot, ref):
        for b in range(bands):
            @pl.when(rank != keeper(b))
            def _():
                band_copy(slot, ref.at[b], b).wait_send()

    def kept_sum(slot):
        for k in range(1, GROUP):
            source = lax.rem(rank + k, GROUP)
            pltpu.make_async_remote_copy(
                src_ref=band_buf.at[slot, source],
                dst_ref=band_buf.at[slot, source],
                send_sem=band_send.at[slot, 0],
                recv_sem=band_recv.at[slot, source],
                device_id={"tiles": base + source},
                device_id_type=MESH,
            ).wait_recv()
        total = band_buf[slot, 0].astype(F32)
        for source in range(1, GROUP):
            total = total + band_buf[slot, source].astype(F32)
        return total.reshape(side, side).astype(BF16)

    def giant_open():
        for k in range(1, GROUP):
            strip_copy(k).wait_recv()
        mean = None
        for k in range(GROUP):
            source = lax.rem(rank + k, GROUP)
            part = giant_ref[:, rank] if k == 0 else strips[source]
            part = jnp.sum(part.astype(F32), axis=0)
            mean = part if mean is None else mean + part
        base_buf[rank] = jnp.maximum(mean / bands, 0.0)
        for k in range(1, GROUP):
            base_copy(k).start()

        @pl.when(keeps)
        def _():
            total = kept_sum(ITERS)
            back = matmul(psf_t[safe_band], total).astype(BF16)
            adj_own[...] = matmul(back, psf_ref[safe_band])

    def giant_mix(slot):
        for b in range(bands):
            mix = mix_band(giant_sed, out_giant, b, bands, sources)
            mix_buf[slot, b] = mix.reshape(GROUP, strip, side)
        send_bands(slot, mix_buf.at[slot])

    def giant_start():
        for k in range(1, GROUP):
            base_copy(k).wait_recv()
        base_map = base_buf[...].reshape(side, side)
        for k in range(sources):
            out_giant[k] = jnp.where(giant_labels_ref[0] == k + 1, base_map, 0.0)
        spread_rows(giant_sed, giant_spectra_ref[0], bands, sources, lanes)
        giant_mix(0)

    def giant_keep(slot):
        @pl.when(keeps)
        def _():
            total = kept_sum(slot)
            gram_own = gram[safe_band]
            grad = adj_own[...] - matmul(matmul(gram_own, total).astype(BF16), gram_own)
            giant_grad[slot, safe_band] = grad.astype(BF16)
            for k in range(1, GROUP):
                grad_copy(slot, k).start()

    def giant_update(slot):
        for b in range(bands):
            @pl.when(rank != keeper(b))
            def _():
                pltpu.make_async_remote_copy(
                    src_ref=giant_grad.at[slot, b],
                    dst_ref=giant_grad.at[slot, b],
                    send_sem=grad_send.at[slot, 0],
                    recv_sem=grad_recv.at[slot, b],
                    device_id={"tiles": base + keeper(b)},
                    device_id_type=MESH,
                ).wait_recv()

        for b in range(bands):
            grad_ref[b] = giant_grad[slot, b].astype(F32)
        update(giant_sed, out_giant, grad_ref, part_ref, energy_ref, None, bands, sources)

    steps = [giant_start]
    for it in range(ITERS):
        steps.append(functools.partial(giant_keep, it))
        if it < ITERS - 1:

            def advance(it=it):
                giant_update(it)
                giant_mix(it + 1)

            steps.append(advance)
        else:
            steps.append(functools.partial(giant_update, it))

    def launch(b):
        for k in range(1, QUAD):
            piece_copy(b, k).start()
        own_copy(b).start()

    at = lax.broadcasted_iota(I32, (8, lanes), 1) - lower * piece_count
    at = jnp.where(lax.broadcasted_iota(I32, (8, lanes), 0) == upper, at, -1)
    line = jnp.zeros((8, lanes), I32)
    for index in range(piece_count):
        line = jnp.where(at == index, home_of_ref[blend_ref[index]], line)
    homes_ref[rank] = line
    for k in range(1, GROUP):
        home_copy(k).start()
    ahead = 2
    launch(0)
    for k in range(1, GROUP):
        strip_copy(k).start()
    send_bands(ITERS, giant_ref)
    for b in range(1, min(ahead, bands)):
        launch(b)

    for b in range(bands):
        psf = psf_ref[b]
        gram[b] = t_matmul(psf, psf).astype(BF16)
        psf_t[b] = jnp.transpose(psf.astype(F32)).astype(BF16)
    for k in range(1, GROUP):
        home_copy(k).wait_recv()
    table_vmem[...] = sort_tables(homes_ref, upper, QUAD * piece_count, lanes)
    to_scalar = pltpu.make_async_copy(table_vmem, table_ref, table_sem)
    to_scalar.start()
    to_scalar.wait()

    def prepare(index, carry):
        spot = lax.broadcasted_iota(I32, corners_ref.shape, 1) == index
        spot = jnp.sum(jnp.where(spot, corners_ref[...], 0), axis=1, keepdims=True)
        row_at, col_at = spot[0:1, :], spot[1:2, :]
        rows = lax.broadcasted_iota(I32, (TILE, side), 0)
        inner = lax.broadcasted_iota(I32, (TILE, side), 1)
        row_hot = jnp.where(rows == inner + row_at, 1.0, 0.0).astype(BF16)
        cols = lax.broadcasted_iota(I32, (side, TILE), 1)
        inner_c = lax.broadcasted_iota(I32, (side, TILE), 0)
        col_hot = jnp.where(cols == inner_c + col_at, 1.0, 0.0).astype(BF16)
        for b in range(bands):
            row_psf[index, b] = matmul(row_hot, psf_ref[b]).astype(BF16)
            col_psf[b, index] = matmul(psf_t[b], col_hot).astype(BF16)
        return carry

    sed_table[...] = jnp.zeros_like(sed_table)

    early = [giant_open] + steps[: bands - 1]
    steps = steps[bands - 1 :]
    def combine(b):
        pair_copy(b).wait_recv()
        for group in range(quads // 2):
            first = (2 * group + parity) * near_blends

            def join(index, carry, group=group, first=first):
                some = table_ref[3, first + index].astype(F32)
                mine_part = running[b % 2, table_ref[2, first + index]] * some
                summed[b, group, index] = (
                    mine_part + pair_buf[b, group, index].astype(F32)
                ).astype(BF16)
                return carry

            lax.fori_loop(0, near_blends, join, 0, unroll=4)
        for k in range(1, owners):
            incoming(b, k).start()
        arrived[b, pair, lower] = summed[b, pair, pl.ds(lower * owned, owned)]

    for b in range(bands):
        for k in range(1, QUAD):
            piece_copy(b, k).wait_recv()
        own_copy(b).wait()
        band_pieces = piece_bufs[b]

        def add(index, total, band_pieces=band_pieces, b=b):
            keep = table_ref[1, index].astype(F32)
            total = total * keep + band_pieces[table_ref[0, index]].astype(F32)
            running[b % 2, index] = total
            return total

        lax.fori_loop(0, QUAD * piece_count, add, jnp.zeros((quarter, lanes), F32), unroll=8)
        for group in range(quads // 2):
            first = (2 * group + 1 - parity) * near_blends

            def put(index, carry, b=b, group=group, first=first):
                some = table_ref[3, first + index].astype(F32)
                aside[b, group, index] = (
                    running[b % 2, table_ref[2, first + index]] * some
                ).astype(BF16)
                return carry

            lax.fori_loop(0, near_blends, put, 0, unroll=4)
        pair_copy(b).start()
        if b + ahead < bands:
            launch(b + ahead)
        if b > 0:
            combine(b - 1)
        if b < len(early):
            early[b]()
    combine(bands - 1)

    for b in range(bands):
        for k in range(1, owners):
            incoming(b, k).wait_recv()

    def blend(n, carry):
        source_of_row = lax.broadcasted_iota(I32, (table, lanes), 0) // bands
        act_ref[...] = jnp.where(source_of_row < counts_ref[n], 1.0, 0.0)
        spread_rows(sed_ref, spectra_ref[n], bands, sources, lanes)
        sed_ref[...] = sed_ref[...] * act_ref[...]
        for b in range(bands):
            total = arrived[b, 0, :, n].astype(F32)
            for g in range(1, quads // 2):
                total = total + arrived[b, g, :, n].astype(F32)
            grad_ref[b] = total.reshape(side, side)
        mean = grad_ref[0]
        for b in range(1, bands):
            mean = mean + grad_ref[b]
        base_map = jnp.maximum(mean / bands, 0.0)
        for k in range(sources):
            morph_ref[k] = (
                jnp.where(labels_ref[n] == k + 1, base_map, 0.0)
                * act_ref[k * bands : k * bands + 1, :]
            )
        for b in range(bands):
            back = matmul(psf_t[b], grad_ref[b].astype(BF16)).astype(BF16)
            adj_ref[b] = matmul(back, psf_ref[b])

        def iteration(it, carry):
            for b in range(bands):
                mix = mix_band(sed_ref, morph_ref, b, bands, sources)
                grad_ref[b] = adj_ref[b] - matmul(matmul(gram[b], mix).astype(BF16), gram[b])
            update(sed_ref, morph_ref, grad_ref, part_ref, energy_ref, act_ref, bands, sources)
            return carry

        lax.fori_loop(0, ITERS, iteration, 0)
        out_morph[n] = morph_ref[...].astype(BF16).reshape(out_morph.shape[1:])
        for k in range(1, count):
            outgoing(0, n, k).start()
        for h in range(2):
            held[h][me * owned + n] = out_morph[n, rank, h]
        diag = lax.broadcasted_iota(I32, (table, lanes), 0) == lax.broadcasted_iota(
            I32, (table, lanes), 1
        )
        line = jnp.sum(jnp.where(diag, sed_ref[...], 0.0), axis=0, keepdims=True)
        here = lax.broadcasted_iota(I32, sed_table.shape, 0) == n
        sed_table[...] = jnp.where(here, line, sed_table[...])

        for index, step in enumerate(steps):
            if index < owned:
                pl.when(n == index)(step)
        return carry

    lax.fori_loop(0, owned, blend, 0)

    def second(n, carry):
        for k in range(1, count):
            outgoing(1, n, k).start()
        return carry

    lax.fori_loop(0, owned, second, 0)
    sed_all[me] = sed_table[...].astype(BF16)
    for k in range(1, count):
        sed_copy(k).start()
    out_sed[...] = sed_table[...]
    lax.fori_loop(0, piece_count, prepare, 0)
    rest = list(steps[owned:])

    def settle(h):
        def one(n, carry):
            for k in range(1, count):
                outgoing(h, n, k).wait_recv()
            return carry

        lax.fori_loop(0, owned, one, 0)

    def pick(h, k, chunks):
        other = lax.rem(rank + k, GROUP)

        def one(index, carry):
            for chunk in chunks:
                found = held[h][
                    table_ref[
                        4 + other // QUAD,
                        lax.rem(other, QUAD) * piece_count + chunk * per_chunk + index,
                    ]
                ]
                if k < GROUP:
                    picked[h, other, chunk, index] = found
                else:
                    landed[chunk, index, rank, h] = found
            return carry

        lax.fori_loop(0, per_chunk, one, 0)

    settle(0)
    for k in range(1, GROUP + 1):
        pick(0, k, range(CHUNKS))
        if k < GROUP:
            half_copy(k).start()
    while len(rest) > 1:
        rest.pop(0)()
    settle(1)
    for chunk in range(CHUNKS):
        for k in range(1, GROUP + 1):
            pick(1, k, [chunk])
            if k < GROUP:
                last_copy(chunk, k).start()

    for step in rest:
        step()
    for k in range(1, count):
        sed_copy(k).wait_recv()
    out_tile[...] = jnp.zeros_like(out_tile)

    for k in range(1, GROUP):
        half_copy(k).wait_recv()

    def finish(chunk, carry):
        for k in range(1, GROUP):
            last_copy(chunk, k).wait_recv()
        for index in range(per_chunk):
            piece = chunk * per_chunk + index
            home = table_ref[4 + upper, lower * piece_count + piece]
            owner = lax.div(home, owned)
            place = home - owner * owned
            rows = sed_all[owner].astype(F32)
            here = lax.broadcasted_iota(I32, rows.shape, 0) == place
            line = jnp.sum(jnp.where(here, rows, 0.0), axis=0, keepdims=True)
            diag = lax.broadcasted_iota(I32, (table, lanes), 0) == lax.broadcasted_iota(
                I32, (table, lanes), 1
            )
            column = jnp.sum(jnp.where(diag, line, 0.0), axis=1, keepdims=True)
            sed_ref[...] = jnp.broadcast_to(column, (table, lanes))
            morph_ref[...] = landed[chunk, index].astype(F32).reshape(sources, side, side)
            for b in range(bands):
                mix = mix_band(sed_ref, morph_ref, b, bands, sources)
                left_ref[b, :, index * side : (index + 1) * side] = matmul(
                    row_psf[piece, b], mix
                ).astype(BF16)
        for b in range(bands):
            right = col_psf[b, pl.ds(chunk * per_chunk, per_chunk)].reshape(
                per_chunk * side, TILE
            )
            out_tile[b] = out_tile[b] + matmul(left_ref[b], right)
        return carry

    lax.fori_loop(0, CHUNKS, finish, 0)

    def drain(n, carry):
        for h in range(2):
            for k in range(1, count):
                outgoing(h, n, k).wait_send()
        return carry

    lax.fori_loop(0, owned, drain, 0)
    for b in range(bands):
        for k in range(1, QUAD):
            piece_copy(b, k).wait_send()
        pair_copy(b).wait_send()
        for k in range(1, owners):
            incoming(b, k).wait_send()
    for k in range(1, GROUP):
        home_copy(k).wait_send()
    for k in range(1, count):
        sed_copy(k).wait_send()
    for k in range(1, GROUP):
        half_copy(k).wait_send()
        for chunk in range(CHUNKS):
            last_copy(chunk, k).wait_send()
    for k in range(1, GROUP):
        strip_copy(k).wait_send()
        base_copy(k).wait_send()
    sent_bands(ITERS, giant_ref)
    for it in range(ITERS):
        sent_bands(it, mix_buf.at[it])

        @pl.when(keeps)
        def _():
            for k in range(1, GROUP):
                grad_copy(it, k).wait_send()


def on_device(
    pieces,
    piece_blend,
    corners,
    blend_home,
    source_count,
    footprint,
    spectra,
    giant_pieces,
    giant_footprint,
    giant_spectra,
    psf_matrix,
):
    count = lax.axis_size("tiles")
    piece_count, bands, side, _ = pieces.shape
    owned = footprint.shape[0]
    blend_count = blend_home.shape[0]
    sources = spectra.shape[1]
    back_rows = sources * side // GROUP // 2
    lanes = side
    table = sources * bands
    strip = side // GROUP
    per_chunk = piece_count // CHUNKS
    quarter = side // QUAD
    pairs = count // QUAD // 2

    dma = pltpu.SemaphoreType.DMA
    whole_map = (GROUP, strip, side)
    final_morph, sed_rows, tile_model, giant_morph = pl.pallas_call(
        functools.partial(core_kernel, count, bands, sources, owned, piece_count),
        out_shape=(
            jax.ShapeDtypeStruct((owned, GROUP, 2, back_rows, lanes), BF16),
            jax.ShapeDtypeStruct((16, lanes), F32),
            jax.ShapeDtypeStruct((bands, TILE, TILE), F32),
            jax.ShapeDtypeStruct((sources, side, side), F32),
        ),
        in_specs=[SMEM, SMEM, SMEM, ANY] + [VMEM] * 7,
        out_specs=(VMEM,) * 4,
        scratch_shapes=[
            pltpu.VMEM((GROUP, 8, lanes), I32),
            pltpu.VMEM((8, lanes), I32),
            pltpu.SMEM((8, lanes), I32),
            pltpu.VMEM((2, QUAD * piece_count, quarter, lanes), F32),
            pltpu.VMEM((bands, pairs, QUAD * owned, quarter, lanes), BF16),
            pltpu.VMEM((bands, pairs, QUAD * owned, quarter, lanes), BF16),
            pltpu.VMEM((bands, pairs, QUAD * owned, quarter, lanes), BF16),
            [pltpu.VMEM((QUAD * piece_count, quarter, lanes), BF16) for _ in range(bands)],
            pltpu.VMEM((bands, pairs, QUAD, owned, quarter, lanes), BF16),
            pltpu.VMEM((sources, side, side), F32),
            pltpu.VMEM((table, lanes), F32),
            pltpu.VMEM((table, lanes), F32),
            pltpu.VMEM((bands, side, side), F32),
            pltpu.VMEM((bands, side, side), F32),
            pltpu.VMEM((table, lanes), F32),
            pltpu.VMEM((table, lanes), F32),
            pltpu.VMEM((bands, side, side), BF16),
            pltpu.VMEM((bands, side, side), BF16),
            pltpu.VMEM((16, lanes), F32),
            pltpu.VMEM((count, 16, lanes), BF16),
            [pltpu.VMEM((blend_count, back_rows, lanes), BF16) for _ in range(2)],
            pltpu.VMEM((2, GROUP, CHUNKS, per_chunk, back_rows, lanes), BF16),
            pltpu.VMEM((CHUNKS, per_chunk, GROUP, 2, back_rows, lanes), BF16),
            pltpu.VMEM((piece_count, bands, TILE, side), BF16),
            pltpu.VMEM((bands, piece_count, side, TILE), BF16),
            pltpu.VMEM((bands, TILE, per_chunk * side), BF16),
            pltpu.VMEM((GROUP, bands, strip, side), BF16),
            pltpu.VMEM((GROUP, strip, side), F32),
            pltpu.VMEM((ITERS + 1, GROUP) + whole_map, BF16),
            pltpu.VMEM((ITERS, bands) + whole_map, BF16),
            pltpu.VMEM((side, side), F32),
            pltpu.VMEM((table, lanes), F32),
            pltpu.VMEM((ITERS, bands, side, side), BF16),
            dma((bands,)),
            dma,
            dma((GROUP - 1,)),
            dma((GROUP - 1,)),
            dma((bands, QUAD - 1)),
            dma((bands, QUAD - 1)),
            dma((bands,)),
            dma((bands,)),
            dma((bands, pairs * QUAD - 1)),
            dma((bands, pairs * QUAD - 1)),
            dma((2, owned, count - 1)),
            dma((2, owned, count - 1)),
            dma((count - 1,)),
            dma((count - 1,)),
            dma((GROUP - 1,)),
            dma((GROUP - 1,)),
            dma((CHUNKS, GROUP - 1)),
            dma((CHUNKS, GROUP - 1)),
            dma((GROUP - 1,)),
            dma((GROUP - 1,)),
            dma((GROUP - 1,)),
            dma((GROUP - 1,)),
            dma((ITERS + 1, bands)),
            dma((ITERS + 1, GROUP)),
            dma((ITERS, GROUP - 1)),
            dma((ITERS, bands)),
        ],
        compiler_params=pltpu.CompilerParams(
            collective_id=0, has_side_effects=True, vmem_limit_bytes=56 << 20
        ),
        name="core",
    )(
        piece_blend,
        blend_home,
        source_count,
        pieces.reshape(piece_count, bands, QUAD, quarter, side),
        footprint,
        spectra,
        psf_matrix,
        corners.T,
        giant_pieces.reshape(bands, GROUP, strip, side),
        giant_footprint,
        giant_spectra,
    )
    final_sed = sed_rows[:owned, :table].reshape(owned, sources, bands).astype(BF16)
    return (
        final_morph.reshape(owned, sources, side, side),
        final_sed,
        tile_model[None],
        giant_morph[None],
    )


def solution(mesh):
    in_specs = (
        P(("groups", "tiles"), None, None, None),
        P(("groups", "tiles")),
        P(("groups", "tiles"), None),
        P("groups"),
        P(("groups", "tiles")),
        P(("groups", "tiles"), None, None),
        P(("groups", "tiles"), None, None),
        P(("groups", "tiles"), None, None, None),
        P(("groups", "tiles"), None, None),
        P(("groups", "tiles"), None, None),
        P(),
    )
    out_specs = (
        P(("groups", "tiles"), None, None, None),
        P(("groups", "tiles"), None, None),
        P(("groups", "tiles"), None, None, None),
        P(("groups", "tiles"), None, None, None),
    )
    return jax.shard_map(
        on_device, mesh=mesh, in_specs=in_specs, out_specs=out_specs, check_vma=False
    )
```

```python
import functools

import jax
import jax.numpy as jnp
from jax import lax
from jax.experimental import pallas as pl
from jax.experimental.pallas import tpu as pltpu
from jax.sharding import PartitionSpec as P

TILE = 256
ITERS = 3
GROUP = 8
QUAD = 4
CHIPS = GROUP // 2
KEEP_CHIP = ((0, 3, 1, 2), (3, 0, 2, 1))
CHUNKS = 4
MESH = pl.DeviceIdType.MESH
F32 = jnp.float32
BF16 = jnp.bfloat16
I32 = jnp.int32

step_size = 0.1

VMEM = pl.BlockSpec(memory_space=pltpu.VMEM)
SMEM = pl.BlockSpec(memory_space=pltpu.SMEM)
ANY = pl.BlockSpec(memory_space=pl.ANY)


def matmul(a, b):
    return jnp.dot(a, b, preferred_element_type=F32)


def t_matmul(a, b):
    return lax.dot_general(a, b, (((0,), (0,)), ((), ())), preferred_element_type=F32)


def barrier_all(me, count):
    barrier = pltpu.get_barrier_semaphore()
    for k in range(1, count):
        pl.semaphore_signal(
            barrier, inc=1, device_id={"tiles": lax.rem(me + k, count)}, device_id_type=MESH
        )
    pl.semaphore_wait(barrier, count - 1)


def remote(src, dst, send_sem, recv_sem, peer):
    return pltpu.make_async_remote_copy(
        src_ref=src,
        dst_ref=dst,
        send_sem=send_sem,
        recv_sem=recv_sem,
        device_id={"tiles": peer},
        device_id_type=MESH,
    )


def mix_band(sed_ref, maps, b, bands, sources):
    total = sed_ref[b : b + 1, :] * maps[0]
    for k in range(1, sources):
        row = k * bands + b
        total = total + sed_ref[row : row + 1, :] * maps[k]
    return total.astype(BF16)


def update(sed_ref, morph_ref, grad_ref, part_ref, energy_ref, act_ref, bands, sources):
    for k in range(sources):
        morph = morph_ref[k]
        energy = jnp.sum(morph * morph, axis=0, keepdims=True)
        push = None
        for b in range(bands):
            row = k * bands + b
            grad = grad_ref[b]
            part_ref[row : row + 1, :] = jnp.sum(morph * grad, axis=0, keepdims=True)
            energy_ref[row : row + 1, :] = energy
            term = sed_ref[row : row + 1, :] * grad
            push = term if push is None else push + term
        fresh = jnp.maximum(morph + step_size * push, 0.0)
        if act_ref is not None:
            fresh = fresh * act_ref[k * bands : k * bands + 1, :]
        morph_ref[k] = fresh
    inner = jnp.sum(part_ref[...], axis=1, keepdims=True)
    energy = jnp.sum(energy_ref[...], axis=1, keepdims=True)
    sed = jnp.maximum(sed_ref[...] + inner / (energy + 1.0), 0.0)
    if act_ref is not None:
        sed = sed * act_ref[...]
    sed_ref[...] = sed


def spread_rows(sed_ref, table, bands, sources, lanes):
    for k in range(sources):
        line = jnp.broadcast_to(table[k : k + 1, :], (bands, bands))
        row = lax.broadcasted_iota(I32, (bands, bands), 0)
        col = lax.broadcasted_iota(I32, (bands, bands), 1)
        value = jnp.sum(jnp.where(row == col, line, 0.0), axis=1, keepdims=True)
        sed_ref[k * bands : (k + 1) * bands, :] = jnp.broadcast_to(value, (bands, lanes))


def sort_tables(homes_ref, upper, used, lanes):
    line = homes_ref[0]
    for source in range(1, GROUP):
        line = line + homes_ref[source]
    near = jnp.where(upper == 0, line[0:1, :], line[1:2, :])
    near = jnp.where(lax.broadcasted_iota(I32, (1, lanes), 1) < used, near, 2 * lanes)
    across = jnp.broadcast_to(near, (lanes, lanes))
    sub = lax.broadcasted_iota(I32, (lanes, lanes), 0)
    lane = lax.broadcasted_iota(I32, (lanes, lanes), 1)
    down = jnp.sum(jnp.where(sub == lane, across, 0), axis=1, keepdims=True)
    key_across = across * lanes + lane
    key_down = down * lanes + sub
    place = jnp.sum(jnp.where(key_across < key_down, 1, 0), axis=1, keepdims=True)
    order = jnp.sum(jnp.where(place == lane, sub, 0), axis=0, keepdims=True)
    sorted_home = jnp.sum(jnp.where(place == lane, down, 0), axis=0, keepdims=True)
    before = jnp.sum(jnp.where(place + 1 == lane, down, 0), axis=0, keepdims=True)
    keep = jnp.where(sorted_home == before, 1, 0)
    upto = jnp.sum(jnp.where(down <= lane, 1, 0), axis=0, keepdims=True)
    same = jnp.sum(jnp.where(down == lane, 1, 0), axis=0, keepdims=True)
    last = jnp.maximum(upto - 1, 0)
    some = jnp.where(same > 0, 1, 0)
    rows = [order, keep, last, some]
    for half in range(GROUP // QUAD):
        rows.append(line[half : half + 1, :])
    which = lax.broadcasted_iota(I32, (8, lanes), 0)
    result = jnp.zeros((8, lanes), I32)
    for index, row in enumerate(rows):
        result = jnp.where(which == index, row, result)
    return result


def core_kernel(
    count,
    bands,
    sources,
    owned,
    piece_count,
    blend_ref,
    home_of_ref,
    counts_ref,
    pieces_ref,
    labels_ref,
    spectra_ref,
    psf_ref,
    corners_ref,
    giant_ref,
    giant_labels_ref,
    giant_spectra_ref,
    out_morph,
    out_sed,
    out_tile,
    out_giant,
    homes_ref,
    table_vmem,
    table_ref,
    running,
    aside,
    pair_buf,
    summed,
    piece_bufs,
    arrived,
    morph_ref,
    sed_ref,
    act_ref,
    adj_ref,
    grad_ref,
    part_ref,
    energy_ref,
    gram,
    psf_t,
    sed_table,
    sed_all,
    held,
    picked,
    landed,
    row_psf,
    col_psf,
    left_ref,
    band_total,
    strips,
    base_buf,
    chip_buf,
    chip_out,
    band_buf,
    mix_buf,
    adj_own,
    giant_sed,
    giant_grad,
    own_sem,
    table_sem,
    home_send,
    home_recv,
    piece_send,
    piece_recv,
    pair_send,
    pair_recv,
    in_send,
    in_recv,
    back_send,
    back_recv,
    sed_send,
    sed_recv,
    half_send,
    half_recv,
    last_send,
    last_recv,
    strip_send,
    strip_recv,
    base_send,
    base_recv,
    chip_send,
    chip_recv,
    band_send,
    band_recv,
    grad_send,
    grad_recv,
    relay_send,
    relay_recv,
):
    me = lax.axis_index("tiles")
    rank = lax.rem(me, GROUP)
    base = me - rank
    mine = me // GROUP
    side = labels_ref.shape[1]
    lanes = side
    strip = side // GROUP
    quarter = side // QUAD
    quads = count // QUAD
    near_blends = QUAD * owned
    table = bands * sources
    per_chunk = piece_count // CHUNKS
    barrier_all(me, count)

    upper = rank // QUAD
    lower = lax.rem(rank, QUAD)
    core = lax.rem(rank, 2)
    chip = rank // 2
    partner_core = base + rank + 1 - 2 * core
    half_bands = bands // 2

    def keeper(i):
        return jnp.where(core == 0, KEEP_CHIP[0][i], KEEP_CHIP[1][i])

    keeps = chip < 0
    own_index = 0
    for i in range(half_bands):
        keeps = jnp.logical_or(keeps, keeper(i) == chip)
        own_index = jnp.where(keeper(i) == chip, i, own_index)
    own_band = 2 * own_index + core

    def home_copy(k):
        other = lax.rem(rank + k, GROUP)
        return remote(
            homes_ref.at[rank], homes_ref.at[rank], home_send.at[k - 1], home_recv.at[k - 1],
            base + other,
        )

    quad = me // QUAD
    pair = quad // 2
    parity = lax.rem(quad, 2)

    def piece_slot(b):
        return piece_bufs[b].at[pl.ds(lower * piece_count, piece_count)]

    def piece_copy(b, k):
        other = lax.rem(lower + k, QUAD)
        return remote(
            pieces_ref.at[:, b, other], piece_slot(b), piece_send.at[b, k - 1],
            piece_recv.at[b, k - 1], quad * QUAD + other,
        )

    def own_copy(b):
        return pltpu.make_async_copy(pieces_ref.at[:, b, lower], piece_slot(b), own_sem.at[b])

    def pair_copy(b):
        partner = (quad + 1 - 2 * parity) * QUAD + lower
        return remote(aside.at[b], pair_buf.at[b], pair_send.at[b], pair_recv.at[b], partner)

    def incoming(b, k):
        to_pair = lax.rem(pair + k // QUAD, quads // 2)
        to_lower = lax.rem(lower + k % QUAD, QUAD)
        return remote(
            summed.at[b, to_pair, pl.ds(to_lower * owned, owned)],
            arrived.at[b, pair, lower],
            in_send.at[b, k - 1],
            in_recv.at[b, k - 1],
            (2 * to_pair + parity) * QUAD + to_lower,
        )

    owners = quads // 2 * QUAD

    def outgoing(h, n, k):
        peer = lax.rem(me + k, count)
        return remote(
            out_morph.at[n, lax.rem(peer, GROUP), h],
            held[h].at[me * owned + n],
            back_send.at[h, n, k - 1],
            back_recv.at[h, n, k - 1],
            peer,
        )

    def sed_copy(k):
        return remote(
            sed_all.at[me], sed_all.at[me], sed_send.at[k - 1], sed_recv.at[k - 1],
            lax.rem(me + k, count),
        )

    def half_copy(k):
        other = lax.rem(rank + k, GROUP)
        return remote(
            picked.at[0, other],
            landed.at[:, :, rank, 0],
            half_send.at[k - 1],
            half_recv.at[k - 1],
            base + other,
        )

    def last_copy(chunk, k):
        other = lax.rem(rank + k, GROUP)
        return remote(
            picked.at[1, other, chunk],
            landed.at[chunk, :, rank, 1],
            last_send.at[chunk, k - 1],
            last_recv.at[chunk, k - 1],
            base + other,
        )

    def strip_copy(k):
        other = lax.rem(rank + k, GROUP)
        return remote(
            band_total.at[other], strips.at[rank], strip_send.at[k - 1], strip_recv.at[k - 1],
            base + other,
        )

    def base_copy(k):
        other = lax.rem(rank + k, GROUP)
        return remote(
            base_buf.at[rank], base_buf.at[rank], base_send.at[k - 1], base_recv.at[k - 1],
            base + other,
        )

    def chip_copy(slot, src):
        return remote(
            src.at[:, 1 - core], chip_buf.at[slot], chip_send.at[slot], chip_recv.at[slot],
            partner_core,
        )

    def band_copy(slot, i):
        return remote(
            chip_out.at[slot, i], band_buf.at[slot, chip], band_send.at[slot, i],
            band_recv.at[slot, chip], base + 2 * keeper(i) + core,
        )

    def grad_copy(slot, k):
        other = lax.rem(chip + k, CHIPS)
        return remote(
            giant_grad.at[slot, core, own_index],
            giant_grad.at[slot, core, own_index],
            grad_send.at[slot, k - 1],
            grad_recv.at[slot, own_index],
            base + 2 * other + core,
        )

    def relay_copy(slot):
        return remote(
            giant_grad.at[slot, core], giant_grad.at[slot, core], relay_send.at[slot],
            relay_recv.at[slot], partner_core,
        )

    def chip_sum(slot, ref):
        chip_copy(slot, ref).wait_recv()
        for i in range(half_bands):
            value = ref[i, core].astype(F32) + chip_buf[slot, i].astype(F32)
            chip_out[slot, i] = value.astype(BF16)

            @pl.when(keeper(i) != chip)
            def _():
                band_copy(slot, i).start()

            @pl.when(keeper(i) == chip)
            def _():
                band_buf[slot, chip] = chip_out[slot, i]

    def sent_bands(slot, ref):
        chip_copy(slot, ref).wait_send()
        for i in range(half_bands):
            @pl.when(keeper(i) != chip)
            def _():
                band_copy(slot, i).wait_send()

    def kept_sum(slot):
        for k in range(1, CHIPS):
            source = lax.rem(chip + k, CHIPS)
            remote(
                band_buf.at[slot, source], band_buf.at[slot, source], band_send.at[slot, 0],
                band_recv.at[slot, source], base + 2 * source + core,
            ).wait_recv()
        total = band_buf[slot, 0].astype(F32)
        for source in range(1, CHIPS):
            total = total + band_buf[slot, source].astype(F32)
        return total.reshape(side, side).astype(BF16)

    def giant_open():
        for k in range(1, GROUP):
            strip_copy(k).wait_recv()
        mean = None
        for k in range(GROUP):
            source = lax.rem(rank + k, GROUP)
            part = band_total[rank] if k == 0 else strips[source]
            mean = part if mean is None else mean + part
        base_buf[rank] = jnp.maximum(mean / bands, 0.0)
        for k in range(1, GROUP):
            base_copy(k).start()

        chip_sum(ITERS, giant_ref)

    def giant_mix(slot):
        for b in range(bands):
            mix = mix_band(giant_sed, out_giant, b, bands, sources)
            mix_buf[slot, b // 2, b % 2] = mix.reshape(GROUP, strip, side)
        chip_copy(slot, mix_buf.at[slot]).start()

    def giant_chip(slot):
        chip_sum(slot, mix_buf.at[slot])

    def giant_start():
        for k in range(1, GROUP):
            base_copy(k).wait_recv()
        base_map = base_buf[...].reshape(side, side)
        for k in range(sources):
            out_giant[k] = jnp.where(giant_labels_ref[0] == k + 1, base_map, 0.0)
        spread_rows(giant_sed, giant_spectra_ref[0], bands, sources, lanes)
        giant_mix(0)

    def giant_keep(slot):
        @pl.when(keeps)
        def _():
            if slot == 0:
                total = kept_sum(ITERS)
                back = matmul(psf_t[own_band], total).astype(BF16)
                adj_own[...] = matmul(back, psf_ref[own_band])
            total = kept_sum(slot)
            gram_own = gram[own_band]
            grad = adj_own[...] - matmul(matmul(gram_own, total).astype(BF16), gram_own)
            giant_grad[slot, core, own_index] = grad.astype(BF16)
            for k in range(1, CHIPS):
                grad_copy(slot, k).start()

    def giant_relay(slot):
        for i in range(half_bands):
            @pl.when(keeper(i) != chip)
            def _():
                remote(
                    giant_grad.at[slot, core, i], giant_grad.at[slot, core, i],
                    grad_send.at[slot, 0], grad_recv.at[slot, i], base + 2 * keeper(i) + core,
                ).wait_recv()

        relay_copy(slot).start()

    def giant_update(slot):
        relay_copy(slot).wait_recv()
        for b in range(bands):
            grad_ref[b] = giant_grad[slot, b % 2, b // 2].astype(F32)
        update(giant_sed, out_giant, grad_ref, part_ref, energy_ref, None, bands, sources)
        if slot + 1 < ITERS:
            giant_mix(slot + 1)

    flow = [(0, 1, giant_open), (1, 0, giant_start), (1, 1, functools.partial(giant_chip, 0))]
    turn = 2
    for it in range(ITERS):
        flow.append((turn, 0, functools.partial(giant_keep, it)))
        flow.append((turn + 1, 0, functools.partial(giant_relay, it)))
        flow.append((turn + 1, 1, functools.partial(giant_update, it)))
        if it + 1 < ITERS:
            flow.append((turn + 2, 0, functools.partial(giant_chip, it + 1)))
        turn += 3

    def giant_turn(b, part):
        while flow and flow[0][:2] <= (b, part):
            flow.pop(0)[2]()

    def launch(b):
        for k in range(1, QUAD):
            piece_copy(b, k).start()
        own_copy(b).start()

    at = lax.broadcasted_iota(I32, (8, lanes), 1) - lower * piece_count
    at = jnp.where(lax.broadcasted_iota(I32, (8, lanes), 0) == upper, at, -1)
    line = jnp.zeros((8, lanes), I32)
    for index in range(piece_count):
        line = jnp.where(at == index, home_of_ref[blend_ref[index]], line)
    homes_ref[rank] = line
    for k in range(1, GROUP):
        home_copy(k).start()
    ahead = 2
    launch(0)
    chip_copy(ITERS, giant_ref).start()
    totals = giant_ref[0, 0].astype(F32)
    for b in range(1, bands):
        totals = totals + giant_ref[b // 2, b % 2].astype(F32)
    band_total[...] = totals
    for k in range(1, GROUP):
        strip_copy(k).start()
    for b in range(1, min(ahead, bands)):
        launch(b)

    for b in range(bands):
        psf = psf_ref[b]
        gram[b] = t_matmul(psf, psf).astype(BF16)
        psf_t[b] = jnp.transpose(psf.astype(F32)).astype(BF16)
    for k in range(1, GROUP):
        home_copy(k).wait_recv()
    table_vmem[...] = sort_tables(homes_ref, upper, QUAD * piece_count, lanes)
    to_scalar = pltpu.make_async_copy(table_vmem, table_ref, table_sem)
    to_scalar.start()
    to_scalar.wait()

    def prepare(index, carry):
        spot = lax.broadcasted_iota(I32, corners_ref.shape, 1) == index
        spot = jnp.sum(jnp.where(spot, corners_ref[...], 0), axis=1, keepdims=True)
        row_at, col_at = spot[0:1, :], spot[1:2, :]
        rows = lax.broadcasted_iota(I32, (TILE, side), 0)
        inner = lax.broadcasted_iota(I32, (TILE, side), 1)
        row_hot = jnp.where(rows == inner + row_at, 1.0, 0.0).astype(BF16)
        cols = lax.broadcasted_iota(I32, (side, TILE), 1)
        inner_c = lax.broadcasted_iota(I32, (side, TILE), 0)
        col_hot = jnp.where(cols == inner_c + col_at, 1.0, 0.0).astype(BF16)
        for b in range(bands):
            row_psf[index, b] = matmul(row_hot, psf_ref[b]).astype(BF16)
            col_psf[b, index] = matmul(psf_t[b], col_hot).astype(BF16)
        return carry

    sed_table[...] = jnp.zeros_like(sed_table)

    def combine(b):
        pair_copy(b).wait_recv()
        for group in range(quads // 2):
            first = (2 * group + parity) * near_blends

            def join(index, carry, group=group, first=first):
                some = table_ref[3, first + index].astype(F32)
                mine_part = running[b % 2, table_ref[2, first + index]] * some
                summed[b, group, index] = (
                    mine_part + pair_buf[b, group, index].astype(F32)
                ).astype(BF16)
                return carry

            lax.fori_loop(0, near_blends, join, 0, unroll=4)
        for k in range(1, owners):
            incoming(b, k).start()
        arrived[b, pair, lower] = summed[b, pair, pl.ds(lower * owned, owned)]

    for b in range(bands):
        for k in range(1, QUAD):
            piece_copy(b, k).wait_recv()
        own_copy(b).wait()
        band_pieces = piece_bufs[b]

        def add(index, total, band_pieces=band_pieces, b=b):
            keep = table_ref[1, index].astype(F32)
            total = total * keep + band_pieces[table_ref[0, index]].astype(F32)
            running[b % 2, index] = total
            return total

        lax.fori_loop(0, QUAD * piece_count, add, jnp.zeros((quarter, lanes), F32), unroll=8)
        for group in range(quads // 2):
            first = (2 * group + 1 - parity) * near_blends

            def put(index, carry, b=b, group=group, first=first):
                some = table_ref[3, first + index].astype(F32)
                aside[b, group, index] = (
                    running[b % 2, table_ref[2, first + index]] * some
                ).astype(BF16)
                return carry

            lax.fori_loop(0, near_blends, put, 0, unroll=4)
        pair_copy(b).start()
        if b + ahead < bands:
            launch(b + ahead)
        giant_turn(b, 0)
        if b > 0:
            combine(b - 1)
        giant_turn(b, 1)
    combine(bands - 1)
    giant_turn(bands, 1)
    beside = {0: flow.pop(0)[2]}
    if owned > 1:
        beside[owned - 1] = flow.pop(0)[2]

    for b in range(bands):
        for k in range(1, owners):
            incoming(b, k).wait_recv()

    def blend(n, carry):
        source_of_row = lax.broadcasted_iota(I32, (table, lanes), 0) // bands
        act_ref[...] = jnp.where(source_of_row < counts_ref[n], 1.0, 0.0)
        spread_rows(sed_ref, spectra_ref[n], bands, sources, lanes)
        sed_ref[...] = sed_ref[...] * act_ref[...]
        for b in range(bands):
            total = arrived[b, 0, :, n].astype(F32)
            for g in range(1, quads // 2):
                total = total + arrived[b, g, :, n].astype(F32)
            grad_ref[b] = total.reshape(side, side)
        mean = grad_ref[0]
        for b in range(1, bands):
            mean = mean + grad_ref[b]
        base_map = jnp.maximum(mean / bands, 0.0)
        for k in range(sources):
            morph_ref[k] = (
                jnp.where(labels_ref[n] == k + 1, base_map, 0.0)
                * act_ref[k * bands : k * bands + 1, :]
            )
        for b in range(bands):
            back = matmul(psf_t[b], grad_ref[b].astype(BF16)).astype(BF16)
            adj_ref[b] = matmul(back, psf_ref[b])

        def iteration(it, carry):
            for b in range(bands):
                mix = mix_band(sed_ref, morph_ref, b, bands, sources)
                grad_ref[b] = adj_ref[b] - matmul(matmul(gram[b], mix).astype(BF16), gram[b])
            update(sed_ref, morph_ref, grad_ref, part_ref, energy_ref, act_ref, bands, sources)
            return carry

        lax.fori_loop(0, ITERS, iteration, 0)
        out_morph[n] = morph_ref[...].astype(BF16).reshape(out_morph.shape[1:])
        for k in range(1, count):
            outgoing(0, n, k).start()
        for h in range(2):
            held[h][me * owned + n] = out_morph[n, rank, h]
        diag = lax.broadcasted_iota(I32, (table, lanes), 0) == lax.broadcasted_iota(
            I32, (table, lanes), 1
        )
        line = jnp.sum(jnp.where(diag, sed_ref[...], 0.0), axis=0, keepdims=True)
        here = lax.broadcasted_iota(I32, sed_table.shape, 0) == n
        sed_table[...] = jnp.where(here, line, sed_table[...])

        for index, step in beside.items():
            pl.when(n == index)(step)
        return carry

    lax.fori_loop(0, owned, blend, 0)

    def second(n, carry):
        for k in range(1, count):
            outgoing(1, n, k).start()
        return carry

    lax.fori_loop(0, owned, second, 0)
    sed_all[me] = sed_table[...].astype(BF16)
    for k in range(1, count):
        sed_copy(k).start()
    out_sed[...] = sed_table[...]
    lax.fori_loop(0, piece_count, prepare, 0)

    def settle(h):
        def one(n, carry):
            for k in range(1, count):
                outgoing(h, n, k).wait_recv()
            return carry

        lax.fori_loop(0, owned, one, 0)

    def pick(h, k, chunks):
        other = lax.rem(rank + k, GROUP)

        def one(index, carry):
            for chunk in chunks:
                found = held[h][
                    table_ref[
                        4 + other // QUAD,
                        lax.rem(other, QUAD) * piece_count + chunk * per_chunk + index,
                    ]
                ]
                if k < GROUP:
                    picked[h, other, chunk, index] = found
                else:
                    landed[chunk, index, rank, h] = found
            return carry

        lax.fori_loop(0, per_chunk, one, 0)

    settle(0)
    for k in range(1, GROUP + 1):
        pick(0, k, range(CHUNKS))
        if k < GROUP:
            half_copy(k).start()
    while len(flow) > 1:
        flow.pop(0)[2]()
    settle(1)
    for chunk in range(CHUNKS):
        for k in range(1, GROUP + 1):
            pick(1, k, [chunk])
            if k < GROUP:
                last_copy(chunk, k).start()

    while flow:
        flow.pop(0)[2]()
    for k in range(1, count):
        sed_copy(k).wait_recv()
    out_tile[...] = jnp.zeros_like(out_tile)

    for k in range(1, GROUP):
        half_copy(k).wait_recv()

    def finish(chunk, carry):
        for k in range(1, GROUP):
            last_copy(chunk, k).wait_recv()
        for index in range(per_chunk):
            piece = chunk * per_chunk + index
            home = table_ref[4 + upper, lower * piece_count + piece]
            owner = lax.div(home, owned)
            place = home - owner * owned
            rows = sed_all[owner].astype(F32)
            here = lax.broadcasted_iota(I32, rows.shape, 0) == place
            line = jnp.sum(jnp.where(here, rows, 0.0), axis=0, keepdims=True)
            diag = lax.broadcasted_iota(I32, (table, lanes), 0) == lax.broadcasted_iota(
                I32, (table, lanes), 1
            )
            column = jnp.sum(jnp.where(diag, line, 0.0), axis=1, keepdims=True)
            sed_ref[...] = jnp.broadcast_to(column, (table, lanes))
            morph_ref[...] = landed[chunk, index].astype(F32).reshape(sources, side, side)
            for b in range(bands):
                mix = mix_band(sed_ref, morph_ref, b, bands, sources)
                left_ref[b, :, index * side : (index + 1) * side] = matmul(
                    row_psf[piece, b], mix
                ).astype(BF16)
        for b in range(bands):
            right = col_psf[b, pl.ds(chunk * per_chunk, per_chunk)].reshape(
                per_chunk * side, TILE
            )
            out_tile[b] = out_tile[b] + matmul(left_ref[b], right)
        return carry

    lax.fori_loop(0, CHUNKS, finish, 0)

    def drain(n, carry):
        for h in range(2):
            for k in range(1, count):
                outgoing(h, n, k).wait_send()
        return carry

    lax.fori_loop(0, owned, drain, 0)
    for b in range(bands):
        for k in range(1, QUAD):
            piece_copy(b, k).wait_send()
        pair_copy(b).wait_send()
        for k in range(1, owners):
            incoming(b, k).wait_send()
    for k in range(1, GROUP):
        home_copy(k).wait_send()
    for k in range(1, count):
        sed_copy(k).wait_send()
    for k in range(1, GROUP):
        half_copy(k).wait_send()
        for chunk in range(CHUNKS):
            last_copy(chunk, k).wait_send()
    for k in range(1, GROUP):
        strip_copy(k).wait_send()
        base_copy(k).wait_send()
    sent_bands(ITERS, giant_ref)
    for it in range(ITERS):
        sent_bands(it, mix_buf.at[it])
        relay_copy(it).wait_send()

        @pl.when(keeps)
        def _():
            for k in range(1, CHIPS):
                grad_copy(it, k).wait_send()


def on_device(
    pieces,
    piece_blend,
    corners,
    blend_home,
    source_count,
    footprint,
    spectra,
    giant_pieces,
    giant_footprint,
    giant_spectra,
    psf_matrix,
):
    count = lax.axis_size("tiles")
    piece_count, bands, side, _ = pieces.shape
    owned = footprint.shape[0]
    blend_count = blend_home.shape[0]
    sources = spectra.shape[1]
    back_rows = sources * side // GROUP // 2
    lanes = side
    table = sources * bands
    strip = side // GROUP
    per_chunk = piece_count // CHUNKS
    quarter = side // QUAD
    pairs = count // QUAD // 2

    dma = pltpu.SemaphoreType.DMA
    whole_map = (GROUP, strip, side)
    final_morph, sed_rows, tile_model, giant_morph = pl.pallas_call(
        functools.partial(core_kernel, count, bands, sources, owned, piece_count),
        out_shape=(
            jax.ShapeDtypeStruct((owned, GROUP, 2, back_rows, lanes), BF16),
            jax.ShapeDtypeStruct((16, lanes), F32),
            jax.ShapeDtypeStruct((bands, TILE, TILE), F32),
            jax.ShapeDtypeStruct((sources, side, side), F32),
        ),
        in_specs=[SMEM, SMEM, SMEM, ANY] + [VMEM] * 7,
        out_specs=(VMEM,) * 4,
        scratch_shapes=[
            pltpu.VMEM((GROUP, 8, lanes), I32),
            pltpu.VMEM((8, lanes), I32),
            pltpu.SMEM((8, lanes), I32),
            pltpu.VMEM((2, QUAD * piece_count, quarter, lanes), F32),
            pltpu.VMEM((bands, pairs, QUAD * owned, quarter, lanes), BF16),
            pltpu.VMEM((bands, pairs, QUAD * owned, quarter, lanes), BF16),
            pltpu.VMEM((bands, pairs, QUAD * owned, quarter, lanes), BF16),
            [pltpu.VMEM((QUAD * piece_count, quarter, lanes), BF16) for _ in range(bands)],
            pltpu.VMEM((bands, pairs, QUAD, owned, quarter, lanes), BF16),
            pltpu.VMEM((sources, side, side), F32),
            pltpu.VMEM((table, lanes), F32),
            pltpu.VMEM((table, lanes), F32),
            pltpu.VMEM((bands, side, side), F32),
            pltpu.VMEM((bands, side, side), F32),
            pltpu.VMEM((table, lanes), F32),
            pltpu.VMEM((table, lanes), F32),
            pltpu.VMEM((bands, side, side), BF16),
            pltpu.VMEM((bands, side, side), BF16),
            pltpu.VMEM((16, lanes), F32),
            pltpu.VMEM((count, 16, lanes), BF16),
            [pltpu.VMEM((blend_count, back_rows, lanes), BF16) for _ in range(2)],
            pltpu.VMEM((2, GROUP, CHUNKS, per_chunk, back_rows, lanes), BF16),
            pltpu.VMEM((CHUNKS, per_chunk, GROUP, 2, back_rows, lanes), BF16),
            pltpu.VMEM((piece_count, bands, TILE, side), BF16),
            pltpu.VMEM((bands, piece_count, side, TILE), BF16),
            pltpu.VMEM((bands, TILE, per_chunk * side), BF16),
            pltpu.VMEM(whole_map, F32),
            pltpu.VMEM(whole_map, F32),
            pltpu.VMEM(whole_map, F32),
            pltpu.VMEM((ITERS + 1, bands // 2) + whole_map, BF16),
            pltpu.VMEM((ITERS + 1, bands // 2) + whole_map, BF16),
            pltpu.VMEM((ITERS + 1, CHIPS) + whole_map, BF16),
            pltpu.VMEM((ITERS, bands // 2, 2) + whole_map, BF16),
            pltpu.VMEM((side, side), F32),
            pltpu.VMEM((table, lanes), F32),
            pltpu.VMEM((ITERS, 2, bands // 2, side, side), BF16),
            dma((bands,)),
            dma,
            dma((GROUP - 1,)),
            dma((GROUP - 1,)),
            dma((bands, QUAD - 1)),
            dma((bands, QUAD - 1)),
            dma((bands,)),
            dma((bands,)),
            dma((bands, pairs * QUAD - 1)),
            dma((bands, pairs * QUAD - 1)),
            dma((2, owned, count - 1)),
            dma((2, owned, count - 1)),
            dma((count - 1,)),
            dma((count - 1,)),
            dma((GROUP - 1,)),
            dma((GROUP - 1,)),
            dma((CHUNKS, GROUP - 1)),
            dma((CHUNKS, GROUP - 1)),
            dma((GROUP - 1,)),
            dma((GROUP - 1,)),
            dma((GROUP - 1,)),
            dma((GROUP - 1,)),
            dma((ITERS + 1,)),
            dma((ITERS + 1,)),
            dma((ITERS + 1, bands // 2)),
            dma((ITERS + 1, CHIPS)),
            dma((ITERS, CHIPS - 1)),
            dma((ITERS, bands // 2)),
            dma((ITERS,)),
            dma((ITERS,)),
        ],
        compiler_params=pltpu.CompilerParams(
            collective_id=0, has_side_effects=True, vmem_limit_bytes=56 << 20
        ),
        name="core",
    )(
        piece_blend,
        blend_home,
        source_count,
        pieces.reshape(piece_count, bands, QUAD, quarter, side),
        footprint,
        spectra,
        psf_matrix,
        corners.T,
        giant_pieces.reshape(bands // 2, 2, GROUP, strip, side),
        giant_footprint,
        giant_spectra,
    )
    final_sed = sed_rows[:owned, :table].reshape(owned, sources, bands).astype(BF16)
    return (
        final_morph.reshape(owned, sources, side, side),
        final_sed,
        tile_model[None],
        giant_morph[None],
    )


def solution(mesh):
    in_specs = (
        P(("groups", "tiles"), None, None, None),
        P(("groups", "tiles")),
        P(("groups", "tiles"), None),
        P("groups"),
        P(("groups", "tiles")),
        P(("groups", "tiles"), None, None),
        P(("groups", "tiles"), None, None),
        P(("groups", "tiles"), None, None, None),
        P(("groups", "tiles"), None, None),
        P(("groups", "tiles"), None, None),
        P(),
    )
    out_specs = (
        P(("groups", "tiles"), None, None, None),
        P(("groups", "tiles"), None, None),
        P(("groups", "tiles"), None, None, None),
        P(("groups", "tiles"), None, None, None),
    )
    return jax.shard_map(
        on_device, mesh=mesh, in_specs=in_specs, out_specs=out_specs, check_vma=False
    )
```

```python
import functools

import jax
import jax.numpy as jnp
from jax import lax
from jax.experimental import pallas as pl
from jax.experimental.pallas import tpu as pltpu
from jax.sharding import PartitionSpec as P

TILE = 256
ITERS = 3
GROUP = 8
QUAD = 4
CHIPS = GROUP // 2
UNIT = 16
KEEP_CHIP = ((0, 3, 1, 2), (3, 0, 2, 1))
CHUNKS = 4
MESH = pl.DeviceIdType.MESH
F32 = jnp.float32
BF16 = jnp.bfloat16
I32 = jnp.int32

step_size = 0.1

VMEM = pl.BlockSpec(memory_space=pltpu.VMEM)
SMEM = pl.BlockSpec(memory_space=pltpu.SMEM)
ANY = pl.BlockSpec(memory_space=pl.ANY)


def matmul(a, b):
    return jnp.dot(a, b, preferred_element_type=F32)


def t_matmul(a, b):
    return lax.dot_general(a, b, (((0,), (0,)), ((), ())), preferred_element_type=F32)


def barrier_all(me, count):
    barrier = pltpu.get_barrier_semaphore()
    for k in range(1, count):
        pl.semaphore_signal(
            barrier, inc=1, device_id={"tiles": lax.rem(me + k, count)}, device_id_type=MESH
        )
    pl.semaphore_wait(barrier, count - 1)


def remote(src, dst, send_sem, recv_sem, peer):
    return pltpu.make_async_remote_copy(
        src_ref=src,
        dst_ref=dst,
        send_sem=send_sem,
        recv_sem=recv_sem,
        device_id={"tiles": peer},
        device_id_type=MESH,
    )


def mix_band(sed_ref, maps, b, bands, sources):
    total = sed_ref[b : b + 1, :] * maps[0]
    for k in range(1, sources):
        row = k * bands + b
        total = total + sed_ref[row : row + 1, :] * maps[k]
    return total.astype(BF16)


def update(sed_ref, morph_ref, grad_ref, part_ref, energy_ref, act_ref, bands, sources):
    for k in range(sources):
        morph = morph_ref[k]
        energy = jnp.sum(morph * morph, axis=0, keepdims=True)
        push = None
        for b in range(bands):
            row = k * bands + b
            grad = grad_ref[b]
            part_ref[row : row + 1, :] = jnp.sum(morph * grad, axis=0, keepdims=True)
            energy_ref[row : row + 1, :] = energy
            term = sed_ref[row : row + 1, :] * grad
            push = term if push is None else push + term
        fresh = jnp.maximum(morph + step_size * push, 0.0)
        if act_ref is not None:
            fresh = fresh * act_ref[k * bands : k * bands + 1, :]
        morph_ref[k] = fresh
    inner = jnp.sum(part_ref[...], axis=1, keepdims=True)
    energy = jnp.sum(energy_ref[...], axis=1, keepdims=True)
    sed = jnp.maximum(sed_ref[...] + inner / (energy + 1.0), 0.0)
    if act_ref is not None:
        sed = sed * act_ref[...]
    sed_ref[...] = sed


def spread_rows(sed_ref, table, bands, sources, lanes):
    for k in range(sources):
        line = jnp.broadcast_to(table[k : k + 1, :], (bands, bands))
        row = lax.broadcasted_iota(I32, (bands, bands), 0)
        col = lax.broadcasted_iota(I32, (bands, bands), 1)
        value = jnp.sum(jnp.where(row == col, line, 0.0), axis=1, keepdims=True)
        sed_ref[k * bands : (k + 1) * bands, :] = jnp.broadcast_to(value, (bands, lanes))


def cuts(bands, side):
    steps = []
    for b in range(bands):
        if b in (0, bands - 1) and side // 2 % (QUAD * UNIT) == 0:
            steps += [(b, 0, side // 2), (b, side // 2, side // 2)]
        else:
            steps.append((b, 0, side))
    return steps


def sort_tables(homes_ref, upper, used, lanes):
    line = homes_ref[0]
    for source in range(1, GROUP):
        line = line + homes_ref[source]
    near = jnp.where(upper == 0, line[0:1, :], line[1:2, :])
    near = jnp.where(lax.broadcasted_iota(I32, (1, lanes), 1) < used, near, 2 * lanes)
    across = jnp.broadcast_to(near, (lanes, lanes))
    sub = lax.broadcasted_iota(I32, (lanes, lanes), 0)
    lane = lax.broadcasted_iota(I32, (lanes, lanes), 1)
    down = jnp.sum(jnp.where(sub == lane, across, 0), axis=1, keepdims=True)
    key_across = across * lanes + lane
    key_down = down * lanes + sub
    place = jnp.sum(jnp.where(key_across < key_down, 1, 0), axis=1, keepdims=True)
    order = jnp.sum(jnp.where(place == lane, sub, 0), axis=0, keepdims=True)
    sorted_home = jnp.sum(jnp.where(place == lane, down, 0), axis=0, keepdims=True)
    before = jnp.sum(jnp.where(place + 1 == lane, down, 0), axis=0, keepdims=True)
    keep = jnp.where(sorted_home == before, 1, 0)
    upto = jnp.sum(jnp.where(down <= lane, 1, 0), axis=0, keepdims=True)
    same = jnp.sum(jnp.where(down == lane, 1, 0), axis=0, keepdims=True)
    last = jnp.maximum(upto - 1, 0)
    some = jnp.where(same > 0, 1, 0)
    rows = [order, keep, last, some]
    for half in range(GROUP // QUAD):
        rows.append(line[half : half + 1, :])
    which = lax.broadcasted_iota(I32, (8, lanes), 0)
    result = jnp.zeros((8, lanes), I32)
    for index, row in enumerate(rows):
        result = jnp.where(which == index, row, result)
    return result


def core_kernel(
    count,
    bands,
    sources,
    owned,
    piece_count,
    blend_ref,
    home_of_ref,
    counts_ref,
    pieces_ref,
    labels_ref,
    spectra_ref,
    psf_ref,
    corners_ref,
    giant_ref,
    giant_labels_ref,
    giant_spectra_ref,
    out_morph,
    out_sed,
    out_tile,
    out_giant,
    homes_ref,
    table_vmem,
    table_ref,
    running,
    aside,
    pair_buf,
    summed,
    piece_bufs,
    arrived,
    morph_ref,
    sed_ref,
    act_ref,
    adj_ref,
    grad_ref,
    part_ref,
    energy_ref,
    gram,
    psf_t,
    sed_table,
    sed_all,
    held,
    picked,
    landed,
    row_psf,
    col_psf,
    left_ref,
    band_total,
    strips,
    base_buf,
    chip_buf,
    chip_out,
    band_buf,
    mix_buf,
    adj_own,
    giant_sed,
    giant_grad,
    own_sem,
    table_sem,
    home_send,
    home_recv,
    piece_send,
    piece_recv,
    pair_send,
    pair_recv,
    in_send,
    in_recv,
    back_send,
    back_recv,
    sed_send,
    sed_recv,
    half_send,
    half_recv,
    last_send,
    last_recv,
    strip_send,
    strip_recv,
    base_send,
    base_recv,
    chip_send,
    chip_recv,
    band_send,
    band_recv,
    grad_send,
    grad_recv,
    relay_send,
    relay_recv,
):
    me = lax.axis_index("tiles")
    rank = lax.rem(me, GROUP)
    base = me - rank
    mine = me // GROUP
    side = labels_ref.shape[1]
    lanes = side
    strip = side // GROUP
    plan = cuts(bands, side)
    units = [rows // QUAD // UNIT for _, _, rows in plan]
    quads = count // QUAD
    near_blends = QUAD * owned
    table = bands * sources
    per_chunk = piece_count // CHUNKS
    barrier_all(me, count)

    upper = rank // QUAD
    lower = lax.rem(rank, QUAD)
    core = lax.rem(rank, 2)
    chip = rank // 2
    partner_core = base + rank + 1 - 2 * core
    half_bands = bands // 2

    def keeper(i):
        return jnp.where(core == 0, KEEP_CHIP[0][i], KEEP_CHIP[1][i])

    keeps = chip < 0
    own_index = 0
    for i in range(half_bands):
        keeps = jnp.logical_or(keeps, keeper(i) == chip)
        own_index = jnp.where(keeper(i) == chip, i, own_index)
    own_band = 2 * own_index + core

    def home_copy(k):
        other = lax.rem(rank + k, GROUP)
        return remote(
            homes_ref.at[rank], homes_ref.at[rank], home_send.at[k - 1], home_recv.at[k - 1],
            base + other,
        )

    quad = me // QUAD
    pair = quad // 2
    parity = lax.rem(quad, 2)

    def piece_slot(c):
        return piece_bufs[c].at[pl.ds(lower * piece_count, piece_count)]

    def piece_source(c, other):
        band, first, _ = plan[c]
        return pieces_ref.at[:, band, pl.ds(first // UNIT + other * units[c], units[c])]

    def piece_copy(c, k):
        other = lax.rem(lower + k, QUAD)
        return remote(
            piece_source(c, other), piece_slot(c), piece_send.at[c, k - 1],
            piece_recv.at[c, k - 1], quad * QUAD + other,
        )

    def own_copy(c):
        return pltpu.make_async_copy(piece_source(c, lower), piece_slot(c), own_sem.at[c])

    def pair_copy(b):
        partner = (quad + 1 - 2 * parity) * QUAD + lower
        return remote(aside[b], pair_buf[b], pair_send.at[b], pair_recv.at[b], partner)

    def incoming(b, k):
        to_pair = lax.rem(pair + k // QUAD, quads // 2)
        to_lower = lax.rem(lower + k % QUAD, QUAD)
        return remote(
            summed[b].at[to_pair, pl.ds(to_lower * owned, owned)],
            arrived[b].at[pair, lower],
            in_send.at[b, k - 1],
            in_recv.at[b, k - 1],
            (2 * to_pair + parity) * QUAD + to_lower,
        )

    owners = quads // 2 * QUAD

    def outgoing(h, n, k):
        peer = lax.rem(me + k, count)
        return remote(
            out_morph.at[n, lax.rem(peer, GROUP), h],
            held[h].at[me * owned + n],
            back_send.at[h, n, k - 1],
            back_recv.at[h, n, k - 1],
            peer,
        )

    def sed_copy(k):
        return remote(
            sed_all.at[me], sed_all.at[me], sed_send.at[k - 1], sed_recv.at[k - 1],
            lax.rem(me + k, count),
        )

    def half_copy(k):
        other = lax.rem(rank + k, GROUP)
        return remote(
            picked.at[0, other],
            landed.at[:, :, rank, 0],
            half_send.at[k - 1],
            half_recv.at[k - 1],
            base + other,
        )

    def last_copy(chunk, k):
        other = lax.rem(rank + k, GROUP)
        return remote(
            picked.at[1, other, chunk],
            landed.at[chunk, :, rank, 1],
            last_send.at[chunk, k - 1],
            last_recv.at[chunk, k - 1],
            base + other,
        )

    def strip_copy(k):
        other = lax.rem(rank + k, GROUP)
        return remote(
            band_total.at[other], strips.at[rank], strip_send.at[k - 1], strip_recv.at[k - 1],
            base + other,
        )

    def base_copy(k):
        other = lax.rem(rank + k, GROUP)
        return remote(
            base_buf.at[rank], base_buf.at[rank], base_send.at[k - 1], base_recv.at[k - 1],
            base + other,
        )

    def chip_copy(slot, src):
        return remote(
            src.at[:, 1 - core], chip_buf.at[slot], chip_send.at[slot], chip_recv.at[slot],
            partner_core,
        )

    def band_copy(slot, i):
        return remote(
            chip_out.at[slot, i], band_buf.at[slot, chip], band_send.at[slot, i],
            band_recv.at[slot, chip], base + 2 * keeper(i) + core,
        )

    def grad_copy(slot, k):
        other = lax.rem(chip + k, CHIPS)
        return remote(
            giant_grad.at[slot, core, own_index],
            giant_grad.at[slot, core, own_index],
            grad_send.at[slot, k - 1],
            grad_recv.at[slot, own_index],
            base + 2 * other + core,
        )

    def relay_copy(slot):
        return remote(
            giant_grad.at[slot, core], giant_grad.at[slot, core], relay_send.at[slot],
            relay_recv.at[slot], partner_core,
        )

    def chip_sum(slot, ref):
        chip_copy(slot, ref).wait_recv()
        for i in range(half_bands):
            value = ref[i, core].astype(F32) + chip_buf[slot, i].astype(F32)
            chip_out[slot, i] = value.astype(BF16)

            @pl.when(keeper(i) != chip)
            def _():
                band_copy(slot, i).start()

            @pl.when(keeper(i) == chip)
            def _():
                band_buf[slot, chip] = chip_out[slot, i]

    def sent_bands(slot, ref):
        chip_copy(slot, ref).wait_send()
        for i in range(half_bands):
            @pl.when(keeper(i) != chip)
            def _():
                band_copy(slot, i).wait_send()

    def kept_sum(slot):
        for k in range(1, CHIPS):
            source = lax.rem(chip + k, CHIPS)
            remote(
                band_buf.at[slot, source], band_buf.at[slot, source], band_send.at[slot, 0],
                band_recv.at[slot, source], base + 2 * source + core,
            ).wait_recv()
        total = band_buf[slot, 0].astype(F32)
        for source in range(1, CHIPS):
            total = total + band_buf[slot, source].astype(F32)
        return total.reshape(side, side).astype(BF16)

    def giant_open():
        for k in range(1, GROUP):
            strip_copy(k).wait_recv()
        mean = None
        for k in range(GROUP):
            source = lax.rem(rank + k, GROUP)
            part = band_total[rank] if k == 0 else strips[source]
            mean = part if mean is None else mean + part
        base_buf[rank] = jnp.maximum(mean / bands, 0.0)
        for k in range(1, GROUP):
            base_copy(k).start()

        chip_sum(ITERS, giant_ref)

    def giant_mix(slot):
        for b in range(bands):
            mix = mix_band(giant_sed, out_giant, b, bands, sources)
            mix_buf[slot, b // 2, b % 2] = mix.reshape(GROUP, strip, side)
        chip_copy(slot, mix_buf.at[slot]).start()

    def giant_chip(slot):
        chip_sum(slot, mix_buf.at[slot])

    def giant_start():
        for k in range(1, GROUP):
            base_copy(k).wait_recv()
        base_map = base_buf[...].reshape(side, side)
        for k in range(sources):
            out_giant[k] = jnp.where(giant_labels_ref[0] == k + 1, base_map, 0.0)
        spread_rows(giant_sed, giant_spectra_ref[0], bands, sources, lanes)
        giant_mix(0)

    def giant_keep(slot):
        @pl.when(keeps)
        def _():
            if slot == 0:
                total = kept_sum(ITERS)
                back = matmul(psf_t[own_band], total).astype(BF16)
                adj_own[...] = matmul(back, psf_ref[own_band])
            total = kept_sum(slot)
            gram_own = gram[own_band]
            grad = adj_own[...] - matmul(matmul(gram_own, total).astype(BF16), gram_own)
            giant_grad[slot, core, own_index] = grad.astype(BF16)
            for k in range(1, CHIPS):
                grad_copy(slot, k).start()

    def giant_relay(slot):
        for i in range(half_bands):
            @pl.when(keeper(i) != chip)
            def _():
                remote(
                    giant_grad.at[slot, core, i], giant_grad.at[slot, core, i],
                    grad_send.at[slot, 0], grad_recv.at[slot, i], base + 2 * keeper(i) + core,
                ).wait_recv()

        relay_copy(slot).start()

    def giant_update(slot):
        relay_copy(slot).wait_recv()
        for b in range(bands):
            grad_ref[b] = giant_grad[slot, b % 2, b // 2].astype(F32)
        update(giant_sed, out_giant, grad_ref, part_ref, energy_ref, None, bands, sources)
        if slot + 1 < ITERS:
            giant_mix(slot + 1)

    flow = [(0, 1, giant_open), (1, 0, giant_start), (1, 1, functools.partial(giant_chip, 0))]
    turn = 2
    for it in range(ITERS):
        flow.append((turn, 0, functools.partial(giant_keep, it)))
        flow.append((turn + 1, 0, functools.partial(giant_relay, it)))
        flow.append((turn + 1, 1, functools.partial(giant_update, it)))
        if it + 1 < ITERS:
            flow.append((turn + 2, 0, functools.partial(giant_chip, it + 1)))
        turn += 3

    def giant_turn(b, part):
        while flow and flow[0][:2] <= (b, part):
            flow.pop(0)[2]()

    def launch(b):
        for k in range(1, QUAD):
            piece_copy(b, k).start()
        own_copy(b).start()

    at = lax.broadcasted_iota(I32, (8, lanes), 1) - lower * piece_count
    at = jnp.where(lax.broadcasted_iota(I32, (8, lanes), 0) == upper, at, -1)
    line = jnp.zeros((8, lanes), I32)
    for index in range(piece_count):
        line = jnp.where(at == index, home_of_ref[blend_ref[index]], line)
    homes_ref[rank] = line
    for k in range(1, GROUP):
        home_copy(k).start()
    ahead = 2
    launch(0)
    chip_copy(ITERS, giant_ref).start()
    totals = giant_ref[0, 0].astype(F32)
    for b in range(1, bands):
        totals = totals + giant_ref[b // 2, b % 2].astype(F32)
    band_total[...] = totals
    for k in range(1, GROUP):
        strip_copy(k).start()
    for c in range(1, min(ahead, len(plan))):
        launch(c)

    for b in range(bands):
        psf = psf_ref[b]
        gram[b] = t_matmul(psf, psf).astype(BF16)
        psf_t[b] = jnp.transpose(psf.astype(F32)).astype(BF16)
    for k in range(1, GROUP):
        home_copy(k).wait_recv()
    table_vmem[...] = sort_tables(homes_ref, upper, QUAD * piece_count, lanes)
    to_scalar = pltpu.make_async_copy(table_vmem, table_ref, table_sem)
    to_scalar.start()
    to_scalar.wait()

    def prepare(index, carry):
        spot = lax.broadcasted_iota(I32, corners_ref.shape, 1) == index
        spot = jnp.sum(jnp.where(spot, corners_ref[...], 0), axis=1, keepdims=True)
        row_at, col_at = spot[0:1, :], spot[1:2, :]
        rows = lax.broadcasted_iota(I32, (TILE, side), 0)
        inner = lax.broadcasted_iota(I32, (TILE, side), 1)
        row_hot = jnp.where(rows == inner + row_at, 1.0, 0.0).astype(BF16)
        cols = lax.broadcasted_iota(I32, (side, TILE), 1)
        inner_c = lax.broadcasted_iota(I32, (side, TILE), 0)
        col_hot = jnp.where(cols == inner_c + col_at, 1.0, 0.0).astype(BF16)
        for b in range(bands):
            row_psf[index, b] = matmul(row_hot, psf_ref[b]).astype(BF16)
            col_psf[b, index] = matmul(psf_t[b], col_hot).astype(BF16)
        return carry

    sed_table[...] = jnp.zeros_like(sed_table)

    def combine(c):
        pair_copy(c).wait_recv()
        for group in range(quads // 2):
            first = (2 * group + parity) * near_blends

            def join(index, carry, group=group, first=first):
                some = table_ref[3, first + index].astype(F32)
                mine_part = running[c % 2, table_ref[2, first + index], : units[c]] * some
                summed[c][group, index] = (
                    mine_part + pair_buf[c][group, index].astype(F32)
                ).astype(BF16)
                return carry

            lax.fori_loop(0, near_blends, join, 0, unroll=4)
        for k in range(1, owners):
            incoming(c, k).start()
        arrived[c][pair, lower] = summed[c][pair, pl.ds(lower * owned, owned)]

    for c in range(len(plan)):
        for k in range(1, QUAD):
            piece_copy(c, k).wait_recv()
        own_copy(c).wait()
        band_pieces = piece_bufs[c]

        def add(index, total, band_pieces=band_pieces, c=c):
            keep = table_ref[1, index].astype(F32)
            total = total * keep + band_pieces[table_ref[0, index]].astype(F32)
            running[c % 2, index, : units[c]] = total
            return total

        lax.fori_loop(0, QUAD * piece_count, add, jnp.zeros((units[c], UNIT, lanes), F32), unroll=8)
        for group in range(quads // 2):
            first = (2 * group + 1 - parity) * near_blends

            def put(index, carry, c=c, group=group, first=first):
                some = table_ref[3, first + index].astype(F32)
                aside[c][group, index] = (
                    running[c % 2, table_ref[2, first + index], : units[c]] * some
                ).astype(BF16)
                return carry

            lax.fori_loop(0, near_blends, put, 0, unroll=4)
        pair_copy(c).start()
        if c + ahead < len(plan):
            launch(c + ahead)
        giant_turn(c, 0)
        if c > 0:
            combine(c - 1)
        giant_turn(c, 1)
    combine(len(plan) - 1)
    beside = {}
    while len(flow) > 2 and len(beside) < owned:
        beside[len(beside)] = flow.pop(0)[2]

    for c in range(len(plan)):
        for k in range(1, owners):
            incoming(c, k).wait_recv()

    def blend(n, carry):
        source_of_row = lax.broadcasted_iota(I32, (table, lanes), 0) // bands
        act_ref[...] = jnp.where(source_of_row < counts_ref[n], 1.0, 0.0)
        spread_rows(sed_ref, spectra_ref[n], bands, sources, lanes)
        sed_ref[...] = sed_ref[...] * act_ref[...]
        for b in range(bands):
            for c, (band, first, rows) in enumerate(plan):
                if band == b:
                    total = arrived[c][0, :, n].astype(F32)
                    for g in range(1, quads // 2):
                        total = total + arrived[c][g, :, n].astype(F32)
                    grad_ref[b, first : first + rows, :] = total.reshape(rows, side)
        mean = grad_ref[0]
        for b in range(1, bands):
            mean = mean + grad_ref[b]
        base_map = jnp.maximum(mean / bands, 0.0)
        for k in range(sources):
            morph_ref[k] = (
                jnp.where(labels_ref[n] == k + 1, base_map, 0.0)
                * act_ref[k * bands : k * bands + 1, :]
            )
        for b in range(bands):
            back = matmul(psf_t[b], grad_ref[b].astype(BF16)).astype(BF16)
            adj_ref[b] = matmul(back, psf_ref[b])

        def iteration(it, carry):
            for b in range(bands):
                mix = mix_band(sed_ref, morph_ref, b, bands, sources)
                grad_ref[b] = adj_ref[b] - matmul(matmul(gram[b], mix).astype(BF16), gram[b])
            update(sed_ref, morph_ref, grad_ref, part_ref, energy_ref, act_ref, bands, sources)
            return carry

        lax.fori_loop(0, ITERS, iteration, 0)
        out_morph[n] = morph_ref[...].astype(BF16).reshape(out_morph.shape[1:])
        for k in range(1, count):
            outgoing(0, n, k).start()
        for h in range(2):
            held[h][me * owned + n] = out_morph[n, rank, h]
        diag = lax.broadcasted_iota(I32, (table, lanes), 0) == lax.broadcasted_iota(
            I32, (table, lanes), 1
        )
        line = jnp.sum(jnp.where(diag, sed_ref[...], 0.0), axis=0, keepdims=True)
        here = lax.broadcasted_iota(I32, sed_table.shape, 0) == n
        sed_table[...] = jnp.where(here, line, sed_table[...])

        for index, step in beside.items():
            pl.when(n == index)(step)
        return carry

    lax.fori_loop(0, owned, blend, 0)

    def second(n, carry):
        for k in range(1, count):
            outgoing(1, n, k).start()
        return carry

    lax.fori_loop(0, owned, second, 0)
    sed_all[me] = sed_table[...].astype(BF16)
    for k in range(1, count):
        sed_copy(k).start()
    out_sed[...] = sed_table[...]
    lax.fori_loop(0, piece_count, prepare, 0)

    def settle(h):
        def one(n, carry):
            for k in range(1, count):
                outgoing(h, n, k).wait_recv()
            return carry

        lax.fori_loop(0, owned, one, 0)

    def pick(h, k, chunks):
        other = lax.rem(rank + k, GROUP)

        def one(index, carry):
            for chunk in chunks:
                found = held[h][
                    table_ref[
                        4 + other // QUAD,
                        lax.rem(other, QUAD) * piece_count + chunk * per_chunk + index,
                    ]
                ]
                if k < GROUP:
                    picked[h, other, chunk, index] = found
                else:
                    landed[chunk, index, rank, h] = found
            return carry

        lax.fori_loop(0, per_chunk, one, 0)

    settle(0)
    for k in range(1, GROUP + 1):
        pick(0, k, range(CHUNKS))
        if k < GROUP:
            half_copy(k).start()
    while len(flow) > 1:
        flow.pop(0)[2]()
    settle(1)
    for chunk in range(CHUNKS):
        for k in range(1, GROUP + 1):
            pick(1, k, [chunk])
            if k < GROUP:
                last_copy(chunk, k).start()

    while flow:
        flow.pop(0)[2]()
    for k in range(1, count):
        sed_copy(k).wait_recv()
    out_tile[...] = jnp.zeros_like(out_tile)

    for k in range(1, GROUP):
        half_copy(k).wait_recv()

    def finish(chunk, carry):
        for k in range(1, GROUP):
            last_copy(chunk, k).wait_recv()
        for index in range(per_chunk):
            piece = chunk * per_chunk + index
            home = table_ref[4 + upper, lower * piece_count + piece]
            owner = lax.div(home, owned)
            place = home - owner * owned
            rows = sed_all[owner].astype(F32)
            here = lax.broadcasted_iota(I32, rows.shape, 0) == place
            line = jnp.sum(jnp.where(here, rows, 0.0), axis=0, keepdims=True)
            diag = lax.broadcasted_iota(I32, (table, lanes), 0) == lax.broadcasted_iota(
                I32, (table, lanes), 1
            )
            column = jnp.sum(jnp.where(diag, line, 0.0), axis=1, keepdims=True)
            sed_ref[...] = jnp.broadcast_to(column, (table, lanes))
            morph_ref[...] = landed[chunk, index].astype(F32).reshape(sources, side, side)
            for b in range(bands):
                mix = mix_band(sed_ref, morph_ref, b, bands, sources)
                left_ref[b, :, index * side : (index + 1) * side] = matmul(
                    row_psf[piece, b], mix
                ).astype(BF16)
        for b in range(bands):
            right = col_psf[b, pl.ds(chunk * per_chunk, per_chunk)].reshape(
                per_chunk * side, TILE
            )
            out_tile[b] = out_tile[b] + matmul(left_ref[b], right)
        return carry

    lax.fori_loop(0, CHUNKS, finish, 0)

    def drain(n, carry):
        for h in range(2):
            for k in range(1, count):
                outgoing(h, n, k).wait_send()
        return carry

    lax.fori_loop(0, owned, drain, 0)
    for c in range(len(plan)):
        for k in range(1, QUAD):
            piece_copy(c, k).wait_send()
        pair_copy(c).wait_send()
        for k in range(1, owners):
            incoming(c, k).wait_send()
    for k in range(1, GROUP):
        home_copy(k).wait_send()
    for k in range(1, count):
        sed_copy(k).wait_send()
    for k in range(1, GROUP):
        half_copy(k).wait_send()
        for chunk in range(CHUNKS):
            last_copy(chunk, k).wait_send()
    for k in range(1, GROUP):
        strip_copy(k).wait_send()
        base_copy(k).wait_send()
    sent_bands(ITERS, giant_ref)
    for it in range(ITERS):
        sent_bands(it, mix_buf.at[it])
        relay_copy(it).wait_send()

        @pl.when(keeps)
        def _():
            for k in range(1, CHIPS):
                grad_copy(it, k).wait_send()


def deliver_kernel(
    bands,
    morph_ref,
    sed_ref,
    tile_ref,
    giant_ref,
    out_morph,
    out_sed,
    out_tile,
    out_giant,
    morph_sem,
    tile_sem,
    giant_sem,
):
    copies = []
    for source, target, sem in (
        (tile_ref, out_tile, tile_sem),
        (morph_ref, out_morph, morph_sem),
        (giant_ref, out_giant, giant_sem),
    ):
        for index in range(source.shape[0]):
            copies.append(
                pltpu.make_async_copy(source.at[index], target.at[index], sem.at[index])
            )
    for copy in copies:
        copy.start()
    owned, sources, _ = out_sed.shape
    for k in range(sources):
        out_sed[:, k, :] = sed_ref[:owned, k * bands : (k + 1) * bands].astype(BF16)
    for copy in copies:
        copy.wait()


def on_device(
    pieces,
    piece_blend,
    corners,
    blend_home,
    source_count,
    footprint,
    spectra,
    giant_pieces,
    giant_footprint,
    giant_spectra,
    psf_matrix,
):
    count = lax.axis_size("tiles")
    piece_count, bands, side, _ = pieces.shape
    owned = footprint.shape[0]
    blend_count = blend_home.shape[0]
    sources = spectra.shape[1]
    back_rows = sources * side // GROUP // 2
    lanes = side
    table = sources * bands
    strip = side // GROUP
    per_chunk = piece_count // CHUNKS
    plan = cuts(bands, side)
    units = [cut // QUAD // UNIT for _, _, cut in plan]
    pairs = count // QUAD // 2

    dma = pltpu.SemaphoreType.DMA
    whole_map = (GROUP, strip, side)
    final_morph, sed_rows, tile_model, giant_morph = pl.pallas_call(
        functools.partial(core_kernel, count, bands, sources, owned, piece_count),
        out_shape=(
            jax.ShapeDtypeStruct((owned, GROUP, 2, back_rows, lanes), BF16),
            jax.ShapeDtypeStruct((16, lanes), F32),
            jax.ShapeDtypeStruct((bands, TILE, TILE), F32),
            jax.ShapeDtypeStruct((sources, side, side), F32),
        ),
        in_specs=[SMEM, SMEM, SMEM, ANY] + [VMEM] * 7,
        out_specs=(VMEM,) * 4,
        scratch_shapes=[
            pltpu.VMEM((GROUP, 8, lanes), I32),
            pltpu.VMEM((8, lanes), I32),
            pltpu.SMEM((8, lanes), I32),
            pltpu.VMEM((2, QUAD * piece_count, max(units), UNIT, lanes), F32),
            [pltpu.VMEM((pairs, QUAD * owned, u, UNIT, lanes), BF16) for u in units],
            [pltpu.VMEM((pairs, QUAD * owned, u, UNIT, lanes), BF16) for u in units],
            [pltpu.VMEM((pairs, QUAD * owned, u, UNIT, lanes), BF16) for u in units],
            [pltpu.VMEM((QUAD * piece_count, u, UNIT, lanes), BF16) for u in units],
            [pltpu.VMEM((pairs, QUAD, owned, u, UNIT, lanes), BF16) for u in units],
            pltpu.VMEM((sources, side, side), F32),
            pltpu.VMEM((table, lanes), F32),
            pltpu.VMEM((table, lanes), F32),
            pltpu.VMEM((bands, side, side), F32),
            pltpu.VMEM((bands, side, side), F32),
            pltpu.VMEM((table, lanes), F32),
            pltpu.VMEM((table, lanes), F32),
            pltpu.VMEM((bands, side, side), BF16),
            pltpu.VMEM((bands, side, side), BF16),
            pltpu.VMEM((16, lanes), F32),
            pltpu.VMEM((count, 16, lanes), BF16),
            [pltpu.VMEM((blend_count, back_rows, lanes), BF16) for _ in range(2)],
            pltpu.VMEM((2, GROUP, CHUNKS, per_chunk, back_rows, lanes), BF16),
            pltpu.VMEM((CHUNKS, per_chunk, GROUP, 2, back_rows, lanes), BF16),
            pltpu.VMEM((piece_count, bands, TILE, side), BF16),
            pltpu.VMEM((bands, piece_count, side, TILE), BF16),
            pltpu.VMEM((bands, TILE, per_chunk * side), BF16),
            pltpu.VMEM(whole_map, F32),
            pltpu.VMEM(whole_map, F32),
            pltpu.VMEM(whole_map, F32),
            pltpu.VMEM((ITERS + 1, bands // 2) + whole_map, BF16),
            pltpu.VMEM((ITERS + 1, bands // 2) + whole_map, BF16),
            pltpu.VMEM((ITERS + 1, CHIPS) + whole_map, BF16),
            pltpu.VMEM((ITERS, bands // 2, 2) + whole_map, BF16),
            pltpu.VMEM((side, side), F32),
            pltpu.VMEM((table, lanes), F32),
            pltpu.VMEM((ITERS, 2, bands // 2, side, side), BF16),
            dma((len(plan),)),
            dma,
            dma((GROUP - 1,)),
            dma((GROUP - 1,)),
            dma((len(plan), QUAD - 1)),
            dma((len(plan), QUAD - 1)),
            dma((len(plan),)),
            dma((len(plan),)),
            dma((len(plan), pairs * QUAD - 1)),
            dma((len(plan), pairs * QUAD - 1)),
            dma((2, owned, count - 1)),
            dma((2, owned, count - 1)),
            dma((count - 1,)),
            dma((count - 1,)),
            dma((GROUP - 1,)),
            dma((GROUP - 1,)),
            dma((CHUNKS, GROUP - 1)),
            dma((CHUNKS, GROUP - 1)),
            dma((GROUP - 1,)),
            dma((GROUP - 1,)),
            dma((GROUP - 1,)),
            dma((GROUP - 1,)),
            dma((ITERS + 1,)),
            dma((ITERS + 1,)),
            dma((ITERS + 1, bands // 2)),
            dma((ITERS + 1, CHIPS)),
            dma((ITERS, CHIPS - 1)),
            dma((ITERS, bands // 2)),
            dma((ITERS,)),
            dma((ITERS,)),
        ],
        compiler_params=pltpu.CompilerParams(
            collective_id=0, has_side_effects=True, vmem_limit_bytes=56 << 20
        ),
        name="core",
    )(
        piece_blend,
        blend_home,
        source_count,
        pieces.reshape(piece_count, bands, side // UNIT, UNIT, side),
        footprint,
        spectra,
        psf_matrix,
        corners.T,
        giant_pieces.reshape(bands // 2, 2, GROUP, strip, side),
        giant_footprint,
        giant_spectra,
    )
    final_morph, final_sed, tile_model, giant_morph = pl.pallas_call(
        functools.partial(deliver_kernel, bands),
        out_shape=(
            jax.ShapeDtypeStruct((owned, sources, side, side), BF16),
            jax.ShapeDtypeStruct((owned, sources, bands), BF16),
            jax.ShapeDtypeStruct((bands, TILE, TILE), F32),
            jax.ShapeDtypeStruct((sources, side, side), F32),
        ),
        in_specs=[ANY, VMEM, ANY, ANY],
        out_specs=(ANY, VMEM, ANY, ANY),
        scratch_shapes=[dma((owned,)), dma((bands,)), dma((sources,))],
        name="deliver",
    )(
        final_morph.reshape(owned, sources, side, side),
        sed_rows,
        tile_model,
        giant_morph,
    )
    return (final_morph, final_sed, tile_model[None], giant_morph[None])


def solution(mesh):
    in_specs = (
        P(("groups", "tiles"), None, None, None),
        P(("groups", "tiles")),
        P(("groups", "tiles"), None),
        P("groups"),
        P(("groups", "tiles")),
        P(("groups", "tiles"), None, None),
        P(("groups", "tiles"), None, None),
        P(("groups", "tiles"), None, None, None),
        P(("groups", "tiles"), None, None),
        P(("groups", "tiles"), None, None),
        P(),
    )
    out_specs = (
        P(("groups", "tiles"), None, None, None),
        P(("groups", "tiles"), None, None),
        P(("groups", "tiles"), None, None, None),
        P(("groups", "tiles"), None, None, None),
    )
    return jax.shard_map(
        on_device, mesh=mesh, in_specs=in_specs, out_specs=out_specs, check_vma=False
    )
```

```python
import functools

import jax
import jax.numpy as jnp
from jax import lax
from jax.experimental import pallas as pl
from jax.experimental.pallas import tpu as pltpu
from jax.sharding import PartitionSpec as P

TILE = 256
ITERS = 3
GROUP = 8
QUAD = 4
CHIPS = GROUP // 2
UNIT = 16
KEEP_CHIP = ((0, 3, 1, 2), (3, 0, 2, 1))
CHUNKS = 4
MESH = pl.DeviceIdType.MESH
F32 = jnp.float32
BF16 = jnp.bfloat16
I32 = jnp.int32

step_size = 0.1

VMEM = pl.BlockSpec(memory_space=pltpu.VMEM)
SMEM = pl.BlockSpec(memory_space=pltpu.SMEM)
ANY = pl.BlockSpec(memory_space=pl.ANY)


def matmul(a, b):
    return jnp.dot(a, b, preferred_element_type=F32)


def t_matmul(a, b):
    return lax.dot_general(a, b, (((0,), (0,)), ((), ())), preferred_element_type=F32)


def barrier_all(me, count):
    barrier = pltpu.get_barrier_semaphore()
    for k in range(1, count):
        pl.semaphore_signal(
            barrier, inc=1, device_id={"tiles": lax.rem(me + k, count)}, device_id_type=MESH
        )
    pl.semaphore_wait(barrier, count - 1)


def remote(src, dst, send_sem, recv_sem, peer):
    return pltpu.make_async_remote_copy(
        src_ref=src,
        dst_ref=dst,
        send_sem=send_sem,
        recv_sem=recv_sem,
        device_id={"tiles": peer},
        device_id_type=MESH,
    )


def mix_band(sed_ref, maps, b, bands, sources):
    total = sed_ref[b : b + 1, :] * maps[0]
    for k in range(1, sources):
        row = k * bands + b
        total = total + sed_ref[row : row + 1, :] * maps[k]
    return total.astype(BF16)


def update(sed_ref, morph_ref, grad_ref, part_ref, energy_ref, act_ref, bands, sources):
    for k in range(sources):
        morph = morph_ref[k]
        energy = jnp.sum(morph * morph, axis=0, keepdims=True)
        push = None
        for b in range(bands):
            row = k * bands + b
            grad = grad_ref[b]
            part_ref[row : row + 1, :] = jnp.sum(morph * grad, axis=0, keepdims=True)
            energy_ref[row : row + 1, :] = energy
            term = sed_ref[row : row + 1, :] * grad
            push = term if push is None else push + term
        fresh = jnp.maximum(morph + step_size * push, 0.0)
        if act_ref is not None:
            fresh = fresh * act_ref[k * bands : k * bands + 1, :]
        morph_ref[k] = fresh
    inner = jnp.sum(part_ref[...], axis=1, keepdims=True)
    energy = jnp.sum(energy_ref[...], axis=1, keepdims=True)
    sed = jnp.maximum(sed_ref[...] + inner / (energy + 1.0), 0.0)
    if act_ref is not None:
        sed = sed * act_ref[...]
    sed_ref[...] = sed


def spread_rows(sed_ref, table, bands, sources, lanes):
    for k in range(sources):
        line = jnp.broadcast_to(table[k : k + 1, :], (bands, bands))
        row = lax.broadcasted_iota(I32, (bands, bands), 0)
        col = lax.broadcasted_iota(I32, (bands, bands), 1)
        value = jnp.sum(jnp.where(row == col, line, 0.0), axis=1, keepdims=True)
        sed_ref[k * bands : (k + 1) * bands, :] = jnp.broadcast_to(value, (bands, lanes))


def cuts(bands, side):
    steps = []
    for b in range(bands):
        if b in (0, bands - 1) and side // 2 % (QUAD * UNIT) == 0:
            steps += [(b, 0, side // 2), (b, side // 2, side // 2)]
        else:
            steps.append((b, 0, side))
    return steps


def sort_tables(homes_ref, upper, used, lanes):
    line = homes_ref[0]
    for source in range(1, GROUP):
        line = line + homes_ref[source]
    near = jnp.where(upper == 0, line[0:1, :], line[1:2, :])
    near = jnp.where(lax.broadcasted_iota(I32, (1, lanes), 1) < used, near, 2 * lanes)
    across = jnp.broadcast_to(near, (lanes, lanes))
    sub = lax.broadcasted_iota(I32, (lanes, lanes), 0)
    lane = lax.broadcasted_iota(I32, (lanes, lanes), 1)
    down = jnp.sum(jnp.where(sub == lane, across, 0), axis=1, keepdims=True)
    key_across = across * lanes + lane
    key_down = down * lanes + sub
    place = jnp.sum(jnp.where(key_across < key_down, 1, 0), axis=1, keepdims=True)
    order = jnp.sum(jnp.where(place == lane, sub, 0), axis=0, keepdims=True)
    sorted_home = jnp.sum(jnp.where(place == lane, down, 0), axis=0, keepdims=True)
    before = jnp.sum(jnp.where(place + 1 == lane, down, 0), axis=0, keepdims=True)
    keep = jnp.where(sorted_home == before, 1, 0)
    upto = jnp.sum(jnp.where(down <= lane, 1, 0), axis=0, keepdims=True)
    same = jnp.sum(jnp.where(down == lane, 1, 0), axis=0, keepdims=True)
    last = jnp.maximum(upto - 1, 0)
    some = jnp.where(same > 0, 1, 0)
    rows = [order, keep, last, some]
    for half in range(GROUP // QUAD):
        rows.append(line[half : half + 1, :])
    which = lax.broadcasted_iota(I32, (8, lanes), 0)
    result = jnp.zeros((8, lanes), I32)
    for index, row in enumerate(rows):
        result = jnp.where(which == index, row, result)
    return result


def core_kernel(
    count,
    bands,
    sources,
    owned,
    piece_count,
    blend_ref,
    home_of_ref,
    counts_ref,
    pieces_ref,
    labels_ref,
    spectra_ref,
    psf_ref,
    corners_ref,
    giant_ref,
    giant_labels_ref,
    giant_spectra_ref,
    out_morph,
    out_sed,
    out_tile,
    out_giant,
    homes_ref,
    table_vmem,
    table_ref,
    running,
    aside,
    pair_buf,
    summed,
    piece_bufs,
    arrived,
    morph_ref,
    sed_ref,
    act_ref,
    adj_ref,
    grad_ref,
    part_ref,
    energy_ref,
    gram,
    psf_t,
    sed_table,
    sed_all,
    held,
    picked,
    landed,
    row_psf,
    col_psf,
    left_ref,
    band_total,
    strips,
    base_buf,
    chip_buf,
    chip_out,
    band_buf,
    mix_buf,
    adj_own,
    giant_sed,
    giant_grad,
    own_sem,
    table_sem,
    home_send,
    home_recv,
    piece_send,
    piece_recv,
    pair_send,
    pair_recv,
    in_send,
    in_recv,
    back_send,
    back_recv,
    sed_send,
    sed_recv,
    half_send,
    half_recv,
    last_send,
    last_recv,
    strip_send,
    strip_recv,
    base_send,
    base_recv,
    chip_send,
    chip_recv,
    band_send,
    band_recv,
    grad_send,
    grad_recv,
    relay_send,
    relay_recv,
):
    me = lax.axis_index("tiles")
    rank = lax.rem(me, GROUP)
    base = me - rank
    mine = me // GROUP
    side = labels_ref.shape[1]
    lanes = side
    strip = side // GROUP
    plan = cuts(bands, side)
    units = [rows // QUAD // UNIT for _, _, rows in plan]
    quads = count // QUAD
    near_blends = QUAD * owned
    table = bands * sources
    per_chunk = piece_count // CHUNKS
    barrier_all(me, count)

    upper = rank // QUAD
    lower = lax.rem(rank, QUAD)
    core = lax.rem(rank, 2)
    chip = rank // 2
    partner_core = base + rank + 1 - 2 * core
    half_bands = bands // 2

    def keeper(i):
        return jnp.where(core == 0, KEEP_CHIP[0][i], KEEP_CHIP[1][i])

    keeps = chip < 0
    own_index = 0
    for i in range(half_bands):
        keeps = jnp.logical_or(keeps, keeper(i) == chip)
        own_index = jnp.where(keeper(i) == chip, i, own_index)
    own_band = 2 * own_index + core

    def home_copy(k):
        other = lax.rem(rank + k, GROUP)
        return remote(
            homes_ref.at[rank], homes_ref.at[rank], home_send.at[k - 1], home_recv.at[k - 1],
            base + other,
        )

    quad = me // QUAD
    pair = quad // 2
    parity = lax.rem(quad, 2)

    def piece_slot(c):
        return piece_bufs[c].at[pl.ds(lower * piece_count, piece_count)]

    def piece_source(c, other):
        band, first, _ = plan[c]
        return pieces_ref.at[:, band, pl.ds(first // UNIT + other * units[c], units[c])]

    def piece_copy(c, k):
        other = lax.rem(lower + k, QUAD)
        return remote(
            piece_source(c, other), piece_slot(c), piece_send.at[c, k - 1],
            piece_recv.at[c, k - 1], quad * QUAD + other,
        )

    def own_copy(c):
        return pltpu.make_async_copy(piece_source(c, lower), piece_slot(c), own_sem.at[c])

    def pair_copy(b):
        partner = (quad + 1 - 2 * parity) * QUAD + lower
        return remote(aside[b], pair_buf[b], pair_send.at[b], pair_recv.at[b], partner)

    def incoming(b, k):
        to_pair = lax.rem(pair + k // QUAD, quads // 2)
        to_lower = lax.rem(lower + k % QUAD, QUAD)
        return remote(
            summed[b].at[to_pair, pl.ds(to_lower * owned, owned)],
            arrived[b].at[pair, lower],
            in_send.at[b, k - 1],
            in_recv.at[b, k - 1],
            (2 * to_pair + parity) * QUAD + to_lower,
        )

    owners = quads // 2 * QUAD

    def outgoing(h, n, k):
        peer = lax.rem(me + k, count)
        return remote(
            out_morph.at[n, lax.rem(peer, GROUP), h],
            held[h].at[me * owned + n],
            back_send.at[h, n, k - 1],
            back_recv.at[h, n, k - 1],
            peer,
        )

    def sed_copy(k):
        return remote(
            sed_all.at[me], sed_all.at[me], sed_send.at[k - 1], sed_recv.at[k - 1],
            lax.rem(me + k, count),
        )

    def half_copy(k):
        other = lax.rem(rank + k, GROUP)
        return remote(
            picked.at[0, other],
            landed.at[:, :, rank, 0],
            half_send.at[k - 1],
            half_recv.at[k - 1],
            base + other,
        )

    def last_copy(chunk, k):
        other = lax.rem(rank + k, GROUP)
        return remote(
            picked.at[1, other, chunk],
            landed.at[chunk, :, rank, 1],
            last_send.at[chunk, k - 1],
            last_recv.at[chunk, k - 1],
            base + other,
        )

    def strip_copy(k):
        other = lax.rem(rank + k, GROUP)
        return remote(
            band_total.at[other], strips.at[rank], strip_send.at[k - 1], strip_recv.at[k - 1],
            base + other,
        )

    def base_copy(k):
        other = lax.rem(rank + k, GROUP)
        return remote(
            base_buf.at[rank], base_buf.at[rank], base_send.at[k - 1], base_recv.at[k - 1],
            base + other,
        )

    def chip_copy(slot, src):
        return remote(
            src.at[:, 1 - core], chip_buf.at[slot], chip_send.at[slot], chip_recv.at[slot],
            partner_core,
        )

    def band_copy(slot, i):
        return remote(
            chip_out.at[slot, i], band_buf.at[slot, chip], band_send.at[slot, i],
            band_recv.at[slot, chip], base + 2 * keeper(i) + core,
        )

    def grad_copy(slot, k):
        other = lax.rem(chip + k, CHIPS)
        return remote(
            giant_grad.at[slot, core, own_index],
            giant_grad.at[slot, core, own_index],
            grad_send.at[slot, k - 1],
            grad_recv.at[slot, own_index],
            base + 2 * other + core,
        )

    def relay_copy(slot):
        return remote(
            giant_grad.at[slot, core], giant_grad.at[slot, core], relay_send.at[slot],
            relay_recv.at[slot], partner_core,
        )

    def chip_sum(slot, ref):
        chip_copy(slot, ref).wait_recv()
        for i in range(half_bands):
            value = ref[i, core].astype(F32) + chip_buf[slot, i].astype(F32)
            chip_out[slot, i] = value.astype(BF16)

            @pl.when(keeper(i) != chip)
            def _():
                band_copy(slot, i).start()

            @pl.when(keeper(i) == chip)
            def _():
                band_buf[slot, chip] = chip_out[slot, i]

    def sent_bands(slot, ref):
        chip_copy(slot, ref).wait_send()
        for i in range(half_bands):
            @pl.when(keeper(i) != chip)
            def _():
                band_copy(slot, i).wait_send()

    def kept_sum(slot):
        for k in range(1, CHIPS):
            source = lax.rem(chip + k, CHIPS)
            remote(
                band_buf.at[slot, source], band_buf.at[slot, source], band_send.at[slot, 0],
                band_recv.at[slot, source], base + 2 * source + core,
            ).wait_recv()
        total = band_buf[slot, 0].astype(F32)
        for source in range(1, CHIPS):
            total = total + band_buf[slot, source].astype(F32)
        return total.reshape(side, side).astype(BF16)

    def giant_open():
        for k in range(1, GROUP):
            strip_copy(k).wait_recv()
        mean = None
        for k in range(GROUP):
            source = lax.rem(rank + k, GROUP)
            part = band_total[rank] if k == 0 else strips[source]
            mean = part if mean is None else mean + part
        base_buf[rank] = jnp.maximum(mean / bands, 0.0)
        for k in range(1, GROUP):
            base_copy(k).start()

        chip_sum(ITERS, giant_ref)

    def giant_mix(slot):
        for b in range(bands):
            mix = mix_band(giant_sed, out_giant, b, bands, sources)
            mix_buf[slot, b // 2, b % 2] = mix.reshape(GROUP, strip, side)
        chip_copy(slot, mix_buf.at[slot]).start()

    def giant_chip(slot):
        chip_sum(slot, mix_buf.at[slot])

    def giant_start():
        for k in range(1, GROUP):
            base_copy(k).wait_recv()
        base_map = base_buf[...].reshape(side, side)
        for k in range(sources):
            out_giant[k] = jnp.where(giant_labels_ref[0] == k + 1, base_map, 0.0)
        spread_rows(giant_sed, giant_spectra_ref[0], bands, sources, lanes)
        giant_mix(0)

    def giant_keep(slot):
        @pl.when(keeps)
        def _():
            if slot == 0:
                total = kept_sum(ITERS)
                back = matmul(psf_t[own_band], total).astype(BF16)
                adj_own[...] = matmul(back, psf_ref[own_band])
            total = kept_sum(slot)
            gram_own = gram[own_band]
            grad = adj_own[...] - matmul(matmul(gram_own, total).astype(BF16), gram_own)
            giant_grad[slot, core, own_index] = grad.astype(BF16)
            for k in range(1, CHIPS):
                grad_copy(slot, k).start()

    def giant_relay(slot):
        for i in range(half_bands):
            @pl.when(keeper(i) != chip)
            def _():
                remote(
                    giant_grad.at[slot, core, i], giant_grad.at[slot, core, i],
                    grad_send.at[slot, 0], grad_recv.at[slot, i], base + 2 * keeper(i) + core,
                ).wait_recv()

        relay_copy(slot).start()

    def giant_update(slot):
        relay_copy(slot).wait_recv()
        for b in range(bands):
            grad_ref[b] = giant_grad[slot, b % 2, b // 2].astype(F32)
        update(giant_sed, out_giant, grad_ref, part_ref, energy_ref, None, bands, sources)
        if slot + 1 < ITERS:
            giant_mix(slot + 1)

    flow = [(0, 1, giant_open), (1, 0, giant_start), (1, 1, functools.partial(giant_chip, 0))]
    turn = 2
    for it in range(ITERS):
        flow.append((turn, 0, functools.partial(giant_keep, it)))
        flow.append((turn + 1, 0, functools.partial(giant_relay, it)))
        flow.append((turn + 1, 1, functools.partial(giant_update, it)))
        if it + 1 < ITERS:
            flow.append((turn + 2, 0, functools.partial(giant_chip, it + 1)))
        turn += 3

    def giant_turn(b, part):
        while flow and flow[0][:2] <= (b, part):
            flow.pop(0)[2]()

    def launch(b):
        for k in range(1, QUAD):
            piece_copy(b, k).start()
        own_copy(b).start()

    at = lax.broadcasted_iota(I32, (8, lanes), 1) - lower * piece_count
    at = jnp.where(lax.broadcasted_iota(I32, (8, lanes), 0) == upper, at, -1)
    line = jnp.zeros((8, lanes), I32)
    for index in range(piece_count):
        line = jnp.where(at == index, home_of_ref[blend_ref[index]], line)
    homes_ref[rank] = line
    for k in range(1, GROUP):
        home_copy(k).start()
    ahead = 2
    launch(0)
    chip_copy(ITERS, giant_ref).start()
    totals = giant_ref[0, 0].astype(F32)
    for b in range(1, bands):
        totals = totals + giant_ref[b // 2, b % 2].astype(F32)
    band_total[...] = totals
    for k in range(1, GROUP):
        strip_copy(k).start()
    for c in range(1, min(ahead, len(plan))):
        launch(c)

    for b in range(bands):
        psf = psf_ref[b]
        gram[b] = t_matmul(psf, psf).astype(BF16)
        psf_t[b] = jnp.transpose(psf.astype(F32)).astype(BF16)
    for k in range(1, GROUP):
        home_copy(k).wait_recv()
    table_vmem[...] = sort_tables(homes_ref, upper, QUAD * piece_count, lanes)
    to_scalar = pltpu.make_async_copy(table_vmem, table_ref, table_sem)
    to_scalar.start()
    to_scalar.wait()

    def prepare(index, carry):
        spot = lax.broadcasted_iota(I32, corners_ref.shape, 1) == index
        spot = jnp.sum(jnp.where(spot, corners_ref[...], 0), axis=1, keepdims=True)
        row_at, col_at = spot[0:1, :], spot[1:2, :]
        rows = lax.broadcasted_iota(I32, (TILE, side), 0)
        inner = lax.broadcasted_iota(I32, (TILE, side), 1)
        row_hot = jnp.where(rows == inner + row_at, 1.0, 0.0).astype(BF16)
        cols = lax.broadcasted_iota(I32, (side, TILE), 1)
        inner_c = lax.broadcasted_iota(I32, (side, TILE), 0)
        col_hot = jnp.where(cols == inner_c + col_at, 1.0, 0.0).astype(BF16)
        for b in range(bands):
            row_psf[index, b] = matmul(row_hot, psf_ref[b]).astype(BF16)
            col_psf[b, index] = matmul(psf_t[b], col_hot).astype(BF16)
        return carry

    sed_table[...] = jnp.zeros_like(sed_table)

    def combine(c):
        pair_copy(c).wait_recv()
        for group in range(quads // 2):
            first = (2 * group + parity) * near_blends

            def join(index, carry, group=group, first=first):
                some = table_ref[3, first + index].astype(F32)
                mine_part = running[c % 2, table_ref[2, first + index], : units[c]] * some
                summed[c][group, index] = (
                    mine_part + pair_buf[c][group, index].astype(F32)
                ).astype(BF16)
                return carry

            lax.fori_loop(0, near_blends, join, 0, unroll=4)
        for k in range(1, owners):
            incoming(c, k).start()
        arrived[c][pair, lower] = summed[c][pair, pl.ds(lower * owned, owned)]

    for c in range(len(plan)):
        for k in range(1, QUAD):
            piece_copy(c, k).wait_recv()
        own_copy(c).wait()
        band_pieces = piece_bufs[c]

        def add(index, total, band_pieces=band_pieces, c=c):
            keep = table_ref[1, index].astype(F32)
            total = total * keep + band_pieces[table_ref[0, index]].astype(F32)
            running[c % 2, index, : units[c]] = total
            return total

        lax.fori_loop(0, QUAD * piece_count, add, jnp.zeros((units[c], UNIT, lanes), F32), unroll=8)
        for group in range(quads // 2):
            first = (2 * group + 1 - parity) * near_blends

            def put(index, carry, c=c, group=group, first=first):
                some = table_ref[3, first + index].astype(F32)
                aside[c][group, index] = (
                    running[c % 2, table_ref[2, first + index], : units[c]] * some
                ).astype(BF16)
                return carry

            lax.fori_loop(0, near_blends, put, 0, unroll=4)
        pair_copy(c).start()
        if c + ahead < len(plan):
            launch(c + ahead)
        giant_turn(c, 0)
        if c > 0:
            combine(c - 1)
        giant_turn(c, 1)
    combine(len(plan) - 1)
    beside = {}
    while len(flow) > 2 and len(beside) < owned:
        beside[len(beside)] = flow.pop(0)[2]

    for c in range(len(plan)):
        for k in range(1, owners):
            incoming(c, k).wait_recv()

    def blend(n, carry):
        source_of_row = lax.broadcasted_iota(I32, (table, lanes), 0) // bands
        act_ref[...] = jnp.where(source_of_row < counts_ref[n], 1.0, 0.0)
        spread_rows(sed_ref, spectra_ref[n], bands, sources, lanes)
        sed_ref[...] = sed_ref[...] * act_ref[...]
        for b in range(bands):
            for c, (band, first, rows) in enumerate(plan):
                if band == b:
                    total = arrived[c][0, :, n].astype(F32)
                    for g in range(1, quads // 2):
                        total = total + arrived[c][g, :, n].astype(F32)
                    grad_ref[b, first : first + rows, :] = total.reshape(rows, side)
        mean = grad_ref[0]
        for b in range(1, bands):
            mean = mean + grad_ref[b]
        base_map = jnp.maximum(mean / bands, 0.0)
        for k in range(sources):
            morph_ref[k] = (
                jnp.where(labels_ref[n] == k + 1, base_map, 0.0)
                * act_ref[k * bands : k * bands + 1, :]
            )
        for b in range(bands):
            back = matmul(psf_t[b], grad_ref[b].astype(BF16)).astype(BF16)
            adj_ref[b] = matmul(back, psf_ref[b])

        def iteration(it, carry):
            for b in range(bands):
                mix = mix_band(sed_ref, morph_ref, b, bands, sources)
                grad_ref[b] = adj_ref[b] - matmul(matmul(gram[b], mix).astype(BF16), gram[b])
            update(sed_ref, morph_ref, grad_ref, part_ref, energy_ref, act_ref, bands, sources)
            return carry

        lax.fori_loop(0, ITERS, iteration, 0)
        out_morph[n] = morph_ref[...].astype(BF16).reshape(out_morph.shape[1:])
        for k in range(1, count):
            outgoing(0, n, k).start()
        for h in range(2):
            held[h][me * owned + n] = out_morph[n, rank, h]
        diag = lax.broadcasted_iota(I32, (table, lanes), 0) == lax.broadcasted_iota(
            I32, (table, lanes), 1
        )
        line = jnp.sum(jnp.where(diag, sed_ref[...], 0.0), axis=0, keepdims=True)
        here = lax.broadcasted_iota(I32, sed_table.shape, 0) == n
        sed_table[...] = jnp.where(here, line, sed_table[...])

        for index, step in beside.items():
            pl.when(n == index)(step)
        return carry

    lax.fori_loop(0, owned, blend, 0)

    def second(n, carry):
        for k in range(1, count):
            outgoing(1, n, k).start()
        return carry

    lax.fori_loop(0, owned, second, 0)
    sed_all[me] = sed_table[...].astype(BF16)
    for k in range(1, count):
        sed_copy(k).start()
    out_sed[...] = sed_table[...]
    lax.fori_loop(0, piece_count, prepare, 0)

    def settle(h):
        def one(n, carry):
            for k in range(1, count):
                outgoing(h, n, k).wait_recv()
            return carry

        lax.fori_loop(0, owned, one, 0)

    def pick(h, k, chunks):
        other = lax.rem(rank + k, GROUP)

        def one(index, carry):
            for chunk in chunks:
                found = held[h][
                    table_ref[
                        4 + other // QUAD,
                        lax.rem(other, QUAD) * piece_count + chunk * per_chunk + index,
                    ]
                ]
                if k < GROUP:
                    picked[h, other, chunk, index] = found
                else:
                    landed[chunk, index, rank, h] = found
            return carry

        lax.fori_loop(0, per_chunk, one, 0)

    settle(0)
    for k in range(1, GROUP + 1):
        pick(0, k, range(CHUNKS))
        if k < GROUP:
            half_copy(k).start()
    while len(flow) > 1:
        flow.pop(0)[2]()
    settle(1)
    for chunk in range(CHUNKS):
        for k in range(1, GROUP + 1):
            pick(1, k, [chunk])
            if k < GROUP:
                last_copy(chunk, k).start()

    while flow:
        flow.pop(0)[2]()
    for k in range(1, count):
        sed_copy(k).wait_recv()
    out_tile[...] = jnp.zeros_like(out_tile)

    for k in range(1, GROUP):
        half_copy(k).wait_recv()

    def finish(chunk, carry):
        for k in range(1, GROUP):
            last_copy(chunk, k).wait_recv()
        for index in range(per_chunk):
            piece = chunk * per_chunk + index
            home = table_ref[4 + upper, lower * piece_count + piece]
            owner = lax.div(home, owned)
            place = home - owner * owned
            rows = sed_all[owner].astype(F32)
            here = lax.broadcasted_iota(I32, rows.shape, 0) == place
            line = jnp.sum(jnp.where(here, rows, 0.0), axis=0, keepdims=True)
            diag = lax.broadcasted_iota(I32, (table, lanes), 0) == lax.broadcasted_iota(
                I32, (table, lanes), 1
            )
            column = jnp.sum(jnp.where(diag, line, 0.0), axis=1, keepdims=True)
            sed_ref[...] = jnp.broadcast_to(column, (table, lanes))
            morph_ref[...] = landed[chunk, index].astype(F32).reshape(sources, side, side)
            for b in range(bands):
                mix = mix_band(sed_ref, morph_ref, b, bands, sources)
                left_ref[b, :, index * side : (index + 1) * side] = matmul(
                    row_psf[piece, b], mix
                ).astype(BF16)
        for b in range(bands):
            right = col_psf[b, pl.ds(chunk * per_chunk, per_chunk)].reshape(
                per_chunk * side, TILE
            )
            out_tile[b] = out_tile[b] + matmul(left_ref[b], right)
        return carry

    lax.fori_loop(0, CHUNKS, finish, 0)

    def drain(n, carry):
        for h in range(2):
            for k in range(1, count):
                outgoing(h, n, k).wait_send()
        return carry

    lax.fori_loop(0, owned, drain, 0)
    for c in range(len(plan)):
        for k in range(1, QUAD):
            piece_copy(c, k).wait_send()
        pair_copy(c).wait_send()
        for k in range(1, owners):
            incoming(c, k).wait_send()
    for k in range(1, GROUP):
        home_copy(k).wait_send()
    for k in range(1, count):
        sed_copy(k).wait_send()
    for k in range(1, GROUP):
        half_copy(k).wait_send()
        for chunk in range(CHUNKS):
            last_copy(chunk, k).wait_send()
    for k in range(1, GROUP):
        strip_copy(k).wait_send()
        base_copy(k).wait_send()
    sent_bands(ITERS, giant_ref)
    for it in range(ITERS):
        sent_bands(it, mix_buf.at[it])
        relay_copy(it).wait_send()

        @pl.when(keeps)
        def _():
            for k in range(1, CHIPS):
                grad_copy(it, k).wait_send()


def deliver_kernel(
    bands,
    morph_ref,
    sed_ref,
    tile_ref,
    giant_ref,
    out_morph,
    out_sed,
    out_tile,
    out_giant,
    morph_buf,
    tile_buf,
    giant_buf,
    morph_sem,
    tile_sem,
    giant_sem,
):
    loads, stores = [], []
    for source, buf, target, sem in (
        (tile_ref, tile_buf, out_tile, tile_sem),
        (morph_ref, morph_buf, out_morph, morph_sem),
        (giant_ref, giant_buf, out_giant, giant_sem),
    ):
        for index in range(source.shape[0]):
            loads.append(
                pltpu.make_async_copy(source.at[index], buf.at[index], sem.at[0, index])
            )
            stores.append(
                pltpu.make_async_copy(buf.at[index], target.at[index], sem.at[1, index])
            )
    for load in loads:
        load.start()
    owned, sources, _ = out_sed.shape
    for k in range(sources):
        out_sed[:, k, :] = sed_ref[:owned, k * bands : (k + 1) * bands].astype(BF16)
    for load, store in zip(loads, stores):
        load.wait()
        store.start()
    for store in stores:
        store.wait()


def on_device(
    pieces,
    piece_blend,
    corners,
    blend_home,
    source_count,
    footprint,
    spectra,
    giant_pieces,
    giant_footprint,
    giant_spectra,
    psf_matrix,
):
    count = lax.axis_size("tiles")
    piece_count, bands, side, _ = pieces.shape
    owned = footprint.shape[0]
    blend_count = blend_home.shape[0]
    sources = spectra.shape[1]
    back_rows = sources * side // GROUP // 2
    lanes = side
    table = sources * bands
    strip = side // GROUP
    per_chunk = piece_count // CHUNKS
    plan = cuts(bands, side)
    units = [cut // QUAD // UNIT for _, _, cut in plan]
    pairs = count // QUAD // 2

    dma = pltpu.SemaphoreType.DMA
    whole_map = (GROUP, strip, side)
    final_morph, sed_rows, tile_model, giant_morph = pl.pallas_call(
        functools.partial(core_kernel, count, bands, sources, owned, piece_count),
        out_shape=(
            jax.ShapeDtypeStruct((owned, GROUP, 2, back_rows, lanes), BF16),
            jax.ShapeDtypeStruct((16, lanes), F32),
            jax.ShapeDtypeStruct((bands, TILE, TILE), F32),
            jax.ShapeDtypeStruct((sources, side, side), F32),
        ),
        in_specs=[SMEM, SMEM, SMEM, ANY] + [VMEM] * 7,
        out_specs=(VMEM,) * 4,
        scratch_shapes=[
            pltpu.VMEM((GROUP, 8, lanes), I32),
            pltpu.VMEM((8, lanes), I32),
            pltpu.SMEM((8, lanes), I32),
            pltpu.VMEM((2, QUAD * piece_count, max(units), UNIT, lanes), F32),
            [pltpu.VMEM((pairs, QUAD * owned, u, UNIT, lanes), BF16) for u in units],
            [pltpu.VMEM((pairs, QUAD * owned, u, UNIT, lanes), BF16) for u in units],
            [pltpu.VMEM((pairs, QUAD * owned, u, UNIT, lanes), BF16) for u in units],
            [pltpu.VMEM((QUAD * piece_count, u, UNIT, lanes), BF16) for u in units],
            [pltpu.VMEM((pairs, QUAD, owned, u, UNIT, lanes), BF16) for u in units],
            pltpu.VMEM((sources, side, side), F32),
            pltpu.VMEM((table, lanes), F32),
            pltpu.VMEM((table, lanes), F32),
            pltpu.VMEM((bands, side, side), F32),
            pltpu.VMEM((bands, side, side), F32),
            pltpu.VMEM((table, lanes), F32),
            pltpu.VMEM((table, lanes), F32),
            pltpu.VMEM((bands, side, side), BF16),
            pltpu.VMEM((bands, side, side), BF16),
            pltpu.VMEM((16, lanes), F32),
            pltpu.VMEM((count, 16, lanes), BF16),
            [pltpu.VMEM((blend_count, back_rows, lanes), BF16) for _ in range(2)],
            pltpu.VMEM((2, GROUP, CHUNKS, per_chunk, back_rows, lanes), BF16),
            pltpu.VMEM((CHUNKS, per_chunk, GROUP, 2, back_rows, lanes), BF16),
            pltpu.VMEM((piece_count, bands, TILE, side), BF16),
            pltpu.VMEM((bands, piece_count, side, TILE), BF16),
            pltpu.VMEM((bands, TILE, per_chunk * side), BF16),
            pltpu.VMEM(whole_map, F32),
            pltpu.VMEM(whole_map, F32),
            pltpu.VMEM(whole_map, F32),
            pltpu.VMEM((ITERS + 1, bands // 2) + whole_map, BF16),
            pltpu.VMEM((ITERS + 1, bands // 2) + whole_map, BF16),
            pltpu.VMEM((ITERS + 1, CHIPS) + whole_map, BF16),
            pltpu.VMEM((ITERS, bands // 2, 2) + whole_map, BF16),
            pltpu.VMEM((side, side), F32),
            pltpu.VMEM((table, lanes), F32),
            pltpu.VMEM((ITERS, 2, bands // 2, side, side), BF16),
            dma((len(plan),)),
            dma,
            dma((GROUP - 1,)),
            dma((GROUP - 1,)),
            dma((len(plan), QUAD - 1)),
            dma((len(plan), QUAD - 1)),
            dma((len(plan),)),
            dma((len(plan),)),
            dma((len(plan), pairs * QUAD - 1)),
            dma((len(plan), pairs * QUAD - 1)),
            dma((2, owned, count - 1)),
            dma((2, owned, count - 1)),
            dma((count - 1,)),
            dma((count - 1,)),
            dma((GROUP - 1,)),
            dma((GROUP - 1,)),
            dma((CHUNKS, GROUP - 1)),
            dma((CHUNKS, GROUP - 1)),
            dma((GROUP - 1,)),
            dma((GROUP - 1,)),
            dma((GROUP - 1,)),
            dma((GROUP - 1,)),
            dma((ITERS + 1,)),
            dma((ITERS + 1,)),
            dma((ITERS + 1, bands // 2)),
            dma((ITERS + 1, CHIPS)),
            dma((ITERS, CHIPS - 1)),
            dma((ITERS, bands // 2)),
            dma((ITERS,)),
            dma((ITERS,)),
        ],
        compiler_params=pltpu.CompilerParams(
            collective_id=0, has_side_effects=True, vmem_limit_bytes=56 << 20
        ),
        name="core",
    )(
        piece_blend,
        blend_home,
        source_count,
        pieces.reshape(piece_count, bands, side // UNIT, UNIT, side),
        footprint,
        spectra,
        psf_matrix,
        corners.T,
        giant_pieces.reshape(bands // 2, 2, GROUP, strip, side),
        giant_footprint,
        giant_spectra,
    )
    final_morph, final_sed, tile_model, giant_morph = pl.pallas_call(
        functools.partial(deliver_kernel, bands),
        out_shape=(
            jax.ShapeDtypeStruct((owned, sources, side, side), BF16),
            jax.ShapeDtypeStruct((owned, sources, bands), BF16),
            jax.ShapeDtypeStruct((bands, TILE, TILE), F32),
            jax.ShapeDtypeStruct((sources, side, side), F32),
        ),
        in_specs=[ANY, VMEM, ANY, ANY],
        out_specs=(ANY, VMEM, ANY, ANY),
        scratch_shapes=[
            pltpu.VMEM((owned, sources, side, side), BF16),
            pltpu.VMEM((bands, TILE, TILE), F32),
            pltpu.VMEM((sources, side, side), F32),
            dma((2, owned)),
            dma((2, bands)),
            dma((2, sources)),
        ],
        name="deliver",
    )(
        final_morph.reshape(owned, sources, side, side),
        sed_rows,
        tile_model,
        giant_morph,
    )
    return (final_morph, final_sed, tile_model[None], giant_morph[None])


def solution(mesh):
    in_specs = (
        P(("groups", "tiles"), None, None, None),
        P(("groups", "tiles")),
        P(("groups", "tiles"), None),
        P("groups"),
        P(("groups", "tiles")),
        P(("groups", "tiles"), None, None),
        P(("groups", "tiles"), None, None),
        P(("groups", "tiles"), None, None, None),
        P(("groups", "tiles"), None, None),
        P(("groups", "tiles"), None, None),
        P(),
    )
    out_specs = (
        P(("groups", "tiles"), None, None, None),
        P(("groups", "tiles"), None, None),
        P(("groups", "tiles"), None, None, None),
        P(("groups", "tiles"), None, None, None),
    )
    return jax.shard_map(
        on_device, mesh=mesh, in_specs=in_specs, out_specs=out_specs, check_vma=False
    )
```

```python
import functools

import jax
import jax.numpy as jnp
from jax import lax
from jax.experimental import pallas as pl
from jax.experimental.pallas import tpu as pltpu
from jax.sharding import PartitionSpec as P

TILE = 256
ITERS = 3
GROUP = 8
QUAD = 4
CHIPS = GROUP // 2
UNIT = 16
KEEP_CHIP = ((0, 3, 1, 2), (3, 0, 2, 1))
CHUNKS = 4
MESH = pl.DeviceIdType.MESH
F32 = jnp.float32
BF16 = jnp.bfloat16
I32 = jnp.int32

step_size = 0.1

VMEM = pl.BlockSpec(memory_space=pltpu.VMEM)
SMEM = pl.BlockSpec(memory_space=pltpu.SMEM)
HBM = pl.BlockSpec(memory_space=pltpu.HBM)


def matmul(a, b):
    return jnp.dot(a, b, preferred_element_type=F32)


def t_matmul(a, b):
    return lax.dot_general(a, b, (((0,), (0,)), ((), ())), preferred_element_type=F32)


def barrier_all(me, count):
    barrier = pltpu.get_barrier_semaphore()
    for k in range(1, count):
        pl.semaphore_signal(
            barrier, inc=1, device_id={"tiles": lax.rem(me + k, count)}, device_id_type=MESH
        )
    pl.semaphore_wait(barrier, count - 1)


def remote(src, dst, send_sem, recv_sem, peer):
    return pltpu.make_async_remote_copy(
        src_ref=src,
        dst_ref=dst,
        send_sem=send_sem,
        recv_sem=recv_sem,
        device_id={"tiles": peer},
        device_id_type=MESH,
    )


def mix_band(sed_ref, maps, b, bands, sources):
    total = sed_ref[b : b + 1, :] * maps[0]
    for k in range(1, sources):
        row = k * bands + b
        total = total + sed_ref[row : row + 1, :] * maps[k]
    return total.astype(BF16)


def update(sed_ref, morph_ref, grad_ref, part_ref, energy_ref, act_ref, bands, sources):
    for k in range(sources):
        morph = morph_ref[k]
        energy = jnp.sum(morph * morph, axis=0, keepdims=True)
        push = None
        for b in range(bands):
            row = k * bands + b
            grad = grad_ref[b]
            part_ref[row : row + 1, :] = jnp.sum(morph * grad, axis=0, keepdims=True)
            energy_ref[row : row + 1, :] = energy
            term = sed_ref[row : row + 1, :] * grad
            push = term if push is None else push + term
        fresh = jnp.maximum(morph + step_size * push, 0.0)
        if act_ref is not None:
            fresh = fresh * act_ref[k * bands : k * bands + 1, :]
        morph_ref[k] = fresh
    inner = jnp.sum(part_ref[...], axis=1, keepdims=True)
    energy = jnp.sum(energy_ref[...], axis=1, keepdims=True)
    sed = jnp.maximum(sed_ref[...] + inner / (energy + 1.0), 0.0)
    if act_ref is not None:
        sed = sed * act_ref[...]
    sed_ref[...] = sed


def spread_rows(sed_ref, table, bands, sources, lanes):
    for k in range(sources):
        line = jnp.broadcast_to(table[k : k + 1, :], (bands, bands))
        row = lax.broadcasted_iota(I32, (bands, bands), 0)
        col = lax.broadcasted_iota(I32, (bands, bands), 1)
        value = jnp.sum(jnp.where(row == col, line, 0.0), axis=1, keepdims=True)
        sed_ref[k * bands : (k + 1) * bands, :] = jnp.broadcast_to(value, (bands, lanes))


def cuts(bands, side):
    steps = []
    for b in range(bands):
        if b in (0, bands - 1) and side // 2 % (QUAD * UNIT) == 0:
            steps += [(b, 0, side // 2), (b, side // 2, side // 2)]
        else:
            steps.append((b, 0, side))
    return steps


def sort_tables(homes_ref, upper, used, lanes):
    line = homes_ref[0]
    for source in range(1, GROUP):
        line = line + homes_ref[source]
    near = jnp.where(upper == 0, line[0:1, :], line[1:2, :])
    near = jnp.where(lax.broadcasted_iota(I32, (1, lanes), 1) < used, near, 2 * lanes)
    across = jnp.broadcast_to(near, (lanes, lanes))
    sub = lax.broadcasted_iota(I32, (lanes, lanes), 0)
    lane = lax.broadcasted_iota(I32, (lanes, lanes), 1)
    down = jnp.sum(jnp.where(sub == lane, across, 0), axis=1, keepdims=True)
    key_across = across * lanes + lane
    key_down = down * lanes + sub
    place = jnp.sum(jnp.where(key_across < key_down, 1, 0), axis=1, keepdims=True)
    order = jnp.sum(jnp.where(place == lane, sub, 0), axis=0, keepdims=True)
    sorted_home = jnp.sum(jnp.where(place == lane, down, 0), axis=0, keepdims=True)
    before = jnp.sum(jnp.where(place + 1 == lane, down, 0), axis=0, keepdims=True)
    keep = jnp.where(sorted_home == before, 1, 0)
    upto = jnp.sum(jnp.where(down <= lane, 1, 0), axis=0, keepdims=True)
    same = jnp.sum(jnp.where(down == lane, 1, 0), axis=0, keepdims=True)
    last = jnp.maximum(upto - 1, 0)
    some = jnp.where(same > 0, 1, 0)
    rows = [order, keep, last, some]
    for half in range(GROUP // QUAD):
        rows.append(line[half : half + 1, :])
    which = lax.broadcasted_iota(I32, (8, lanes), 0)
    result = jnp.zeros((8, lanes), I32)
    for index, row in enumerate(rows):
        result = jnp.where(which == index, row, result)
    return result


def core_kernel(
    count,
    bands,
    sources,
    owned,
    piece_count,
    blend_ref,
    home_of_ref,
    counts_ref,
    pieces_ref,
    labels_in,
    spectra_in,
    psf_in,
    corners_in,
    giant_in,
    giant_labels_in,
    giant_spectra_in,
    out_morph,
    out_sed,
    out_tile,
    out_giant,
    labels_ref,
    spectra_ref,
    psf_ref,
    corners_ref,
    giant_ref,
    giant_labels_ref,
    giant_spectra_ref,
    input_sem,
    homes_ref,
    table_vmem,
    table_ref,
    running,
    aside,
    pair_buf,
    summed,
    piece_bufs,
    arrived,
    morph_ref,
    sed_ref,
    act_ref,
    adj_ref,
    grad_ref,
    part_ref,
    energy_ref,
    gram,
    psf_t,
    sed_table,
    sed_all,
    held,
    picked,
    landed,
    row_psf,
    col_psf,
    left_ref,
    band_total,
    strips,
    base_buf,
    chip_buf,
    chip_out,
    band_buf,
    mix_buf,
    adj_own,
    giant_sed,
    giant_grad,
    own_sem,
    table_sem,
    home_send,
    home_recv,
    piece_send,
    piece_recv,
    pair_send,
    pair_recv,
    in_send,
    in_recv,
    back_send,
    back_recv,
    sed_send,
    sed_recv,
    half_send,
    half_recv,
    last_send,
    last_recv,
    strip_send,
    strip_recv,
    base_send,
    base_recv,
    chip_send,
    chip_recv,
    band_send,
    band_recv,
    grad_send,
    grad_recv,
    relay_send,
    relay_recv,
):
    me = lax.axis_index("tiles")
    rank = lax.rem(me, GROUP)
    base = me - rank
    mine = me // GROUP
    side = labels_ref.shape[1]
    lanes = side
    strip = side // GROUP
    plan = cuts(bands, side)
    units = [rows // QUAD // UNIT for _, _, rows in plan]
    quads = count // QUAD
    near_blends = QUAD * owned
    table = bands * sources
    per_chunk = piece_count // CHUNKS
    inputs = []
    for source, target in (
        (giant_in, giant_ref),
        (psf_in, psf_ref),
        (spectra_in, spectra_ref),
        (corners_in, corners_ref),
        (giant_labels_in, giant_labels_ref),
        (giant_spectra_in, giant_spectra_ref),
        (labels_in, labels_ref),
    ):
        inputs.append(pltpu.make_async_copy(source, target, input_sem.at[len(inputs)]))
        inputs[-1].start()
    upper = rank // QUAD
    lower = lax.rem(rank, QUAD)
    at = lax.broadcasted_iota(I32, (8, lanes), 1) - lower * piece_count
    at = jnp.where(lax.broadcasted_iota(I32, (8, lanes), 0) == upper, at, -1)
    line = jnp.zeros((8, lanes), I32)
    for index in range(piece_count):
        line = jnp.where(at == index, home_of_ref[blend_ref[index]], line)
    homes_ref[rank] = line
    barrier_all(me, count)

    core = lax.rem(rank, 2)
    chip = rank // 2
    partner_core = base + rank + 1 - 2 * core
    half_bands = bands // 2

    def keeper(i):
        return jnp.where(core == 0, KEEP_CHIP[0][i], KEEP_CHIP[1][i])

    keeps = chip < 0
    own_index = 0
    for i in range(half_bands):
        keeps = jnp.logical_or(keeps, keeper(i) == chip)
        own_index = jnp.where(keeper(i) == chip, i, own_index)
    own_band = 2 * own_index + core

    def home_copy(k):
        other = lax.rem(rank + k, GROUP)
        return remote(
            homes_ref.at[rank], homes_ref.at[rank], home_send.at[k - 1], home_recv.at[k - 1],
            base + other,
        )

    quad = me // QUAD
    pair = quad // 2
    parity = lax.rem(quad, 2)

    def piece_slot(c):
        return piece_bufs[c].at[pl.ds(lower * piece_count, piece_count)]

    def piece_source(c, other):
        band, first, _ = plan[c]
        return pieces_ref.at[:, band, pl.ds(first // UNIT + other * units[c], units[c])]

    def piece_copy(c, k):
        other = lax.rem(lower + k, QUAD)
        return remote(
            piece_source(c, other), piece_slot(c), piece_send.at[c, k - 1],
            piece_recv.at[c, k - 1], quad * QUAD + other,
        )

    def own_copy(c):
        return pltpu.make_async_copy(piece_source(c, lower), piece_slot(c), own_sem.at[c])

    def pair_copy(b):
        partner = (quad + 1 - 2 * parity) * QUAD + lower
        return remote(aside[b], pair_buf[b], pair_send.at[b], pair_recv.at[b], partner)

    def incoming(b, k):
        to_pair = lax.rem(pair + k // QUAD, quads // 2)
        to_lower = lax.rem(lower + k % QUAD, QUAD)
        return remote(
            summed[b].at[to_pair, pl.ds(to_lower * owned, owned)],
            arrived[b].at[pair, lower],
            in_send.at[b, k - 1],
            in_recv.at[b, k - 1],
            (2 * to_pair + parity) * QUAD + to_lower,
        )

    owners = quads // 2 * QUAD

    def outgoing(h, n, k):
        peer = lax.rem(me + k, count)
        return remote(
            out_morph.at[n, lax.rem(peer, GROUP), h],
            held[h].at[me * owned + n],
            back_send.at[h, n, k - 1],
            back_recv.at[h, n, k - 1],
            peer,
        )

    def sed_copy(k):
        return remote(
            sed_all.at[me], sed_all.at[me], sed_send.at[k - 1], sed_recv.at[k - 1],
            lax.rem(me + k, count),
        )

    def half_copy(k):
        other = lax.rem(rank + k, GROUP)
        return remote(
            picked.at[0, other],
            landed.at[:, :, rank, 0],
            half_send.at[k - 1],
            half_recv.at[k - 1],
            base + other,
        )

    def last_copy(chunk, k):
        other = lax.rem(rank + k, GROUP)
        return remote(
            picked.at[1, other, chunk],
            landed.at[chunk, :, rank, 1],
            last_send.at[chunk, k - 1],
            last_recv.at[chunk, k - 1],
            base + other,
        )

    def strip_copy(k):
        other = lax.rem(rank + k, GROUP)
        return remote(
            band_total.at[other], strips.at[rank], strip_send.at[k - 1], strip_recv.at[k - 1],
            base + other,
        )

    def base_copy(k):
        other = lax.rem(rank + k, GROUP)
        return remote(
            base_buf.at[rank], base_buf.at[rank], base_send.at[k - 1], base_recv.at[k - 1],
            base + other,
        )

    def chip_copy(slot, src):
        return remote(
            src.at[:, 1 - core], chip_buf.at[slot], chip_send.at[slot], chip_recv.at[slot],
            partner_core,
        )

    def band_copy(slot, i):
        return remote(
            chip_out.at[slot, i], band_buf.at[slot, chip], band_send.at[slot, i],
            band_recv.at[slot, chip], base + 2 * keeper(i) + core,
        )

    def grad_copy(slot, k):
        other = lax.rem(chip + k, CHIPS)
        return remote(
            giant_grad.at[slot, core, own_index],
            giant_grad.at[slot, core, own_index],
            grad_send.at[slot, k - 1],
            grad_recv.at[slot, own_index],
            base + 2 * other + core,
        )

    def relay_copy(slot):
        return remote(
            giant_grad.at[slot, core], giant_grad.at[slot, core], relay_send.at[slot],
            relay_recv.at[slot], partner_core,
        )

    def chip_sum(slot, ref):
        chip_copy(slot, ref).wait_recv()
        for i in range(half_bands):
            value = ref[i, core].astype(F32) + chip_buf[slot, i].astype(F32)
            chip_out[slot, i] = value.astype(BF16)

            @pl.when(keeper(i) != chip)
            def _():
                band_copy(slot, i).start()

            @pl.when(keeper(i) == chip)
            def _():
                band_buf[slot, chip] = chip_out[slot, i]

    def sent_bands(slot, ref):
        chip_copy(slot, ref).wait_send()
        for i in range(half_bands):
            @pl.when(keeper(i) != chip)
            def _():
                band_copy(slot, i).wait_send()

    def kept_sum(slot):
        for k in range(1, CHIPS):
            source = lax.rem(chip + k, CHIPS)
            remote(
                band_buf.at[slot, source], band_buf.at[slot, source], band_send.at[slot, 0],
                band_recv.at[slot, source], base + 2 * source + core,
            ).wait_recv()
        total = band_buf[slot, 0].astype(F32)
        for source in range(1, CHIPS):
            total = total + band_buf[slot, source].astype(F32)
        return total.reshape(side, side).astype(BF16)

    def giant_open():
        for k in range(1, GROUP):
            strip_copy(k).wait_recv()
        mean = None
        for k in range(GROUP):
            source = lax.rem(rank + k, GROUP)
            part = band_total[rank] if k == 0 else strips[source]
            mean = part if mean is None else mean + part
        base_buf[rank] = jnp.maximum(mean / bands, 0.0)
        for k in range(1, GROUP):
            base_copy(k).start()

        chip_sum(ITERS, giant_ref)

    def giant_mix(slot):
        for b in range(bands):
            mix = mix_band(giant_sed, out_giant, b, bands, sources)
            mix_buf[slot, b // 2, b % 2] = mix.reshape(GROUP, strip, side)
        chip_copy(slot, mix_buf.at[slot]).start()

    def giant_chip(slot):
        chip_sum(slot, mix_buf.at[slot])

    def giant_start():
        for k in range(1, GROUP):
            base_copy(k).wait_recv()
        base_map = base_buf[...].reshape(side, side)
        for k in range(sources):
            out_giant[k] = jnp.where(giant_labels_ref[0] == k + 1, base_map, 0.0)
        spread_rows(giant_sed, giant_spectra_ref[0], bands, sources, lanes)
        giant_mix(0)

    def giant_keep(slot):
        @pl.when(keeps)
        def _():
            if slot == 0:
                total = kept_sum(ITERS)
                back = matmul(psf_t[own_band], total).astype(BF16)
                adj_own[...] = matmul(back, psf_ref[own_band])
            total = kept_sum(slot)
            gram_own = gram[own_band]
            grad = adj_own[...] - matmul(matmul(gram_own, total).astype(BF16), gram_own)
            giant_grad[slot, core, own_index] = grad.astype(BF16)
            for k in range(1, CHIPS):
                grad_copy(slot, k).start()

    def giant_relay(slot):
        for i in range(half_bands):
            @pl.when(keeper(i) != chip)
            def _():
                remote(
                    giant_grad.at[slot, core, i], giant_grad.at[slot, core, i],
                    grad_send.at[slot, 0], grad_recv.at[slot, i], base + 2 * keeper(i) + core,
                ).wait_recv()

        relay_copy(slot).start()

    def giant_update(slot):
        relay_copy(slot).wait_recv()
        for b in range(bands):
            grad_ref[b] = giant_grad[slot, b % 2, b // 2].astype(F32)
        update(giant_sed, out_giant, grad_ref, part_ref, energy_ref, None, bands, sources)
        if slot + 1 < ITERS:
            giant_mix(slot + 1)

    flow = [(0, 1, giant_open), (1, 0, giant_start), (1, 1, functools.partial(giant_chip, 0))]
    turn = 2
    for it in range(ITERS):
        flow.append((turn, 0, functools.partial(giant_keep, it)))
        flow.append((turn + 1, 0, functools.partial(giant_relay, it)))
        flow.append((turn + 1, 1, functools.partial(giant_update, it)))
        if it + 1 < ITERS:
            flow.append((turn + 2, 0, functools.partial(giant_chip, it + 1)))
        turn += 3

    def giant_turn(b, part):
        while flow and flow[0][:2] <= (b, part):
            flow.pop(0)[2]()

    def launch(b):
        for k in range(1, QUAD):
            piece_copy(b, k).start()
        own_copy(b).start()

    for k in range(1, GROUP):
        home_copy(k).start()
    ahead = 1
    launch(0)
    for copy in inputs:
        copy.wait()
    chip_copy(ITERS, giant_ref).start()
    totals = giant_ref[0, 0].astype(F32)
    for b in range(1, bands):
        totals = totals + giant_ref[b // 2, b % 2].astype(F32)
    band_total[...] = totals
    for k in range(1, GROUP):
        strip_copy(k).start()
    for c in range(1, min(ahead, len(plan))):
        launch(c)

    for b in range(bands):
        psf = psf_ref[b]
        gram[b] = t_matmul(psf, psf).astype(BF16)
        psf_t[b] = jnp.transpose(psf.astype(F32)).astype(BF16)
    for k in range(1, GROUP):
        home_copy(k).wait_recv()
    table_vmem[...] = sort_tables(homes_ref, upper, QUAD * piece_count, lanes)
    to_scalar = pltpu.make_async_copy(table_vmem, table_ref, table_sem)
    to_scalar.start()
    to_scalar.wait()

    def prepare(index, carry):
        spot = lax.broadcasted_iota(I32, corners_ref.shape, 1) == index
        spot = jnp.sum(jnp.where(spot, corners_ref[...], 0), axis=1, keepdims=True)
        row_at, col_at = spot[0:1, :], spot[1:2, :]
        rows = lax.broadcasted_iota(I32, (TILE, side), 0)
        inner = lax.broadcasted_iota(I32, (TILE, side), 1)
        row_hot = jnp.where(rows == inner + row_at, 1.0, 0.0).astype(BF16)
        cols = lax.broadcasted_iota(I32, (side, TILE), 1)
        inner_c = lax.broadcasted_iota(I32, (side, TILE), 0)
        col_hot = jnp.where(cols == inner_c + col_at, 1.0, 0.0).astype(BF16)
        for b in range(bands):
            row_psf[index, b] = matmul(row_hot, psf_ref[b]).astype(BF16)
            col_psf[b, index] = matmul(psf_t[b], col_hot).astype(BF16)
        return carry

    sed_table[...] = jnp.zeros_like(sed_table)

    def combine(c):
        pair_copy(c).wait_recv()
        for group in range(quads // 2):
            first = (2 * group + parity) * near_blends

            def join(index, carry, group=group, first=first):
                some = table_ref[3, first + index].astype(F32)
                mine_part = running[c % 2, table_ref[2, first + index], : units[c]] * some
                summed[c][group, index] = (
                    mine_part + pair_buf[c][group, index].astype(F32)
                ).astype(BF16)
                return carry

            lax.fori_loop(0, near_blends, join, 0, unroll=4)
        for k in range(1, owners):
            incoming(c, k).start()
        arrived[c][pair, lower] = summed[c][pair, pl.ds(lower * owned, owned)]

    for c in range(len(plan)):
        for k in range(1, QUAD):
            piece_copy(c, k).wait_recv()
        own_copy(c).wait()
        band_pieces = piece_bufs[c]

        def add(index, total, band_pieces=band_pieces, c=c):
            keep = table_ref[1, index].astype(F32)
            total = total * keep + band_pieces[table_ref[0, index]].astype(F32)
            running[c % 2, index, : units[c]] = total
            return total

        lax.fori_loop(0, QUAD * piece_count, add, jnp.zeros((units[c], UNIT, lanes), F32), unroll=8)
        for group in range(quads // 2):
            first = (2 * group + 1 - parity) * near_blends

            def put(index, carry, c=c, group=group, first=first):
                some = table_ref[3, first + index].astype(F32)
                aside[c][group, index] = (
                    running[c % 2, table_ref[2, first + index], : units[c]] * some
                ).astype(BF16)
                return carry

            lax.fori_loop(0, near_blends, put, 0, unroll=4)
        pair_copy(c).start()
        if c + ahead < len(plan):
            launch(c + ahead)
        if c > 0:
            combine(c - 1)
        giant_turn(c, 1)
    combine(len(plan) - 1)
    beside = {}
    while len(flow) > 2 and len(beside) < owned:
        beside[len(beside)] = flow.pop(0)[2]

    for c in range(len(plan)):
        for k in range(1, owners):
            incoming(c, k).wait_recv()

    def blend(n, carry):
        source_of_row = lax.broadcasted_iota(I32, (table, lanes), 0) // bands
        act_ref[...] = jnp.where(source_of_row < counts_ref[n], 1.0, 0.0)
        spread_rows(sed_ref, spectra_ref[n], bands, sources, lanes)
        sed_ref[...] = sed_ref[...] * act_ref[...]
        for b in range(bands):
            for c, (band, first, rows) in enumerate(plan):
                if band == b:
                    total = arrived[c][0, :, n].astype(F32)
                    for g in range(1, quads // 2):
                        total = total + arrived[c][g, :, n].astype(F32)
                    grad_ref[b, first : first + rows, :] = total.reshape(rows, side)
        mean = grad_ref[0]
        for b in range(1, bands):
            mean = mean + grad_ref[b]
        base_map = jnp.maximum(mean / bands, 0.0)
        for k in range(sources):
            morph_ref[k] = (
                jnp.where(labels_ref[n] == k + 1, base_map, 0.0)
                * act_ref[k * bands : k * bands + 1, :]
            )
        for b in range(bands):
            back = matmul(psf_t[b], grad_ref[b].astype(BF16)).astype(BF16)
            adj_ref[b] = matmul(back, psf_ref[b])

        def iteration(it, carry):
            for b in range(bands):
                mix = mix_band(sed_ref, morph_ref, b, bands, sources)
                grad_ref[b] = adj_ref[b] - matmul(matmul(gram[b], mix).astype(BF16), gram[b])
            update(sed_ref, morph_ref, grad_ref, part_ref, energy_ref, act_ref, bands, sources)
            return carry

        lax.fori_loop(0, ITERS, iteration, 0)
        out_morph[n] = morph_ref[...].astype(BF16).reshape(out_morph.shape[1:])
        for k in range(1, count):
            outgoing(0, n, k).start()
        for h in range(2):
            held[h][me * owned + n] = out_morph[n, rank, h]
        diag = lax.broadcasted_iota(I32, (table, lanes), 0) == lax.broadcasted_iota(
            I32, (table, lanes), 1
        )
        line = jnp.sum(jnp.where(diag, sed_ref[...], 0.0), axis=0, keepdims=True)
        here = lax.broadcasted_iota(I32, sed_table.shape, 0) == n
        sed_table[...] = jnp.where(here, line, sed_table[...])

        for index, step in beside.items():
            pl.when(n == index)(step)
        return carry

    lax.fori_loop(0, owned, blend, 0)

    def second(n, carry):
        for k in range(1, count):
            outgoing(1, n, k).start()
        return carry

    lax.fori_loop(0, owned, second, 0)
    sed_all[me] = sed_table[...].astype(BF16)
    for k in range(1, count):
        sed_copy(k).start()
    out_sed[...] = sed_table[...]
    lax.fori_loop(0, piece_count, prepare, 0)

    def settle(h):
        def one(n, carry):
            for k in range(1, count):
                outgoing(h, n, k).wait_recv()
            return carry

        lax.fori_loop(0, owned, one, 0)

    def pick(h, k, chunks):
        other = lax.rem(rank + k, GROUP)

        def one(index, carry):
            for chunk in chunks:
                found = held[h][
                    table_ref[
                        4 + other // QUAD,
                        lax.rem(other, QUAD) * piece_count + chunk * per_chunk + index,
                    ]
                ]
                if k < GROUP:
                    picked[h, other, chunk, index] = found
                else:
                    landed[chunk, index, rank, h] = found
            return carry

        lax.fori_loop(0, per_chunk, one, 0)

    settle(0)
    for k in range(1, GROUP + 1):
        pick(0, k, range(CHUNKS))
        if k < GROUP:
            half_copy(k).start()
    while len(flow) > 1:
        flow.pop(0)[2]()
    settle(1)
    for chunk in range(CHUNKS):
        for k in range(1, GROUP + 1):
            pick(1, k, [chunk])
            if k < GROUP:
                last_copy(chunk, k).start()

    while flow:
        flow.pop(0)[2]()
    for k in range(1, count):
        sed_copy(k).wait_recv()
    out_tile[...] = jnp.zeros_like(out_tile)

    for k in range(1, GROUP):
        half_copy(k).wait_recv()

    def finish(chunk, carry):
        for k in range(1, GROUP):
            last_copy(chunk, k).wait_recv()
        for index in range(per_chunk):
            piece = chunk * per_chunk + index
            home = table_ref[4 + upper, lower * piece_count + piece]
            owner = lax.div(home, owned)
            place = home - owner * owned
            rows = sed_all[owner].astype(F32)
            here = lax.broadcasted_iota(I32, rows.shape, 0) == place
            line = jnp.sum(jnp.where(here, rows, 0.0), axis=0, keepdims=True)
            diag = lax.broadcasted_iota(I32, (table, lanes), 0) == lax.broadcasted_iota(
                I32, (table, lanes), 1
            )
            column = jnp.sum(jnp.where(diag, line, 0.0), axis=1, keepdims=True)
            sed_ref[...] = jnp.broadcast_to(column, (table, lanes))
            morph_ref[...] = landed[chunk, index].astype(F32).reshape(sources, side, side)
            for b in range(bands):
                mix = mix_band(sed_ref, morph_ref, b, bands, sources)
                left_ref[b, :, index * side : (index + 1) * side] = matmul(
                    row_psf[piece, b], mix
                ).astype(BF16)
        for b in range(bands):
            right = col_psf[b, pl.ds(chunk * per_chunk, per_chunk)].reshape(
                per_chunk * side, TILE
            )
            out_tile[b] = out_tile[b] + matmul(left_ref[b], right)
        return carry

    lax.fori_loop(0, CHUNKS, finish, 0)

    def drain(n, carry):
        for h in range(2):
            for k in range(1, count):
                outgoing(h, n, k).wait_send()
        return carry

    lax.fori_loop(0, owned, drain, 0)
    for c in range(len(plan)):
        for k in range(1, QUAD):
            piece_copy(c, k).wait_send()
        pair_copy(c).wait_send()
        for k in range(1, owners):
            incoming(c, k).wait_send()
    for k in range(1, GROUP):
        home_copy(k).wait_send()
    for k in range(1, count):
        sed_copy(k).wait_send()
    for k in range(1, GROUP):
        half_copy(k).wait_send()
        for chunk in range(CHUNKS):
            last_copy(chunk, k).wait_send()
    for k in range(1, GROUP):
        strip_copy(k).wait_send()
        base_copy(k).wait_send()
    sent_bands(ITERS, giant_ref)
    for it in range(ITERS):
        sent_bands(it, mix_buf.at[it])
        relay_copy(it).wait_send()

        @pl.when(keeps)
        def _():
            for k in range(1, CHIPS):
                grad_copy(it, k).wait_send()


def deliver_kernel(
    bands,
    morph_ref,
    sed_ref,
    tile_ref,
    giant_ref,
    out_morph,
    out_sed,
    out_tile,
    out_giant,
    morph_buf,
    tile_buf,
    giant_buf,
    morph_sem,
    tile_sem,
    giant_sem,
):
    loads, stores = [], []
    for source, buf, target, sem in (
        (tile_ref, tile_buf, out_tile, tile_sem),
        (morph_ref, morph_buf, out_morph, morph_sem),
        (giant_ref, giant_buf, out_giant, giant_sem),
    ):
        for index in range(source.shape[0]):
            loads.append(
                pltpu.make_async_copy(source.at[index], buf.at[index], sem.at[0, index])
            )
            stores.append(
                pltpu.make_async_copy(buf.at[index], target.at[index], sem.at[1, index])
            )
    for load in loads:
        load.start()
    owned, sources, _ = out_sed.shape
    for k in range(sources):
        out_sed[:, k, :] = sed_ref[:owned, k * bands : (k + 1) * bands].astype(BF16)
    for load, store in zip(loads, stores):
        load.wait()
        store.start()
    for store in stores:
        store.wait()


def on_device(
    pieces,
    piece_blend,
    corners,
    blend_home,
    source_count,
    footprint,
    spectra,
    giant_pieces,
    giant_footprint,
    giant_spectra,
    psf_matrix,
):
    count = lax.axis_size("tiles")
    piece_count, bands, side, _ = pieces.shape
    owned = footprint.shape[0]
    blend_count = blend_home.shape[0]
    sources = spectra.shape[1]
    back_rows = sources * side // GROUP // 2
    lanes = side
    table = sources * bands
    strip = side // GROUP
    per_chunk = piece_count // CHUNKS
    plan = cuts(bands, side)
    units = [cut // QUAD // UNIT for _, _, cut in plan]
    pairs = count // QUAD // 2

    dma = pltpu.SemaphoreType.DMA
    whole_map = (GROUP, strip, side)
    final_morph, sed_rows, tile_model, giant_morph = pl.pallas_call(
        functools.partial(core_kernel, count, bands, sources, owned, piece_count),
        out_shape=(
            jax.ShapeDtypeStruct((owned, GROUP, 2, back_rows, lanes), BF16),
            jax.ShapeDtypeStruct((16, lanes), F32),
            jax.ShapeDtypeStruct((bands, TILE, TILE), F32),
            jax.ShapeDtypeStruct((sources, side, side), F32),
        ),
        in_specs=[SMEM, SMEM, SMEM] + [HBM] * 8,
        out_specs=(VMEM,) * 4,
        scratch_shapes=[
            pltpu.VMEM(footprint.shape, I32),
            pltpu.VMEM(spectra.shape, F32),
            pltpu.VMEM(psf_matrix.shape, BF16),
            pltpu.VMEM((2, piece_count), I32),
            pltpu.VMEM((bands // 2, 2, GROUP, strip, side), BF16),
            pltpu.VMEM(giant_footprint.shape, I32),
            pltpu.VMEM(giant_spectra.shape, F32),
            dma((7,)),
            pltpu.VMEM((GROUP, 8, lanes), I32),
            pltpu.VMEM((8, lanes), I32),
            pltpu.SMEM((8, lanes), I32),
            pltpu.VMEM((2, QUAD * piece_count, max(units), UNIT, lanes), F32),
            [pltpu.VMEM((pairs, QUAD * owned, u, UNIT, lanes), BF16) for u in units],
            [pltpu.VMEM((pairs, QUAD * owned, u, UNIT, lanes), BF16) for u in units],
            [pltpu.VMEM((pairs, QUAD * owned, u, UNIT, lanes), BF16) for u in units],
            [pltpu.VMEM((QUAD * piece_count, u, UNIT, lanes), BF16) for u in units],
            [pltpu.VMEM((pairs, QUAD, owned, u, UNIT, lanes), BF16) for u in units],
            pltpu.VMEM((sources, side, side), F32),
            pltpu.VMEM((table, lanes), F32),
            pltpu.VMEM((table, lanes), F32),
            pltpu.VMEM((bands, side, side), F32),
            pltpu.VMEM((bands, side, side), F32),
            pltpu.VMEM((table, lanes), F32),
            pltpu.VMEM((table, lanes), F32),
            pltpu.VMEM((bands, side, side), BF16),
            pltpu.VMEM((bands, side, side), BF16),
            pltpu.VMEM((16, lanes), F32),
            pltpu.VMEM((count, 16, lanes), BF16),
            [pltpu.VMEM((blend_count, back_rows, lanes), BF16) for _ in range(2)],
            pltpu.VMEM((2, GROUP, CHUNKS, per_chunk, back_rows, lanes), BF16),
            pltpu.VMEM((CHUNKS, per_chunk, GROUP, 2, back_rows, lanes), BF16),
            pltpu.VMEM((piece_count, bands, TILE, side), BF16),
            pltpu.VMEM((bands, piece_count, side, TILE), BF16),
            pltpu.VMEM((bands, TILE, per_chunk * side), BF16),
            pltpu.VMEM(whole_map, F32),
            pltpu.VMEM(whole_map, F32),
            pltpu.VMEM(whole_map, F32),
            pltpu.VMEM((ITERS + 1, bands // 2) + whole_map, BF16),
            pltpu.VMEM((ITERS + 1, bands // 2) + whole_map, BF16),
            pltpu.VMEM((ITERS + 1, CHIPS) + whole_map, BF16),
            pltpu.VMEM((ITERS, bands // 2, 2) + whole_map, BF16),
            pltpu.VMEM((side, side), F32),
            pltpu.VMEM((table, lanes), F32),
            pltpu.VMEM((ITERS, 2, bands // 2, side, side), BF16),
            dma((len(plan),)),
            dma,
            dma((GROUP - 1,)),
            dma((GROUP - 1,)),
            dma((len(plan), QUAD - 1)),
            dma((len(plan), QUAD - 1)),
            dma((len(plan),)),
            dma((len(plan),)),
            dma((len(plan), pairs * QUAD - 1)),
            dma((len(plan), pairs * QUAD - 1)),
            dma((2, owned, count - 1)),
            dma((2, owned, count - 1)),
            dma((count - 1,)),
            dma((count - 1,)),
            dma((GROUP - 1,)),
            dma((GROUP - 1,)),
            dma((CHUNKS, GROUP - 1)),
            dma((CHUNKS, GROUP - 1)),
            dma((GROUP - 1,)),
            dma((GROUP - 1,)),
            dma((GROUP - 1,)),
            dma((GROUP - 1,)),
            dma((ITERS + 1,)),
            dma((ITERS + 1,)),
            dma((ITERS + 1, bands // 2)),
            dma((ITERS + 1, CHIPS)),
            dma((ITERS, CHIPS - 1)),
            dma((ITERS, bands // 2)),
            dma((ITERS,)),
            dma((ITERS,)),
        ],
        compiler_params=pltpu.CompilerParams(
            collective_id=0, has_side_effects=True, vmem_limit_bytes=56 << 20
        ),
        name="core",
    )(
        piece_blend,
        blend_home,
        source_count,
        pieces.reshape(piece_count, bands, side // UNIT, UNIT, side),
        footprint,
        spectra,
        psf_matrix,
        corners.T,
        giant_pieces.reshape(bands // 2, 2, GROUP, strip, side),
        giant_footprint,
        giant_spectra,
    )
    final_morph, final_sed, tile_model, giant_morph = pl.pallas_call(
        functools.partial(deliver_kernel, bands),
        out_shape=(
            jax.ShapeDtypeStruct((owned, sources, side, side), BF16),
            jax.ShapeDtypeStruct((owned, sources, bands), BF16),
            jax.ShapeDtypeStruct((bands, TILE, TILE), F32),
            jax.ShapeDtypeStruct((sources, side, side), F32),
        ),
        in_specs=[HBM, VMEM, HBM, HBM],
        out_specs=(HBM, VMEM, HBM, HBM),
        scratch_shapes=[
            pltpu.VMEM((owned, sources, side, side), BF16),
            pltpu.VMEM((bands, TILE, TILE), F32),
            pltpu.VMEM((sources, side, side), F32),
            dma((2, owned)),
            dma((2, bands)),
            dma((2, sources)),
        ],
        name="deliver",
    )(
        final_morph.reshape(owned, sources, side, side),
        sed_rows,
        tile_model,
        giant_morph,
    )
    return (final_morph, final_sed, tile_model[None], giant_morph[None])


def solution(mesh):
    in_specs = (
        P(("groups", "tiles"), None, None, None),
        P(("groups", "tiles")),
        P(("groups", "tiles"), None),
        P("groups"),
        P(("groups", "tiles")),
        P(("groups", "tiles"), None, None),
        P(("groups", "tiles"), None, None),
        P(("groups", "tiles"), None, None, None),
        P(("groups", "tiles"), None, None),
        P(("groups", "tiles"), None, None),
        P(),
    )
    out_specs = (
        P(("groups", "tiles"), None, None, None),
        P(("groups", "tiles"), None, None),
        P(("groups", "tiles"), None, None, None),
        P(("groups", "tiles"), None, None, None),
    )
    return jax.shard_map(
        on_device, mesh=mesh, in_specs=in_specs, out_specs=out_specs, check_vma=False
    )
```

```python
import functools

import jax
import jax.numpy as jnp
from jax import lax
from jax.experimental import pallas as pl
from jax.experimental.pallas import tpu as pltpu
from jax.sharding import PartitionSpec as P

TILE = 256
ITERS = 3
GROUP = 8
QUAD = 4
CHIPS = GROUP // 2
UNIT = 16
KEEP_CHIP = ((0, 3, 1, 2), (3, 0, 2, 1))
CHUNKS = 4
MESH = pl.DeviceIdType.MESH
F32 = jnp.float32
BF16 = jnp.bfloat16
I32 = jnp.int32

step_size = 0.1

VMEM = pl.BlockSpec(memory_space=pltpu.VMEM)
SMEM = pl.BlockSpec(memory_space=pltpu.SMEM)
HBM = pl.BlockSpec(memory_space=pltpu.HBM)


def matmul(a, b):
    return jnp.dot(a, b, preferred_element_type=F32)


def t_matmul(a, b):
    return lax.dot_general(a, b, (((0,), (0,)), ((), ())), preferred_element_type=F32)


def barrier_all(me, count):
    barrier = pltpu.get_barrier_semaphore()
    for k in range(1, count):
        pl.semaphore_signal(
            barrier, inc=1, device_id={"tiles": lax.rem(me + k, count)}, device_id_type=MESH
        )
    pl.semaphore_wait(barrier, count - 1)


def remote(src, dst, send_sem, recv_sem, peer):
    return pltpu.make_async_remote_copy(
        src_ref=src,
        dst_ref=dst,
        send_sem=send_sem,
        recv_sem=recv_sem,
        device_id={"tiles": peer},
        device_id_type=MESH,
    )


def mix_band(sed_ref, maps, b, bands, sources):
    total = sed_ref[b : b + 1, :] * maps[0]
    for k in range(1, sources):
        row = k * bands + b
        total = total + sed_ref[row : row + 1, :] * maps[k]
    return total.astype(BF16)


def update(sed_ref, morph_ref, grad_ref, part_ref, energy_ref, act_ref, bands, sources):
    for k in range(sources):
        morph = morph_ref[k]
        energy = jnp.sum(morph * morph, axis=0, keepdims=True)
        push = None
        for b in range(bands):
            row = k * bands + b
            grad = grad_ref[b]
            part_ref[row : row + 1, :] = jnp.sum(morph * grad, axis=0, keepdims=True)
            energy_ref[row : row + 1, :] = energy
            term = sed_ref[row : row + 1, :] * grad
            push = term if push is None else push + term
        fresh = jnp.maximum(morph + step_size * push, 0.0)
        if act_ref is not None:
            fresh = fresh * act_ref[k * bands : k * bands + 1, :]
        morph_ref[k] = fresh
    inner = jnp.sum(part_ref[...], axis=1, keepdims=True)
    energy = jnp.sum(energy_ref[...], axis=1, keepdims=True)
    sed = jnp.maximum(sed_ref[...] + inner / (energy + 1.0), 0.0)
    if act_ref is not None:
        sed = sed * act_ref[...]
    sed_ref[...] = sed


def spread_rows(sed_ref, table, bands, sources, lanes):
    for k in range(sources):
        line = jnp.broadcast_to(table[k : k + 1, :], (bands, bands))
        row = lax.broadcasted_iota(I32, (bands, bands), 0)
        col = lax.broadcasted_iota(I32, (bands, bands), 1)
        value = jnp.sum(jnp.where(row == col, line, 0.0), axis=1, keepdims=True)
        sed_ref[k * bands : (k + 1) * bands, :] = jnp.broadcast_to(value, (bands, lanes))


def cuts(bands, side):
    steps = []
    for b in range(bands):
        if b in (0, bands - 1) and side // 2 % (QUAD * UNIT) == 0:
            steps += [(b, 0, side // 2), (b, side // 2, side // 2)]
        else:
            steps.append((b, 0, side))
    return steps


def sort_tables(homes_ref, upper, used, lanes):
    line = homes_ref[0]
    for source in range(1, GROUP):
        line = line + homes_ref[source]
    near = jnp.where(upper == 0, line[0:1, :], line[1:2, :])
    near = jnp.where(lax.broadcasted_iota(I32, (1, lanes), 1) < used, near, 2 * lanes)
    across = jnp.broadcast_to(near, (lanes, lanes))
    sub = lax.broadcasted_iota(I32, (lanes, lanes), 0)
    lane = lax.broadcasted_iota(I32, (lanes, lanes), 1)
    down = jnp.sum(jnp.where(sub == lane, across, 0), axis=1, keepdims=True)
    key_across = across * lanes + lane
    key_down = down * lanes + sub
    place = jnp.sum(jnp.where(key_across < key_down, 1, 0), axis=1, keepdims=True)
    order = jnp.sum(jnp.where(place == lane, sub, 0), axis=0, keepdims=True)
    sorted_home = jnp.sum(jnp.where(place == lane, down, 0), axis=0, keepdims=True)
    before = jnp.sum(jnp.where(place + 1 == lane, down, 0), axis=0, keepdims=True)
    keep = jnp.where(sorted_home == before, 1, 0)
    upto = jnp.sum(jnp.where(down <= lane, 1, 0), axis=0, keepdims=True)
    same = jnp.sum(jnp.where(down == lane, 1, 0), axis=0, keepdims=True)
    last = jnp.maximum(upto - 1, 0)
    some = jnp.where(same > 0, 1, 0)
    rows = [order, keep, last, some]
    for half in range(GROUP // QUAD):
        rows.append(line[half : half + 1, :])
    which = lax.broadcasted_iota(I32, (8, lanes), 0)
    result = jnp.zeros((8, lanes), I32)
    for index, row in enumerate(rows):
        result = jnp.where(which == index, row, result)
    return result


def core_kernel(
    count,
    bands,
    sources,
    owned,
    piece_count,
    blend_ref,
    home_of_ref,
    counts_ref,
    pieces_ref,
    labels_in,
    spectra_in,
    psf_in,
    corners_in,
    giant_in,
    giant_labels_in,
    giant_spectra_in,
    out_morph,
    out_sed,
    out_tile,
    out_giant,
    labels_ref,
    spectra_ref,
    psf_ref,
    corners_ref,
    giant_ref,
    giant_labels_ref,
    giant_spectra_ref,
    input_sem,
    homes_ref,
    table_vmem,
    table_ref,
    running,
    aside,
    pair_buf,
    summed,
    piece_bufs,
    arrived,
    morph_ref,
    sed_ref,
    act_ref,
    adj_ref,
    grad_ref,
    part_ref,
    energy_ref,
    gram,
    psf_t,
    sed_table,
    sed_all,
    held,
    picked,
    landed,
    row_psf,
    col_psf,
    left_ref,
    band_total,
    strips,
    base_buf,
    chip_buf,
    chip_out,
    band_buf,
    mix_buf,
    adj_own,
    giant_sed,
    giant_grad,
    own_sem,
    table_sem,
    home_send,
    home_recv,
    piece_send,
    piece_recv,
    pair_send,
    pair_recv,
    in_send,
    in_recv,
    back_send,
    back_recv,
    sed_send,
    sed_recv,
    half_send,
    half_recv,
    last_send,
    last_recv,
    strip_send,
    strip_recv,
    base_send,
    base_recv,
    chip_send,
    chip_recv,
    band_send,
    band_recv,
    grad_send,
    grad_recv,
    relay_send,
    relay_recv,
):
    me = lax.axis_index("tiles")
    rank = lax.rem(me, GROUP)
    base = me - rank
    mine = me // GROUP
    side = labels_ref.shape[1]
    lanes = side
    strip = side // GROUP
    plan = cuts(bands, side)
    units = [rows // QUAD // UNIT for _, _, rows in plan]
    quads = count // QUAD
    near_blends = QUAD * owned
    table = bands * sources
    per_chunk = piece_count // CHUNKS
    inputs = []
    for source, target in (
        (giant_in, giant_ref),
        (psf_in, psf_ref),
        (spectra_in, spectra_ref),
        (corners_in, corners_ref),
        (giant_labels_in, giant_labels_ref),
        (giant_spectra_in, giant_spectra_ref),
        (labels_in, labels_ref),
    ):
        inputs.append(pltpu.make_async_copy(source, target, input_sem.at[len(inputs)]))
        inputs[-1].start()
    upper = rank // QUAD
    lower = lax.rem(rank, QUAD)
    at = lax.broadcasted_iota(I32, (8, lanes), 1) - lower * piece_count
    at = jnp.where(lax.broadcasted_iota(I32, (8, lanes), 0) == upper, at, -1)
    line = jnp.zeros((8, lanes), I32)
    for index in range(piece_count):
        line = jnp.where(at == index, home_of_ref[blend_ref[index]], line)
    homes_ref[rank] = line
    barrier_all(me, count)

    core = lax.rem(rank, 2)
    chip = rank // 2
    partner_core = base + rank + 1 - 2 * core
    half_bands = bands // 2

    def keeper(i):
        return jnp.where(core == 0, KEEP_CHIP[0][i], KEEP_CHIP[1][i])

    keeps = chip < 0
    own_index = 0
    for i in range(half_bands):
        keeps = jnp.logical_or(keeps, keeper(i) == chip)
        own_index = jnp.where(keeper(i) == chip, i, own_index)
    own_band = 2 * own_index + core

    def home_copy(k):
        other = lax.rem(rank + k, GROUP)
        return remote(
            homes_ref.at[rank], homes_ref.at[rank], home_send.at[k - 1], home_recv.at[k - 1],
            base + other,
        )

    quad = me // QUAD
    pair = quad // 2
    parity = lax.rem(quad, 2)

    def piece_slot(c):
        return piece_bufs[c].at[pl.ds(lower * piece_count, piece_count)]

    def piece_source(c, other):
        band, first, _ = plan[c]
        return pieces_ref.at[:, band, pl.ds(first // UNIT + other * units[c], units[c])]

    def piece_copy(c, k):
        other = lax.rem(lower + k, QUAD)
        return remote(
            piece_source(c, other), piece_slot(c), piece_send.at[c, k - 1],
            piece_recv.at[c, k - 1], quad * QUAD + other,
        )

    def own_copy(c):
        return pltpu.make_async_copy(piece_source(c, lower), piece_slot(c), own_sem.at[c])

    def pair_copy(b):
        partner = (quad + 1 - 2 * parity) * QUAD + lower
        return remote(aside[b], pair_buf[b], pair_send.at[b], pair_recv.at[b], partner)

    def incoming(b, k):
        to_pair = lax.rem(pair + k // QUAD, quads // 2)
        to_lower = lax.rem(lower + k % QUAD, QUAD)
        return remote(
            summed[b].at[to_pair, pl.ds(to_lower * owned, owned)],
            arrived[b].at[pair, lower],
            in_send.at[b, k - 1],
            in_recv.at[b, k - 1],
            (2 * to_pair + parity) * QUAD + to_lower,
        )

    owners = quads // 2 * QUAD

    def outgoing(h, n, k):
        peer = lax.rem(me + k, count)
        return remote(
            out_morph.at[n, lax.rem(peer, GROUP), h],
            held[h].at[me * owned + n],
            back_send.at[h, n, k - 1],
            back_recv.at[h, n, k - 1],
            peer,
        )

    def sed_copy(k):
        return remote(
            sed_all.at[me], sed_all.at[me], sed_send.at[k - 1], sed_recv.at[k - 1],
            lax.rem(me + k, count),
        )

    def half_copy(k):
        other = lax.rem(rank + k, GROUP)
        return remote(
            picked.at[0, other],
            landed.at[:, :, rank, 0],
            half_send.at[k - 1],
            half_recv.at[k - 1],
            base + other,
        )

    def last_copy(chunk, k):
        other = lax.rem(rank + k, GROUP)
        return remote(
            picked.at[1, other, chunk],
            landed.at[chunk, :, rank, 1],
            last_send.at[chunk, k - 1],
            last_recv.at[chunk, k - 1],
            base + other,
        )

    def strip_copy(k):
        other = lax.rem(rank + k, GROUP)
        return remote(
            band_total.at[other], strips.at[rank], strip_send.at[k - 1], strip_recv.at[k - 1],
            base + other,
        )

    def base_copy(k):
        other = lax.rem(rank + k, GROUP)
        return remote(
            base_buf.at[rank], base_buf.at[rank], base_send.at[k - 1], base_recv.at[k - 1],
            base + other,
        )

    def chip_copy(slot, src):
        return remote(
            src.at[:, 1 - core], chip_buf.at[slot], chip_send.at[slot], chip_recv.at[slot],
            partner_core,
        )

    def band_copy(slot, i):
        return remote(
            chip_out.at[slot, i], band_buf.at[slot, chip], band_send.at[slot, i],
            band_recv.at[slot, chip], base + 2 * keeper(i) + core,
        )

    def grad_copy(slot, k):
        other = lax.rem(chip + k, CHIPS)
        return remote(
            giant_grad.at[slot, core, own_index],
            giant_grad.at[slot, core, own_index],
            grad_send.at[slot, k - 1],
            grad_recv.at[slot, own_index],
            base + 2 * other + core,
        )

    def relay_copy(slot):
        return remote(
            giant_grad.at[slot, core], giant_grad.at[slot, core], relay_send.at[slot],
            relay_recv.at[slot], partner_core,
        )

    def chip_sum(slot, ref):
        chip_copy(slot, ref).wait_recv()
        for i in range(half_bands):
            value = ref[i, core].astype(F32) + chip_buf[slot, i].astype(F32)
            chip_out[slot, i] = value.astype(BF16)

            @pl.when(keeper(i) != chip)
            def _():
                band_copy(slot, i).start()

            @pl.when(keeper(i) == chip)
            def _():
                band_buf[slot, chip] = chip_out[slot, i]

    def sent_bands(slot, ref):
        chip_copy(slot, ref).wait_send()
        for i in range(half_bands):
            @pl.when(keeper(i) != chip)
            def _():
                band_copy(slot, i).wait_send()

    def kept_sum(slot):
        for k in range(1, CHIPS):
            source = lax.rem(chip + k, CHIPS)
            remote(
                band_buf.at[slot, source], band_buf.at[slot, source], band_send.at[slot, 0],
                band_recv.at[slot, source], base + 2 * source + core,
            ).wait_recv()
        total = band_buf[slot, 0].astype(F32)
        for source in range(1, CHIPS):
            total = total + band_buf[slot, source].astype(F32)
        return total.reshape(side, side).astype(BF16)

    def giant_open():
        for k in range(1, GROUP):
            strip_copy(k).wait_recv()
        mean = None
        for k in range(GROUP):
            source = lax.rem(rank + k, GROUP)
            part = band_total[rank] if k == 0 else strips[source]
            mean = part if mean is None else mean + part
        base_buf[rank] = jnp.maximum(mean / bands, 0.0)
        for k in range(1, GROUP):
            base_copy(k).start()

        chip_sum(ITERS, giant_ref)

    def giant_mix(slot):
        for b in range(bands):
            mix = mix_band(giant_sed, out_giant, b, bands, sources)
            mix_buf[slot, b // 2, b % 2] = mix.reshape(GROUP, strip, side)
        chip_copy(slot, mix_buf.at[slot]).start()

    def giant_chip(slot):
        chip_sum(slot, mix_buf.at[slot])

    def giant_start():
        for k in range(1, GROUP):
            base_copy(k).wait_recv()
        base_map = base_buf[...].reshape(side, side)
        for k in range(sources):
            out_giant[k] = jnp.where(giant_labels_ref[0] == k + 1, base_map, 0.0)
        spread_rows(giant_sed, giant_spectra_ref[0], bands, sources, lanes)
        giant_mix(0)

    def giant_keep(slot):
        @pl.when(keeps)
        def _():
            if slot == 0:
                total = kept_sum(ITERS)
                back = matmul(psf_t[own_band], total).astype(BF16)
                adj_own[...] = matmul(back, psf_ref[own_band])
            total = kept_sum(slot)
            gram_own = gram[own_band]
            grad = adj_own[...] - matmul(matmul(gram_own, total).astype(BF16), gram_own)
            giant_grad[slot, core, own_index] = grad.astype(BF16)
            for k in range(1, CHIPS):
                grad_copy(slot, k).start()

    def giant_relay(slot):
        for i in range(half_bands):
            @pl.when(keeper(i) != chip)
            def _():
                remote(
                    giant_grad.at[slot, core, i], giant_grad.at[slot, core, i],
                    grad_send.at[slot, 0], grad_recv.at[slot, i], base + 2 * keeper(i) + core,
                ).wait_recv()

        relay_copy(slot).start()

    def giant_update(slot):
        relay_copy(slot).wait_recv()
        for b in range(bands):
            grad_ref[b] = giant_grad[slot, b % 2, b // 2].astype(F32)
        update(giant_sed, out_giant, grad_ref, part_ref, energy_ref, None, bands, sources)
        if slot + 1 < ITERS:
            giant_mix(slot + 1)

    flow = [(0, 1, giant_open), (1, 0, giant_start), (1, 1, functools.partial(giant_chip, 0))]
    turn = 2
    for it in range(ITERS):
        flow.append((turn, 0, functools.partial(giant_keep, it)))
        flow.append((turn + 1, 0, functools.partial(giant_relay, it)))
        flow.append((turn + 1, 1, functools.partial(giant_update, it)))
        if it + 1 < ITERS:
            flow.append((turn + 2, 0, functools.partial(giant_chip, it + 1)))
        turn += 3

    def giant_turn(b, part):
        while flow and flow[0][:2] <= (b, part):
            flow.pop(0)[2]()

    def launch(b):
        for k in range(1, QUAD):
            piece_copy(b, k).start()
        own_copy(b).start()

    for k in range(1, GROUP):
        home_copy(k).start()
    ahead = 1
    launch(0)
    for copy in inputs:
        copy.wait()
    chip_copy(ITERS, giant_ref).start()
    totals = giant_ref[0, 0].astype(F32)
    for b in range(1, bands):
        totals = totals + giant_ref[b // 2, b % 2].astype(F32)
    band_total[...] = totals
    for k in range(1, GROUP):
        strip_copy(k).start()
    for c in range(1, min(ahead, len(plan))):
        launch(c)

    for b in range(bands):
        psf = psf_ref[b]
        gram[b] = t_matmul(psf, psf).astype(BF16)
        psf_t[b] = jnp.transpose(psf.astype(F32)).astype(BF16)
    for k in range(1, GROUP):
        home_copy(k).wait_recv()
    table_vmem[...] = sort_tables(homes_ref, upper, QUAD * piece_count, lanes)
    to_scalar = pltpu.make_async_copy(table_vmem, table_ref, table_sem)
    to_scalar.start()
    to_scalar.wait()

    def prepare(index, carry):
        spot = lax.broadcasted_iota(I32, corners_ref.shape, 1) == index
        spot = jnp.sum(jnp.where(spot, corners_ref[...], 0), axis=1, keepdims=True)
        row_at, col_at = spot[0:1, :], spot[1:2, :]
        rows = lax.broadcasted_iota(I32, (TILE, side), 0)
        inner = lax.broadcasted_iota(I32, (TILE, side), 1)
        row_hot = jnp.where(rows == inner + row_at, 1.0, 0.0).astype(BF16)
        cols = lax.broadcasted_iota(I32, (side, TILE), 1)
        inner_c = lax.broadcasted_iota(I32, (side, TILE), 0)
        col_hot = jnp.where(cols == inner_c + col_at, 1.0, 0.0).astype(BF16)
        for b in range(bands):
            row_psf[index, b] = matmul(row_hot, psf_ref[b]).astype(BF16)
            col_psf[b, index] = matmul(psf_t[b], col_hot).astype(BF16)
        return carry

    sed_table[...] = jnp.zeros_like(sed_table)

    def combine(c):
        pair_copy(c).wait_recv()
        for group in range(quads // 2):
            first = (2 * group + parity) * near_blends

            def join(index, carry, group=group, first=first):
                some = table_ref[3, first + index].astype(F32)
                mine_part = running[c % 2, table_ref[2, first + index], : units[c]] * some
                summed[c][group, index] = (
                    mine_part + pair_buf[c][group, index].astype(F32)
                ).astype(BF16)
                return carry

            lax.fori_loop(0, near_blends, join, 0, unroll=4)
        for k in range(1, owners):
            incoming(c, k).start()
        arrived[c][pair, lower] = summed[c][pair, pl.ds(lower * owned, owned)]

    for c in range(len(plan)):
        for k in range(1, QUAD):
            piece_copy(c, k).wait_recv()
        own_copy(c).wait()
        if c + ahead < len(plan):
            launch(c + ahead)
        band_pieces = piece_bufs[c]

        def add(index, total, band_pieces=band_pieces, c=c):
            keep = table_ref[1, index].astype(F32)
            total = total * keep + band_pieces[table_ref[0, index]].astype(F32)
            running[c % 2, index, : units[c]] = total
            return total

        lax.fori_loop(0, QUAD * piece_count, add, jnp.zeros((units[c], UNIT, lanes), F32), unroll=8)
        for group in range(quads // 2):
            first = (2 * group + 1 - parity) * near_blends

            def put(index, carry, c=c, group=group, first=first):
                some = table_ref[3, first + index].astype(F32)
                aside[c][group, index] = (
                    running[c % 2, table_ref[2, first + index], : units[c]] * some
                ).astype(BF16)
                return carry

            lax.fori_loop(0, near_blends, put, 0, unroll=4)
        pair_copy(c).start()
        giant_turn(c, 0)
        if c > 0:
            combine(c - 1)
        giant_turn(c, 1)
    combine(len(plan) - 1)
    beside = {}
    while len(flow) > 2 and len(beside) < owned:
        beside[len(beside)] = flow.pop(0)[2]

    for c in range(len(plan)):
        for k in range(1, owners):
            incoming(c, k).wait_recv()

    def blend(n, carry):
        source_of_row = lax.broadcasted_iota(I32, (table, lanes), 0) // bands
        act_ref[...] = jnp.where(source_of_row < counts_ref[n], 1.0, 0.0)
        spread_rows(sed_ref, spectra_ref[n], bands, sources, lanes)
        sed_ref[...] = sed_ref[...] * act_ref[...]
        for b in range(bands):
            for c, (band, first, rows) in enumerate(plan):
                if band == b:
                    total = arrived[c][0, :, n].astype(F32)
                    for g in range(1, quads // 2):
                        total = total + arrived[c][g, :, n].astype(F32)
                    grad_ref[b, first : first + rows, :] = total.reshape(rows, side)
        mean = grad_ref[0]
        for b in range(1, bands):
            mean = mean + grad_ref[b]
        base_map = jnp.maximum(mean / bands, 0.0)
        for k in range(sources):
            morph_ref[k] = (
                jnp.where(labels_ref[n] == k + 1, base_map, 0.0)
                * act_ref[k * bands : k * bands + 1, :]
            )
        for b in range(bands):
            back = matmul(psf_t[b], grad_ref[b].astype(BF16)).astype(BF16)
            adj_ref[b] = matmul(back, psf_ref[b])

        def iteration(it, carry):
            for b in range(bands):
                mix = mix_band(sed_ref, morph_ref, b, bands, sources)
                grad_ref[b] = adj_ref[b] - matmul(matmul(gram[b], mix).astype(BF16), gram[b])
            update(sed_ref, morph_ref, grad_ref, part_ref, energy_ref, act_ref, bands, sources)
            return carry

        lax.fori_loop(0, ITERS, iteration, 0)
        out_morph[n] = morph_ref[...].astype(BF16).reshape(out_morph.shape[1:])
        for k in range(1, count):
            outgoing(0, n, k).start()
        for h in range(2):
            held[h][me * owned + n] = out_morph[n, rank, h]
        diag = lax.broadcasted_iota(I32, (table, lanes), 0) == lax.broadcasted_iota(
            I32, (table, lanes), 1
        )
        line = jnp.sum(jnp.where(diag, sed_ref[...], 0.0), axis=0, keepdims=True)
        here = lax.broadcasted_iota(I32, sed_table.shape, 0) == n
        sed_table[...] = jnp.where(here, line, sed_table[...])

        for index, step in beside.items():
            pl.when(n == index)(step)
        return carry

    lax.fori_loop(0, owned, blend, 0)

    def second(n, carry):
        for k in range(1, count):
            outgoing(1, n, k).start()
        return carry

    lax.fori_loop(0, owned, second, 0)
    sed_all[me] = sed_table[...].astype(BF16)
    for k in range(1, count):
        sed_copy(k).start()
    out_sed[...] = sed_table[...]
    lax.fori_loop(0, piece_count, prepare, 0)

    def settle(h):
        def one(n, carry):
            for k in range(1, count):
                outgoing(h, n, k).wait_recv()
            return carry

        lax.fori_loop(0, owned, one, 0)

    def pick(h, k, chunks):
        other = lax.rem(rank + k, GROUP)

        def one(index, carry):
            for chunk in chunks:
                found = held[h][
                    table_ref[
                        4 + other // QUAD,
                        lax.rem(other, QUAD) * piece_count + chunk * per_chunk + index,
                    ]
                ]
                if k < GROUP:
                    picked[h, other, chunk, index] = found
                else:
                    landed[chunk, index, rank, h] = found
            return carry

        lax.fori_loop(0, per_chunk, one, 0)

    settle(0)
    for k in range(1, GROUP + 1):
        pick(0, k, range(CHUNKS))
        if k < GROUP:
            half_copy(k).start()
    while len(flow) > 1:
        flow.pop(0)[2]()
    settle(1)
    for chunk in range(CHUNKS):
        for k in range(1, GROUP + 1):
            pick(1, k, [chunk])
            if k < GROUP:
                last_copy(chunk, k).start()

    while flow:
        flow.pop(0)[2]()
    for k in range(1, count):
        sed_copy(k).wait_recv()
    out_tile[...] = jnp.zeros_like(out_tile)

    for k in range(1, GROUP):
        half_copy(k).wait_recv()

    def finish(chunk, carry):
        for k in range(1, GROUP):
            last_copy(chunk, k).wait_recv()
        for index in range(per_chunk):
            piece = chunk * per_chunk + index
            home = table_ref[4 + upper, lower * piece_count + piece]
            owner = lax.div(home, owned)
            place = home - owner * owned
            rows = sed_all[owner].astype(F32)
            here = lax.broadcasted_iota(I32, rows.shape, 0) == place
            line = jnp.sum(jnp.where(here, rows, 0.0), axis=0, keepdims=True)
            diag = lax.broadcasted_iota(I32, (table, lanes), 0) == lax.broadcasted_iota(
                I32, (table, lanes), 1
            )
            column = jnp.sum(jnp.where(diag, line, 0.0), axis=1, keepdims=True)
            sed_ref[...] = jnp.broadcast_to(column, (table, lanes))
            morph_ref[...] = landed[chunk, index].astype(F32).reshape(sources, side, side)
            for b in range(bands):
                mix = mix_band(sed_ref, morph_ref, b, bands, sources)
                left_ref[b, :, index * side : (index + 1) * side] = matmul(
                    row_psf[piece, b], mix
                ).astype(BF16)
        for b in range(bands):
            right = col_psf[b, pl.ds(chunk * per_chunk, per_chunk)].reshape(
                per_chunk * side, TILE
            )
            out_tile[b] = out_tile[b] + matmul(left_ref[b], right)
        return carry

    lax.fori_loop(0, CHUNKS, finish, 0)

    def drain(n, carry):
        for h in range(2):
            for k in range(1, count):
                outgoing(h, n, k).wait_send()
        return carry

    lax.fori_loop(0, owned, drain, 0)
    for c in range(len(plan)):
        for k in range(1, QUAD):
            piece_copy(c, k).wait_send()
        pair_copy(c).wait_send()
        for k in range(1, owners):
            incoming(c, k).wait_send()
    for k in range(1, GROUP):
        home_copy(k).wait_send()
    for k in range(1, count):
        sed_copy(k).wait_send()
    for k in range(1, GROUP):
        half_copy(k).wait_send()
        for chunk in range(CHUNKS):
            last_copy(chunk, k).wait_send()
    for k in range(1, GROUP):
        strip_copy(k).wait_send()
        base_copy(k).wait_send()
    sent_bands(ITERS, giant_ref)
    for it in range(ITERS):
        sent_bands(it, mix_buf.at[it])
        relay_copy(it).wait_send()

        @pl.when(keeps)
        def _():
            for k in range(1, CHIPS):
                grad_copy(it, k).wait_send()


def deliver_kernel(
    bands,
    morph_ref,
    sed_ref,
    tile_ref,
    giant_ref,
    out_morph,
    out_sed,
    out_tile,
    out_giant,
    morph_buf,
    tile_buf,
    giant_buf,
    morph_sem,
    tile_sem,
    giant_sem,
):
    loads, stores = [], []
    for source, buf, target, sem in (
        (tile_ref, tile_buf, out_tile, tile_sem),
        (morph_ref, morph_buf, out_morph, morph_sem),
        (giant_ref, giant_buf, out_giant, giant_sem),
    ):
        for index in range(source.shape[0]):
            loads.append(
                pltpu.make_async_copy(source.at[index], buf.at[index], sem.at[0, index])
            )
            stores.append(
                pltpu.make_async_copy(buf.at[index], target.at[index], sem.at[1, index])
            )
    for load in loads:
        load.start()
    owned, sources, _ = out_sed.shape
    for k in range(sources):
        out_sed[:, k, :] = sed_ref[:owned, k * bands : (k + 1) * bands].astype(BF16)
    for load, store in zip(loads, stores):
        load.wait()
        store.start()
    for store in stores:
        store.wait()


def on_device(
    pieces,
    piece_blend,
    corners,
    blend_home,
    source_count,
    footprint,
    spectra,
    giant_pieces,
    giant_footprint,
    giant_spectra,
    psf_matrix,
):
    count = lax.axis_size("tiles")
    piece_count, bands, side, _ = pieces.shape
    owned = footprint.shape[0]
    blend_count = blend_home.shape[0]
    sources = spectra.shape[1]
    back_rows = sources * side // GROUP // 2
    lanes = side
    table = sources * bands
    strip = side // GROUP
    per_chunk = piece_count // CHUNKS
    plan = cuts(bands, side)
    units = [cut // QUAD // UNIT for _, _, cut in plan]
    pairs = count // QUAD // 2

    dma = pltpu.SemaphoreType.DMA
    whole_map = (GROUP, strip, side)
    final_morph, sed_rows, tile_model, giant_morph = pl.pallas_call(
        functools.partial(core_kernel, count, bands, sources, owned, piece_count),
        out_shape=(
            jax.ShapeDtypeStruct((owned, GROUP, 2, back_rows, lanes), BF16),
            jax.ShapeDtypeStruct((16, lanes), F32),
            jax.ShapeDtypeStruct((bands, TILE, TILE), F32),
            jax.ShapeDtypeStruct((sources, side, side), F32),
        ),
        in_specs=[SMEM, SMEM, SMEM] + [HBM] * 8,
        out_specs=(VMEM,) * 4,
        scratch_shapes=[
            pltpu.VMEM(footprint.shape, I32),
            pltpu.VMEM(spectra.shape, F32),
            pltpu.VMEM(psf_matrix.shape, BF16),
            pltpu.VMEM((2, piece_count), I32),
            pltpu.VMEM((bands // 2, 2, GROUP, strip, side), BF16),
            pltpu.VMEM(giant_footprint.shape, I32),
            pltpu.VMEM(giant_spectra.shape, F32),
            dma((7,)),
            pltpu.VMEM((GROUP, 8, lanes), I32),
            pltpu.VMEM((8, lanes), I32),
            pltpu.SMEM((8, lanes), I32),
            pltpu.VMEM((2, QUAD * piece_count, max(units), UNIT, lanes), F32),
            [pltpu.VMEM((pairs, QUAD * owned, u, UNIT, lanes), BF16) for u in units],
            [pltpu.VMEM((pairs, QUAD * owned, u, UNIT, lanes), BF16) for u in units],
            [pltpu.VMEM((pairs, QUAD * owned, u, UNIT, lanes), BF16) for u in units],
            [pltpu.VMEM((QUAD * piece_count, u, UNIT, lanes), BF16) for u in units],
            [pltpu.VMEM((pairs, QUAD, owned, u, UNIT, lanes), BF16) for u in units],
            pltpu.VMEM((sources, side, side), F32),
            pltpu.VMEM((table, lanes), F32),
            pltpu.VMEM((table, lanes), F32),
            pltpu.VMEM((bands, side, side), F32),
            pltpu.VMEM((bands, side, side), F32),
            pltpu.VMEM((table, lanes), F32),
            pltpu.VMEM((table, lanes), F32),
            pltpu.VMEM((bands, side, side), BF16),
            pltpu.VMEM((bands, side, side), BF16),
            pltpu.VMEM((16, lanes), F32),
            pltpu.VMEM((count, 16, lanes), BF16),
            [pltpu.VMEM((blend_count, back_rows, lanes), BF16) for _ in range(2)],
            pltpu.VMEM((2, GROUP, CHUNKS, per_chunk, back_rows, lanes), BF16),
            pltpu.VMEM((CHUNKS, per_chunk, GROUP, 2, back_rows, lanes), BF16),
            pltpu.VMEM((piece_count, bands, TILE, side), BF16),
            pltpu.VMEM((bands, piece_count, side, TILE), BF16),
            pltpu.VMEM((bands, TILE, per_chunk * side), BF16),
            pltpu.VMEM(whole_map, F32),
            pltpu.VMEM(whole_map, F32),
            pltpu.VMEM(whole_map, F32),
            pltpu.VMEM((ITERS + 1, bands // 2) + whole_map, BF16),
            pltpu.VMEM((ITERS + 1, bands // 2) + whole_map, BF16),
            pltpu.VMEM((ITERS + 1, CHIPS) + whole_map, BF16),
            pltpu.VMEM((ITERS, bands // 2, 2) + whole_map, BF16),
            pltpu.VMEM((side, side), F32),
            pltpu.VMEM((table, lanes), F32),
            pltpu.VMEM((ITERS, 2, bands // 2, side, side), BF16),
            dma((len(plan),)),
            dma,
            dma((GROUP - 1,)),
            dma((GROUP - 1,)),
            dma((len(plan), QUAD - 1)),
            dma((len(plan), QUAD - 1)),
            dma((len(plan),)),
            dma((len(plan),)),
            dma((len(plan), pairs * QUAD - 1)),
            dma((len(plan), pairs * QUAD - 1)),
            dma((2, owned, count - 1)),
            dma((2, owned, count - 1)),
            dma((count - 1,)),
            dma((count - 1,)),
            dma((GROUP - 1,)),
            dma((GROUP - 1,)),
            dma((CHUNKS, GROUP - 1)),
            dma((CHUNKS, GROUP - 1)),
            dma((GROUP - 1,)),
            dma((GROUP - 1,)),
            dma((GROUP - 1,)),
            dma((GROUP - 1,)),
            dma((ITERS + 1,)),
            dma((ITERS + 1,)),
            dma((ITERS + 1, bands // 2)),
            dma((ITERS + 1, CHIPS)),
            dma((ITERS, CHIPS - 1)),
            dma((ITERS, bands // 2)),
            dma((ITERS,)),
            dma((ITERS,)),
        ],
        compiler_params=pltpu.CompilerParams(
            collective_id=0, has_side_effects=True, vmem_limit_bytes=56 << 20
        ),
        name="core",
    )(
        piece_blend,
        blend_home,
        source_count,
        pieces.reshape(piece_count, bands, side // UNIT, UNIT, side),
        footprint,
        spectra,
        psf_matrix,
        corners.T,
        giant_pieces.reshape(bands // 2, 2, GROUP, strip, side),
        giant_footprint,
        giant_spectra,
    )
    final_morph, final_sed, tile_model, giant_morph = pl.pallas_call(
        functools.partial(deliver_kernel, bands),
        out_shape=(
            jax.ShapeDtypeStruct((owned, sources, side, side), BF16),
            jax.ShapeDtypeStruct((owned, sources, bands), BF16),
            jax.ShapeDtypeStruct((bands, TILE, TILE), F32),
            jax.ShapeDtypeStruct((sources, side, side), F32),
        ),
        in_specs=[HBM, VMEM, HBM, HBM],
        out_specs=(HBM, VMEM, HBM, HBM),
        scratch_shapes=[
            pltpu.VMEM((owned, sources, side, side), BF16),
            pltpu.VMEM((bands, TILE, TILE), F32),
            pltpu.VMEM((sources, side, side), F32),
            dma((2, owned)),
            dma((2, bands)),
            dma((2, sources)),
        ],
        name="deliver",
    )(
        final_morph.reshape(owned, sources, side, side),
        sed_rows,
        tile_model,
        giant_morph,
    )
    return (final_morph, final_sed, tile_model[None], giant_morph[None])


def solution(mesh):
    in_specs = (
        P(("groups", "tiles"), None, None, None),
        P(("groups", "tiles")),
        P(("groups", "tiles"), None),
        P("groups"),
        P(("groups", "tiles")),
        P(("groups", "tiles"), None, None),
        P(("groups", "tiles"), None, None),
        P(("groups", "tiles"), None, None, None),
        P(("groups", "tiles"), None, None),
        P(("groups", "tiles"), None, None),
        P(),
    )
    out_specs = (
        P(("groups", "tiles"), None, None, None),
        P(("groups", "tiles"), None, None),
        P(("groups", "tiles"), None, None, None),
        P(("groups", "tiles"), None, None, None),
    )
    return jax.shard_map(
        on_device, mesh=mesh, in_specs=in_specs, out_specs=out_specs, check_vma=False
    )
```

```python
import functools

import jax
import jax.numpy as jnp
from jax import lax
from jax.experimental import pallas as pl
from jax.experimental.pallas import tpu as pltpu
from jax.sharding import PartitionSpec as P

TILE = 256
ITERS = 3
GROUP = 8
QUAD = 4
CHIPS = GROUP // 2
UNIT = 16
KEEP_CHIP = ((0, 3, 1, 2), (3, 0, 2, 1))
CHUNKS = 4
MESH = pl.DeviceIdType.MESH
F32 = jnp.float32
BF16 = jnp.bfloat16
I32 = jnp.int32

step_size = 0.1

VMEM = pl.BlockSpec(memory_space=pltpu.VMEM)
SMEM = pl.BlockSpec(memory_space=pltpu.SMEM)
HBM = pl.BlockSpec(memory_space=pltpu.HBM)


def matmul(a, b):
    return jnp.dot(a, b, preferred_element_type=F32)


def t_matmul(a, b):
    return lax.dot_general(a, b, (((0,), (0,)), ((), ())), preferred_element_type=F32)


def barrier_all(me, count):
    barrier = pltpu.get_barrier_semaphore()
    for k in range(1, count):
        pl.semaphore_signal(
            barrier, inc=1, device_id={"tiles": lax.rem(me + k, count)}, device_id_type=MESH
        )
    pl.semaphore_wait(barrier, count - 1)


def remote(src, dst, send_sem, recv_sem, peer):
    return pltpu.make_async_remote_copy(
        src_ref=src,
        dst_ref=dst,
        send_sem=send_sem,
        recv_sem=recv_sem,
        device_id={"tiles": peer},
        device_id_type=MESH,
    )


def mix_band(sed_ref, maps, b, bands, sources):
    total = sed_ref[b : b + 1, :] * maps[0]
    for k in range(1, sources):
        row = k * bands + b
        total = total + sed_ref[row : row + 1, :] * maps[k]
    return total.astype(BF16)


def update(sed_ref, morph_ref, grad_ref, part_ref, energy_ref, act_ref, bands, sources):
    for k in range(sources):
        morph = morph_ref[k]
        energy = jnp.sum(morph * morph, axis=0, keepdims=True)
        push = None
        for b in range(bands):
            row = k * bands + b
            grad = grad_ref[b]
            part_ref[row : row + 1, :] = jnp.sum(morph * grad, axis=0, keepdims=True)
            energy_ref[row : row + 1, :] = energy
            term = sed_ref[row : row + 1, :] * grad
            push = term if push is None else push + term
        fresh = jnp.maximum(morph + step_size * push, 0.0)
        if act_ref is not None:
            fresh = fresh * act_ref[k * bands : k * bands + 1, :]
        morph_ref[k] = fresh
    inner = jnp.sum(part_ref[...], axis=1, keepdims=True)
    energy = jnp.sum(energy_ref[...], axis=1, keepdims=True)
    sed = jnp.maximum(sed_ref[...] + inner / (energy + 1.0), 0.0)
    if act_ref is not None:
        sed = sed * act_ref[...]
    sed_ref[...] = sed


def spread_rows(sed_ref, table, bands, sources, lanes):
    for k in range(sources):
        line = jnp.broadcast_to(table[k : k + 1, :], (bands, bands))
        row = lax.broadcasted_iota(I32, (bands, bands), 0)
        col = lax.broadcasted_iota(I32, (bands, bands), 1)
        value = jnp.sum(jnp.where(row == col, line, 0.0), axis=1, keepdims=True)
        sed_ref[k * bands : (k + 1) * bands, :] = jnp.broadcast_to(value, (bands, lanes))


def cuts(bands, side):
    steps = []
    for b in range(bands):
        if b in (0, bands - 1) and side // 2 % (QUAD * UNIT) == 0:
            steps += [(b, 0, side // 2), (b, side // 2, side // 2)]
        else:
            steps.append((b, 0, side))
    return steps


def sort_tables(homes_ref, upper, used, lanes):
    line = homes_ref[0]
    for source in range(1, GROUP):
        line = line + homes_ref[source]
    near = jnp.where(upper == 0, line[0:1, :], line[1:2, :])
    near = jnp.where(lax.broadcasted_iota(I32, (1, lanes), 1) < used, near, 2 * lanes)
    across = jnp.broadcast_to(near, (lanes, lanes))
    sub = lax.broadcasted_iota(I32, (lanes, lanes), 0)
    lane = lax.broadcasted_iota(I32, (lanes, lanes), 1)
    down = jnp.sum(jnp.where(sub == lane, across, 0), axis=1, keepdims=True)
    key_across = across * lanes + lane
    key_down = down * lanes + sub
    place = jnp.sum(jnp.where(key_across < key_down, 1, 0), axis=1, keepdims=True)
    order = jnp.sum(jnp.where(place == lane, sub, 0), axis=0, keepdims=True)
    sorted_home = jnp.sum(jnp.where(place == lane, down, 0), axis=0, keepdims=True)
    before = jnp.sum(jnp.where(place + 1 == lane, down, 0), axis=0, keepdims=True)
    keep = jnp.where(sorted_home == before, 1, 0)
    upto = jnp.sum(jnp.where(down <= lane, 1, 0), axis=0, keepdims=True)
    same = jnp.sum(jnp.where(down == lane, 1, 0), axis=0, keepdims=True)
    last = jnp.maximum(upto - 1, 0)
    some = jnp.where(same > 0, 1, 0)
    rows = [order, keep, last, some]
    for half in range(GROUP // QUAD):
        rows.append(line[half : half + 1, :])
    which = lax.broadcasted_iota(I32, (8, lanes), 0)
    result = jnp.zeros((8, lanes), I32)
    for index, row in enumerate(rows):
        result = jnp.where(which == index, row, result)
    return result


def core_kernel(
    count,
    bands,
    sources,
    owned,
    piece_count,
    blend_ref,
    home_of_ref,
    counts_ref,
    pieces_ref,
    labels_in,
    spectra_in,
    psf_in,
    corners_in,
    giant_in,
    giant_labels_in,
    giant_spectra_in,
    out_morph,
    out_sed,
    out_tile,
    out_giant,
    labels_ref,
    spectra_ref,
    psf_ref,
    corners_ref,
    giant_ref,
    giant_labels_ref,
    giant_spectra_ref,
    input_sem,
    homes_ref,
    table_vmem,
    table_ref,
    running,
    aside,
    pair_buf,
    summed,
    piece_bufs,
    arrived,
    morph_ref,
    sed_ref,
    act_ref,
    adj_ref,
    grad_ref,
    part_ref,
    energy_ref,
    gram,
    psf_t,
    sed_table,
    sed_all,
    held,
    picked,
    landed,
    row_psf,
    col_psf,
    left_ref,
    band_total,
    strips,
    base_buf,
    chip_buf,
    chip_out,
    band_buf,
    mix_buf,
    adj_own,
    giant_sed,
    giant_grad,
    own_sem,
    table_sem,
    home_send,
    home_recv,
    piece_send,
    piece_recv,
    pair_send,
    pair_recv,
    in_send,
    in_recv,
    back_send,
    back_recv,
    sed_send,
    sed_recv,
    half_send,
    half_recv,
    last_send,
    last_recv,
    strip_send,
    strip_recv,
    base_send,
    base_recv,
    chip_send,
    chip_recv,
    band_send,
    band_recv,
    grad_send,
    grad_recv,
    relay_send,
    relay_recv,
):
    me = lax.axis_index("tiles")
    rank = lax.rem(me, GROUP)
    base = me - rank
    mine = me // GROUP
    side = labels_ref.shape[1]
    lanes = side
    strip = side // GROUP
    plan = cuts(bands, side)
    units = [rows // QUAD // UNIT for _, _, rows in plan]
    quads = count // QUAD
    near_blends = QUAD * owned
    table = bands * sources
    per_chunk = piece_count // CHUNKS
    inputs = []
    for source, target in (
        (giant_in, giant_ref),
        (psf_in, psf_ref),
        (spectra_in, spectra_ref),
        (corners_in, corners_ref),
        (giant_labels_in, giant_labels_ref),
        (giant_spectra_in, giant_spectra_ref),
        (labels_in, labels_ref),
    ):
        inputs.append(pltpu.make_async_copy(source, target, input_sem.at[len(inputs)]))
        inputs[-1].start()
    upper = rank // QUAD
    lower = lax.rem(rank, QUAD)
    at = lax.broadcasted_iota(I32, (8, lanes), 1) - lower * piece_count
    at = jnp.where(lax.broadcasted_iota(I32, (8, lanes), 0) == upper, at, -1)
    line = jnp.zeros((8, lanes), I32)
    for index in range(piece_count):
        line = jnp.where(at == index, home_of_ref[blend_ref[index]], line)
    homes_ref[rank] = line
    barrier_all(me, count)

    core = lax.rem(rank, 2)
    chip = rank // 2
    partner_core = base + rank + 1 - 2 * core
    half_bands = bands // 2

    def keeper(i):
        return jnp.where(core == 0, KEEP_CHIP[0][i], KEEP_CHIP[1][i])

    keeps = chip < 0
    own_index = 0
    for i in range(half_bands):
        keeps = jnp.logical_or(keeps, keeper(i) == chip)
        own_index = jnp.where(keeper(i) == chip, i, own_index)
    own_band = 2 * own_index + core

    def home_copy(k):
        other = lax.rem(rank + k, GROUP)
        return remote(
            homes_ref.at[rank], homes_ref.at[rank], home_send.at[k - 1], home_recv.at[k - 1],
            base + other,
        )

    quad = me // QUAD
    pair = quad // 2
    parity = lax.rem(quad, 2)

    def piece_slot(c):
        return piece_bufs[c].at[pl.ds(lower * piece_count, piece_count)]

    def piece_source(c, other):
        band, first, _ = plan[c]
        return pieces_ref.at[:, band, pl.ds(first // UNIT + other * units[c], units[c])]

    def piece_copy(c, k):
        other = lax.rem(lower + k, QUAD)
        return remote(
            piece_source(c, other), piece_slot(c), piece_send.at[c, k - 1],
            piece_recv.at[c, k - 1], quad * QUAD + other,
        )

    def own_copy(c):
        return pltpu.make_async_copy(piece_source(c, lower), piece_slot(c), own_sem.at[c])

    def pair_copy(b):
        partner = (quad + 1 - 2 * parity) * QUAD + lower
        return remote(aside[b], pair_buf[b], pair_send.at[b], pair_recv.at[b], partner)

    def incoming(b, k):
        to_pair = lax.rem(pair + k // QUAD, quads // 2)
        to_lower = lax.rem(lower + k % QUAD, QUAD)
        return remote(
            summed[b].at[to_pair, pl.ds(to_lower * owned, owned)],
            arrived[b].at[pair, lower],
            in_send.at[b, k - 1],
            in_recv.at[b, k - 1],
            (2 * to_pair + parity) * QUAD + to_lower,
        )

    owners = quads // 2 * QUAD

    def outgoing(h, n, k):
        peer = lax.rem(me + k, count)
        return remote(
            out_morph.at[n, lax.rem(peer, GROUP), h],
            held[h].at[me * owned + n],
            back_send.at[h, n, k - 1],
            back_recv.at[h, n, k - 1],
            peer,
        )

    def sed_copy(k):
        return remote(
            sed_all.at[me], sed_all.at[me], sed_send.at[k - 1], sed_recv.at[k - 1],
            lax.rem(me + k, count),
        )

    def half_copy(k):
        other = lax.rem(rank + k, GROUP)
        return remote(
            picked.at[0, other],
            landed.at[:, :, rank, 0],
            half_send.at[k - 1],
            half_recv.at[k - 1],
            base + other,
        )

    def last_copy(chunk, k):
        other = lax.rem(rank + k, GROUP)
        return remote(
            picked.at[1, other, chunk],
            landed.at[chunk, :, rank, 1],
            last_send.at[chunk, k - 1],
            last_recv.at[chunk, k - 1],
            base + other,
        )

    def strip_copy(k):
        other = lax.rem(rank + k, GROUP)
        return remote(
            band_total.at[other], strips.at[rank], strip_send.at[k - 1], strip_recv.at[k - 1],
            base + other,
        )

    def base_copy(k):
        other = lax.rem(rank + k, GROUP)
        return remote(
            base_buf.at[rank], base_buf.at[rank], base_send.at[k - 1], base_recv.at[k - 1],
            base + other,
        )

    def chip_copy(slot, src):
        return remote(
            src.at[:, 1 - core], chip_buf.at[slot], chip_send.at[slot], chip_recv.at[slot],
            partner_core,
        )

    def band_copy(slot, i):
        return remote(
            chip_out.at[slot, i], band_buf.at[slot, chip], band_send.at[slot, i],
            band_recv.at[slot, chip], base + 2 * keeper(i) + core,
        )

    def grad_copy(slot, k):
        other = lax.rem(chip + k, CHIPS)
        return remote(
            giant_grad.at[slot, core, own_index],
            giant_grad.at[slot, core, own_index],
            grad_send.at[slot, k - 1],
            grad_recv.at[slot, own_index],
            base + 2 * other + core,
        )

    def relay_copy(slot):
        return remote(
            giant_grad.at[slot, core], giant_grad.at[slot, core], relay_send.at[slot],
            relay_recv.at[slot], partner_core,
        )

    def chip_sum(slot, ref):
        chip_copy(slot, ref).wait_recv()
        for i in range(half_bands):
            value = ref[i, core].astype(F32) + chip_buf[slot, i].astype(F32)
            chip_out[slot, i] = value.astype(BF16)

            @pl.when(keeper(i) != chip)
            def _():
                band_copy(slot, i).start()

            @pl.when(keeper(i) == chip)
            def _():
                band_buf[slot, chip] = chip_out[slot, i]

    def sent_bands(slot, ref):
        chip_copy(slot, ref).wait_send()
        for i in range(half_bands):
            @pl.when(keeper(i) != chip)
            def _():
                band_copy(slot, i).wait_send()

    def kept_sum(slot):
        for k in range(1, CHIPS):
            source = lax.rem(chip + k, CHIPS)
            remote(
                band_buf.at[slot, source], band_buf.at[slot, source], band_send.at[slot, 0],
                band_recv.at[slot, source], base + 2 * source + core,
            ).wait_recv()
        total = band_buf[slot, 0].astype(F32)
        for source in range(1, CHIPS):
            total = total + band_buf[slot, source].astype(F32)
        return total.reshape(side, side).astype(BF16)

    def giant_open():
        for k in range(1, GROUP):
            strip_copy(k).wait_recv()
        mean = None
        for k in range(GROUP):
            source = lax.rem(rank + k, GROUP)
            part = band_total[rank] if k == 0 else strips[source]
            mean = part if mean is None else mean + part
        base_buf[rank] = jnp.maximum(mean / bands, 0.0)
        for k in range(1, GROUP):
            base_copy(k).start()

        chip_sum(ITERS, giant_ref)

    def giant_mix(slot):
        for b in range(bands):
            mix = mix_band(giant_sed, out_giant, b, bands, sources)
            mix_buf[slot, b // 2, b % 2] = mix.reshape(GROUP, strip, side)
        chip_copy(slot, mix_buf.at[slot]).start()

    def giant_chip(slot):
        chip_sum(slot, mix_buf.at[slot])

    def giant_start():
        for k in range(1, GROUP):
            base_copy(k).wait_recv()
        base_map = base_buf[...].reshape(side, side)
        for k in range(sources):
            out_giant[k] = jnp.where(giant_labels_ref[0] == k + 1, base_map, 0.0)
        spread_rows(giant_sed, giant_spectra_ref[0], bands, sources, lanes)
        giant_mix(0)

    def giant_keep(slot):
        @pl.when(keeps)
        def _():
            if slot == 0:
                total = kept_sum(ITERS)
                back = matmul(psf_t[own_band], total).astype(BF16)
                adj_own[...] = matmul(back, psf_ref[own_band])
            total = kept_sum(slot)
            gram_own = gram[own_band]
            grad = adj_own[...] - matmul(matmul(gram_own, total).astype(BF16), gram_own)
            giant_grad[slot, core, own_index] = grad.astype(BF16)
            for k in range(1, CHIPS):
                grad_copy(slot, k).start()

    def giant_relay(slot):
        for i in range(half_bands):
            @pl.when(keeper(i) != chip)
            def _():
                remote(
                    giant_grad.at[slot, core, i], giant_grad.at[slot, core, i],
                    grad_send.at[slot, 0], grad_recv.at[slot, i], base + 2 * keeper(i) + core,
                ).wait_recv()

        relay_copy(slot).start()

    def giant_update(slot):
        relay_copy(slot).wait_recv()
        for b in range(bands):
            grad_ref[b] = giant_grad[slot, b % 2, b // 2].astype(F32)
        update(giant_sed, out_giant, grad_ref, part_ref, energy_ref, None, bands, sources)
        if slot + 1 < ITERS:
            giant_mix(slot + 1)

    flow = [(0, 1, giant_open), (1, 0, giant_start), (1, 1, functools.partial(giant_chip, 0))]
    turn = 2
    for it in range(ITERS):
        flow.append((turn, 0, functools.partial(giant_keep, it)))
        flow.append((turn + 1, 0, functools.partial(giant_relay, it)))
        flow.append((turn + 1, 1, functools.partial(giant_update, it)))
        if it + 1 < ITERS:
            flow.append((turn + 2, 0, functools.partial(giant_chip, it + 1)))
        turn += 3

    def giant_turn(b, part):
        while flow and flow[0][:2] <= (b, part):
            flow.pop(0)[2]()

    def launch(b):
        for k in range(1, QUAD):
            piece_copy(b, k).start()
        own_copy(b).start()

    for k in range(1, GROUP):
        home_copy(k).start()
    ahead = 1
    launch(0)
    for copy in inputs:
        copy.wait()
    chip_copy(ITERS, giant_ref).start()
    totals = giant_ref[0, 0].astype(F32)
    for b in range(1, bands):
        totals = totals + giant_ref[b // 2, b % 2].astype(F32)
    band_total[...] = totals
    for k in range(1, GROUP):
        strip_copy(k).start()
    for c in range(1, min(ahead, len(plan))):
        launch(c)

    for b in range(bands):
        psf = psf_ref[b]
        gram[b] = t_matmul(psf, psf).astype(BF16)
        psf_t[b] = jnp.transpose(psf.astype(F32)).astype(BF16)
    for k in range(1, GROUP):
        home_copy(k).wait_recv()
    table_vmem[...] = sort_tables(homes_ref, upper, QUAD * piece_count, lanes)
    to_scalar = pltpu.make_async_copy(table_vmem, table_ref, table_sem)
    to_scalar.start()
    to_scalar.wait()

    def prepare(index, carry):
        spot = lax.broadcasted_iota(I32, corners_ref.shape, 1) == index
        spot = jnp.sum(jnp.where(spot, corners_ref[...], 0), axis=1, keepdims=True)
        row_at, col_at = spot[0:1, :], spot[1:2, :]
        rows = lax.broadcasted_iota(I32, (TILE, side), 0)
        inner = lax.broadcasted_iota(I32, (TILE, side), 1)
        row_hot = jnp.where(rows == inner + row_at, 1.0, 0.0).astype(BF16)
        cols = lax.broadcasted_iota(I32, (side, TILE), 1)
        inner_c = lax.broadcasted_iota(I32, (side, TILE), 0)
        col_hot = jnp.where(cols == inner_c + col_at, 1.0, 0.0).astype(BF16)
        for b in range(bands):
            row_psf[index, b] = matmul(row_hot, psf_ref[b]).astype(BF16)
            col_psf[b, index] = matmul(psf_t[b], col_hot).astype(BF16)
        return carry

    sed_table[...] = jnp.zeros_like(sed_table)

    def combine(c):
        pair_copy(c).wait_recv()
        for group in range(quads // 2):
            first = (2 * group + parity) * near_blends

            def join(index, carry, group=group, first=first):
                some = table_ref[3, first + index].astype(F32)
                mine_part = running[c % 2, table_ref[2, first + index], : units[c]] * some
                summed[c][group, index] = (
                    mine_part + pair_buf[c][group, index].astype(F32)
                ).astype(BF16)
                return carry

            lax.fori_loop(0, near_blends, join, 0, unroll=16)
        for k in range(1, owners):
            incoming(c, k).start()
        arrived[c][pair, lower] = summed[c][pair, pl.ds(lower * owned, owned)]

    for c in range(len(plan)):
        for k in range(1, QUAD):
            piece_copy(c, k).wait_recv()
        own_copy(c).wait()
        if c + ahead < len(plan):
            launch(c + ahead)
        band_pieces = piece_bufs[c]

        def add(index, total, band_pieces=band_pieces, c=c):
            keep = table_ref[1, index].astype(F32)
            total = total * keep + band_pieces[table_ref[0, index]].astype(F32)
            running[c % 2, index, : units[c]] = total
            return total

        lax.fori_loop(0, QUAD * piece_count, add, jnp.zeros((units[c], UNIT, lanes), F32), unroll=8)
        for group in range(quads // 2):
            first = (2 * group + 1 - parity) * near_blends

            def put(index, carry, c=c, group=group, first=first):
                some = table_ref[3, first + index].astype(F32)
                aside[c][group, index] = (
                    running[c % 2, table_ref[2, first + index], : units[c]] * some
                ).astype(BF16)
                return carry

            lax.fori_loop(0, near_blends, put, 0, unroll=16)
        pair_copy(c).start()
        giant_turn(c, 0)
        if c > 0:
            combine(c - 1)
        giant_turn(c, 1)
    combine(len(plan) - 1)
    beside = {}
    while len(flow) > 2 and len(beside) < owned:
        beside[len(beside)] = flow.pop(0)[2]

    for c in range(len(plan)):
        for k in range(1, owners):
            incoming(c, k).wait_recv()

    def blend(n, carry):
        source_of_row = lax.broadcasted_iota(I32, (table, lanes), 0) // bands
        act_ref[...] = jnp.where(source_of_row < counts_ref[n], 1.0, 0.0)
        spread_rows(sed_ref, spectra_ref[n], bands, sources, lanes)
        sed_ref[...] = sed_ref[...] * act_ref[...]
        for b in range(bands):
            for c, (band, first, rows) in enumerate(plan):
                if band == b:
                    total = arrived[c][0, :, n].astype(F32)
                    for g in range(1, quads // 2):
                        total = total + arrived[c][g, :, n].astype(F32)
                    grad_ref[b, first : first + rows, :] = total.reshape(rows, side)
        mean = grad_ref[0]
        for b in range(1, bands):
            mean = mean + grad_ref[b]
        base_map = jnp.maximum(mean / bands, 0.0)
        for k in range(sources):
            morph_ref[k] = (
                jnp.where(labels_ref[n] == k + 1, base_map, 0.0)
                * act_ref[k * bands : k * bands + 1, :]
            )
        for b in range(bands):
            back = matmul(psf_t[b], grad_ref[b].astype(BF16)).astype(BF16)
            adj_ref[b] = matmul(back, psf_ref[b])

        def iteration(it, carry):
            for b in range(bands):
                mix = mix_band(sed_ref, morph_ref, b, bands, sources)
                grad_ref[b] = adj_ref[b] - matmul(matmul(gram[b], mix).astype(BF16), gram[b])
            update(sed_ref, morph_ref, grad_ref, part_ref, energy_ref, act_ref, bands, sources)
            return carry

        lax.fori_loop(0, ITERS, iteration, 0)
        out_morph[n] = morph_ref[...].astype(BF16).reshape(out_morph.shape[1:])
        for k in range(1, count):
            outgoing(0, n, k).start()
        for h in range(2):
            held[h][me * owned + n] = out_morph[n, rank, h]
        diag = lax.broadcasted_iota(I32, (table, lanes), 0) == lax.broadcasted_iota(
            I32, (table, lanes), 1
        )
        line = jnp.sum(jnp.where(diag, sed_ref[...], 0.0), axis=0, keepdims=True)
        here = lax.broadcasted_iota(I32, sed_table.shape, 0) == n
        sed_table[...] = jnp.where(here, line, sed_table[...])

        for index, step in beside.items():
            pl.when(n == index)(step)
        return carry

    lax.fori_loop(0, owned, blend, 0)

    def second(n, carry):
        for k in range(1, count):
            outgoing(1, n, k).start()
        return carry

    lax.fori_loop(0, owned, second, 0)
    sed_all[me] = sed_table[...].astype(BF16)
    for k in range(1, count):
        sed_copy(k).start()
    out_sed[...] = sed_table[...]
    lax.fori_loop(0, piece_count, prepare, 0)

    def settle(h):
        def one(n, carry):
            for k in range(1, count):
                outgoing(h, n, k).wait_recv()
            return carry

        lax.fori_loop(0, owned, one, 0)

    def pick(h, k, chunks):
        other = lax.rem(rank + k, GROUP)

        def one(index, carry):
            for chunk in chunks:
                found = held[h][
                    table_ref[
                        4 + other // QUAD,
                        lax.rem(other, QUAD) * piece_count + chunk * per_chunk + index,
                    ]
                ]
                if k < GROUP:
                    picked[h, other, chunk, index] = found
                else:
                    landed[chunk, index, rank, h] = found
            return carry

        lax.fori_loop(0, per_chunk, one, 0)

    settle(0)
    for k in range(1, GROUP + 1):
        pick(0, k, range(CHUNKS))
        if k < GROUP:
            half_copy(k).start()
    while len(flow) > 1:
        flow.pop(0)[2]()
    settle(1)
    for chunk in range(CHUNKS):
        for k in range(1, GROUP + 1):
            pick(1, k, [chunk])
            if k < GROUP:
                last_copy(chunk, k).start()

    while flow:
        flow.pop(0)[2]()
    for k in range(1, count):
        sed_copy(k).wait_recv()
    out_tile[...] = jnp.zeros_like(out_tile)

    for k in range(1, GROUP):
        half_copy(k).wait_recv()

    def finish(chunk, carry):
        for k in range(1, GROUP):
            last_copy(chunk, k).wait_recv()
        for index in range(per_chunk):
            piece = chunk * per_chunk + index
            home = table_ref[4 + upper, lower * piece_count + piece]
            owner = lax.div(home, owned)
            place = home - owner * owned
            rows = sed_all[owner].astype(F32)
            here = lax.broadcasted_iota(I32, rows.shape, 0) == place
            line = jnp.sum(jnp.where(here, rows, 0.0), axis=0, keepdims=True)
            diag = lax.broadcasted_iota(I32, (table, lanes), 0) == lax.broadcasted_iota(
                I32, (table, lanes), 1
            )
            column = jnp.sum(jnp.where(diag, line, 0.0), axis=1, keepdims=True)
            sed_ref[...] = jnp.broadcast_to(column, (table, lanes))
            morph_ref[...] = landed[chunk, index].astype(F32).reshape(sources, side, side)
            for b in range(bands):
                mix = mix_band(sed_ref, morph_ref, b, bands, sources)
                left_ref[b, :, index * side : (index + 1) * side] = matmul(
                    row_psf[piece, b], mix
                ).astype(BF16)
        for b in range(bands):
            right = col_psf[b, pl.ds(chunk * per_chunk, per_chunk)].reshape(
                per_chunk * side, TILE
            )
            out_tile[b] = out_tile[b] + matmul(left_ref[b], right)
        return carry

    lax.fori_loop(0, CHUNKS, finish, 0)

    def drain(n, carry):
        for h in range(2):
            for k in range(1, count):
                outgoing(h, n, k).wait_send()
        return carry

    lax.fori_loop(0, owned, drain, 0)
    for c in range(len(plan)):
        for k in range(1, QUAD):
            piece_copy(c, k).wait_send()
        pair_copy(c).wait_send()
        for k in range(1, owners):
            incoming(c, k).wait_send()
    for k in range(1, GROUP):
        home_copy(k).wait_send()
    for k in range(1, count):
        sed_copy(k).wait_send()
    for k in range(1, GROUP):
        half_copy(k).wait_send()
        for chunk in range(CHUNKS):
            last_copy(chunk, k).wait_send()
    for k in range(1, GROUP):
        strip_copy(k).wait_send()
        base_copy(k).wait_send()
    sent_bands(ITERS, giant_ref)
    for it in range(ITERS):
        sent_bands(it, mix_buf.at[it])
        relay_copy(it).wait_send()

        @pl.when(keeps)
        def _():
            for k in range(1, CHIPS):
                grad_copy(it, k).wait_send()


def deliver_kernel(
    bands,
    morph_ref,
    sed_ref,
    tile_ref,
    giant_ref,
    out_morph,
    out_sed,
    out_tile,
    out_giant,
    morph_buf,
    tile_buf,
    giant_buf,
    morph_sem,
    tile_sem,
    giant_sem,
):
    loads, stores = [], []
    for source, buf, target, sem in (
        (tile_ref, tile_buf, out_tile, tile_sem),
        (morph_ref, morph_buf, out_morph, morph_sem),
        (giant_ref, giant_buf, out_giant, giant_sem),
    ):
        for index in range(source.shape[0]):
            loads.append(
                pltpu.make_async_copy(source.at[index], buf.at[index], sem.at[0, index])
            )
            stores.append(
                pltpu.make_async_copy(buf.at[index], target.at[index], sem.at[1, index])
            )
    for load in loads:
        load.start()
    owned, sources, _ = out_sed.shape
    for k in range(sources):
        out_sed[:, k, :] = sed_ref[:owned, k * bands : (k + 1) * bands].astype(BF16)
    for load, store in zip(loads, stores):
        load.wait()
        store.start()
    for store in stores:
        store.wait()


def on_device(
    pieces,
    piece_blend,
    corners,
    blend_home,
    source_count,
    footprint,
    spectra,
    giant_pieces,
    giant_footprint,
    giant_spectra,
    psf_matrix,
):
    count = lax.axis_size("tiles")
    piece_count, bands, side, _ = pieces.shape
    owned = footprint.shape[0]
    blend_count = blend_home.shape[0]
    sources = spectra.shape[1]
    back_rows = sources * side // GROUP // 2
    lanes = side
    table = sources * bands
    strip = side // GROUP
    per_chunk = piece_count // CHUNKS
    plan = cuts(bands, side)
    units = [cut // QUAD // UNIT for _, _, cut in plan]
    pairs = count // QUAD // 2

    dma = pltpu.SemaphoreType.DMA
    whole_map = (GROUP, strip, side)
    final_morph, sed_rows, tile_model, giant_morph = pl.pallas_call(
        functools.partial(core_kernel, count, bands, sources, owned, piece_count),
        out_shape=(
            jax.ShapeDtypeStruct((owned, GROUP, 2, back_rows, lanes), BF16),
            jax.ShapeDtypeStruct((16, lanes), F32),
            jax.ShapeDtypeStruct((bands, TILE, TILE), F32),
            jax.ShapeDtypeStruct((sources, side, side), F32),
        ),
        in_specs=[SMEM, SMEM, SMEM] + [HBM] * 8,
        out_specs=(VMEM,) * 4,
        scratch_shapes=[
            pltpu.VMEM(footprint.shape, I32),
            pltpu.VMEM(spectra.shape, F32),
            pltpu.VMEM(psf_matrix.shape, BF16),
            pltpu.VMEM((2, piece_count), I32),
            pltpu.VMEM((bands // 2, 2, GROUP, strip, side), BF16),
            pltpu.VMEM(giant_footprint.shape, I32),
            pltpu.VMEM(giant_spectra.shape, F32),
            dma((7,)),
            pltpu.VMEM((GROUP, 8, lanes), I32),
            pltpu.VMEM((8, lanes), I32),
            pltpu.SMEM((8, lanes), I32),
            pltpu.VMEM((2, QUAD * piece_count, max(units), UNIT, lanes), F32),
            [pltpu.VMEM((pairs, QUAD * owned, u, UNIT, lanes), BF16) for u in units],
            [pltpu.VMEM((pairs, QUAD * owned, u, UNIT, lanes), BF16) for u in units],
            [pltpu.VMEM((pairs, QUAD * owned, u, UNIT, lanes), BF16) for u in units],
            [pltpu.VMEM((QUAD * piece_count, u, UNIT, lanes), BF16) for u in units],
            [pltpu.VMEM((pairs, QUAD, owned, u, UNIT, lanes), BF16) for u in units],
            pltpu.VMEM((sources, side, side), F32),
            pltpu.VMEM((table, lanes), F32),
            pltpu.VMEM((table, lanes), F32),
            pltpu.VMEM((bands, side, side), F32),
            pltpu.VMEM((bands, side, side), F32),
            pltpu.VMEM((table, lanes), F32),
            pltpu.VMEM((table, lanes), F32),
            pltpu.VMEM((bands, side, side), BF16),
            pltpu.VMEM((bands, side, side), BF16),
            pltpu.VMEM((16, lanes), F32),
            pltpu.VMEM((count, 16, lanes), BF16),
            [pltpu.VMEM((blend_count, back_rows, lanes), BF16) for _ in range(2)],
            pltpu.VMEM((2, GROUP, CHUNKS, per_chunk, back_rows, lanes), BF16),
            pltpu.VMEM((CHUNKS, per_chunk, GROUP, 2, back_rows, lanes), BF16),
            pltpu.VMEM((piece_count, bands, TILE, side), BF16),
            pltpu.VMEM((bands, piece_count, side, TILE), BF16),
            pltpu.VMEM((bands, TILE, per_chunk * side), BF16),
            pltpu.VMEM(whole_map, F32),
            pltpu.VMEM(whole_map, F32),
            pltpu.VMEM(whole_map, F32),
            pltpu.VMEM((ITERS + 1, bands // 2) + whole_map, BF16),
            pltpu.VMEM((ITERS + 1, bands // 2) + whole_map, BF16),
            pltpu.VMEM((ITERS + 1, CHIPS) + whole_map, BF16),
            pltpu.VMEM((ITERS, bands // 2, 2) + whole_map, BF16),
            pltpu.VMEM((side, side), F32),
            pltpu.VMEM((table, lanes), F32),
            pltpu.VMEM((ITERS, 2, bands // 2, side, side), BF16),
            dma((len(plan),)),
            dma,
            dma((GROUP - 1,)),
            dma((GROUP - 1,)),
            dma((len(plan), QUAD - 1)),
            dma((len(plan), QUAD - 1)),
            dma((len(plan),)),
            dma((len(plan),)),
            dma((len(plan), pairs * QUAD - 1)),
            dma((len(plan), pairs * QUAD - 1)),
            dma((2, owned, count - 1)),
            dma((2, owned, count - 1)),
            dma((count - 1,)),
            dma((count - 1,)),
            dma((GROUP - 1,)),
            dma((GROUP - 1,)),
            dma((CHUNKS, GROUP - 1)),
            dma((CHUNKS, GROUP - 1)),
            dma((GROUP - 1,)),
            dma((GROUP - 1,)),
            dma((GROUP - 1,)),
            dma((GROUP - 1,)),
            dma((ITERS + 1,)),
            dma((ITERS + 1,)),
            dma((ITERS + 1, bands // 2)),
            dma((ITERS + 1, CHIPS)),
            dma((ITERS, CHIPS - 1)),
            dma((ITERS, bands // 2)),
            dma((ITERS,)),
            dma((ITERS,)),
        ],
        compiler_params=pltpu.CompilerParams(
            collective_id=0, has_side_effects=True, vmem_limit_bytes=56 << 20
        ),
        name="core",
    )(
        piece_blend,
        blend_home,
        source_count,
        pieces.reshape(piece_count, bands, side // UNIT, UNIT, side),
        footprint,
        spectra,
        psf_matrix,
        corners.T,
        giant_pieces.reshape(bands // 2, 2, GROUP, strip, side),
        giant_footprint,
        giant_spectra,
    )
    final_morph, final_sed, tile_model, giant_morph = pl.pallas_call(
        functools.partial(deliver_kernel, bands),
        out_shape=(
            jax.ShapeDtypeStruct((owned, sources, side, side), BF16),
            jax.ShapeDtypeStruct((owned, sources, bands), BF16),
            jax.ShapeDtypeStruct((bands, TILE, TILE), F32),
            jax.ShapeDtypeStruct((sources, side, side), F32),
        ),
        in_specs=[HBM, VMEM, HBM, HBM],
        out_specs=(HBM, VMEM, HBM, HBM),
        scratch_shapes=[
            pltpu.VMEM((owned, sources, side, side), BF16),
            pltpu.VMEM((bands, TILE, TILE), F32),
            pltpu.VMEM((sources, side, side), F32),
            dma((2, owned)),
            dma((2, bands)),
            dma((2, sources)),
        ],
        name="deliver",
    )(
        final_morph.reshape(owned, sources, side, side),
        sed_rows,
        tile_model,
        giant_morph,
    )
    return (final_morph, final_sed, tile_model[None], giant_morph[None])


def solution(mesh):
    in_specs = (
        P(("groups", "tiles"), None, None, None),
        P(("groups", "tiles")),
        P(("groups", "tiles"), None),
        P("groups"),
        P(("groups", "tiles")),
        P(("groups", "tiles"), None, None),
        P(("groups", "tiles"), None, None),
        P(("groups", "tiles"), None, None, None),
        P(("groups", "tiles"), None, None),
        P(("groups", "tiles"), None, None),
        P(),
    )
    out_specs = (
        P(("groups", "tiles"), None, None, None),
        P(("groups", "tiles"), None, None),
        P(("groups", "tiles"), None, None, None),
        P(("groups", "tiles"), None, None, None),
    )
    return jax.shard_map(
        on_device, mesh=mesh, in_specs=in_specs, out_specs=out_specs, check_vma=False
    )
```
